128 devices in a mesh: gx: 4 (over x), yz: 32 (over y, z, core).
Axes of the slice: x: 4, y: 4, z: 4, core: 2. Of those that a mesh axis runs over, the one named last changes fastest.
Arguments:
- fields: bfloat16 [24576, 5, 512], P(('gx', 'yz')), may hold values from -6 to 6
- solver_counts: int32 [128], replicated, may hold values from 16 to 192, as said below
- cnn_owner: int32 [8192], replicated, may hold values from 0 to 127, as said below
- in_weight: bfloat16 [32, 5], replicated, may hold values from -2.5 to 2.5
- in_bias: float32 [32], replicated, may hold values from -3 to 3
- depth_weight: float32 [32, 27], replicated, may hold values from -1.25 to 1.25
- depth_bias: float32 [32], replicated, may hold values from -3 to 3
- mix_weight: bfloat16 [32, 32], replicated, may hold values from -1 to 1
- mix_bias: float32 [32], replicated, may hold values from -3 to 3
- out_weight: bfloat16 [6, 32], replicated, may hold values from -1 to 1
- out_bias: float32 [6], replicated, may hold values from -3 to 3
Outputs:
- closure: bfloat16 [24576, 6, 512], P(('gx', 'yz'))
The draws below stay inside these ranges and needn't reach their ends.
Inputs may be any that keep to these rules, and one draw needn't show every extreme that they name: Solver owner e holds its patches in slots 0 to solver_counts[e] - 1; the counts sum to 8192 and each is a multiple of a quarter of 64. `cnn_owner`: every network owner receives exactly 64 patches, and at most 2 from one solver owner.
All inputs are finite; a program needn't handle non-finite values.
Results may differ from the reference program's by a relative error of at most 0.0067.
Values may be sent and summed in bfloat16 or wider, within the bound.
A program may use at most 192 MiB of HBM per device.

```python
import jax
import jax.numpy as jnp
from jax import lax

P_SIZE = 8
BZ = 16
BYP = 4
CIN = 5
HID = 32
COUT = 6
CELLS = 512
MEAN = 64
CAP = 192
NDEV = 128
NPATCH = 8192
N_GX = 4
N_YZ = 32


def draw_solver_counts(key, part):
    device_total = N_GX * N_YZ
    quarter = MEAN // 4
    key_perm = jax.random.fold_in(key, 3)
    key_kind = jax.random.fold_in(key, 5)
    pattern_pick = jax.random.randint(key_kind, (device_total // 4,), 0, 3)
    pattern_pick = jnp.where(jnp.arange(device_total // 4) == 0, 0, pattern_pick)
    patterns = jnp.array([[12, 2, 1, 1], [4, 4, 4, 4], [8, 4, 2, 2]], dtype=jnp.int32)
    values = (patterns[pattern_pick] * quarter).reshape(device_total)
    placing = jax.random.permutation(key_perm, device_total)
    return values[jnp.argsort(placing)].astype(jnp.int32)


def draw_cnn_owner(key, part):
    device_total = N_GX * N_YZ
    shuffled = jax.random.permutation(jax.random.fold_in(key, 7), device_total)
    return shuffled[jnp.arange(NPATCH) % device_total].astype(jnp.int32)


def level_of(rng, extent, cuts, least, top_value):
    def one(dim, shards_of):
        steps = jax.random.uniform(jax.random.fold_in(jax.random.fold_in(rng, 6), dim), (shards_of,), jnp.float32, least / len(cuts), top_value / len(cuts))
        return jnp.repeat(jnp.exp(steps), extent[dim] // shards_of).reshape((-1,) + (1,) * (len(extent) - dim - 1))

    level = one(*cuts[0])
    for cut in cuts[1:]:
        level = level * one(*cut)
    return level


def gaussian(key, extent, deviation, bound, pieces=(), kind=jnp.bfloat16):
    level = level_of(key, extent, pieces, -0.22, 0.18) if pieces else 1.0
    values = jax.random.normal(key, extent, jnp.float32) * deviation * level
    return jnp.minimum(jnp.maximum(values, -bound), bound).astype(kind)


def setup_inputs(seed: int = 0) -> dict:
    key_of = jax.random.split(jax.random.key(seed), 12)
    return {
        "fields": gaussian(key_of[0], (NDEV * CAP, CIN, CELLS), 1.0, 6.0, ((0, 128),)),
        "solver_counts": draw_solver_counts(jax.random.fold_in(key_of[11], 71), 0),
        "cnn_owner": draw_cnn_owner(jax.random.fold_in(key_of[11], 71), 0),
        "in_weight": gaussian(key_of[3], (HID, CIN), CIN ** -0.5, 2.5),
        "in_bias": gaussian(key_of[4], (HID,), 0.5, 3.0, (), jnp.float32),
        "depth_weight": gaussian(key_of[5], (HID, 27), 27 ** -0.5, 1.25, (), jnp.float32),
        "depth_bias": gaussian(key_of[6], (HID,), 0.5, 3.0, (), jnp.float32),
        "mix_weight": gaussian(key_of[7], (HID, HID), HID ** -0.5, 1.0),
        "mix_bias": gaussian(key_of[8], (HID,), 0.5, 3.0, (), jnp.float32),
        "out_weight": gaussian(key_of[9], (COUT, HID), HID ** -0.5, 1.0),
        "out_bias": gaussian(key_of[10], (COUT,), 0.5, 3.0, (), jnp.float32),
    }


def patch_tables(solver_counts, cnn_owner):
    total = cnn_owner.shape[0]
    order_index = jnp.arange(total, dtype=jnp.int32)
    run_ends = jnp.cumsum(solver_counts).astype(jnp.int32)
    run_starts = (run_ends - solver_counts).astype(jnp.int32)
    owners = jnp.arange(run_ends.shape[0], dtype=jnp.int32)
    source = jnp.sum((order_index[:, None] >= run_ends[None, :]).astype(jnp.int32), axis=1).astype(jnp.int32)
    start_of = jnp.sum(jnp.where(source[:, None] == owners[None, :], run_starts[None, :], 0), axis=1).astype(jnp.int32)
    solver_slot = (order_index - start_of).astype(jnp.int32)
    one_hot = (cnn_owner[:, None] == owners[None, :]).astype(jnp.int32)
    before = (jnp.cumsum(one_hot, axis=0).astype(jnp.int32) - one_hot).astype(jnp.int32)
    brick_slot = jnp.sum(before * one_hot, axis=1).astype(jnp.int32)
    run_base = jnp.sum(jnp.take(before, start_of, axis=0) * one_hot, axis=1).astype(jnp.int32)
    pair_rank = (brick_slot - run_base).astype(jnp.int32)
    return source, solver_slot, brick_slot, pair_rank


def gelu_tanh(value):
    return jax.nn.gelu(value, approximate=True)


def depth_and_mix(first_hidden, depth_weight, depth_bias, mix_weight, mix_bias, out_weight, out_bias):
    rows_x = first_hidden.shape[1] - 2
    rows_y = first_hidden.shape[2] - 2
    depth_total = jnp.zeros((first_hidden.shape[0], rows_x, rows_y, first_hidden.shape[3]), jnp.float32)
    for step_x in range(3):
        for step_y in range(3):
            for step_z in range(3):
                shifted = first_hidden[:, step_x:step_x + rows_x, step_y:step_y + rows_y, :]
                shifted = jnp.roll(shifted, 1 - step_z, axis=3)
                weight = depth_weight[:, 9 * step_x + 3 * step_y + step_z]
                depth_total = depth_total + weight[:, None, None, None] * shifted.astype(jnp.float32)
    depth = (depth_total + depth_bias[:, None, None, None]).astype(jnp.bfloat16)
    mixed = jnp.einsum('gh,hxyz->gxyz', mix_weight.astype(jnp.float32), depth.astype(jnp.float32))
    mixed = gelu_tanh(mixed + mix_bias[:, None, None, None]).astype(jnp.bfloat16)
    result = jnp.einsum('gh,hxyz->gxyz', out_weight.astype(jnp.float32), mixed.astype(jnp.float32))
    return (result + out_bias[:, None, None, None]).astype(jnp.bfloat16)


def reference(fields, solver_counts, cnn_owner, in_weight, in_bias, depth_weight, depth_bias, mix_weight, mix_bias, out_weight, out_bias):
    source, solver_slot, brick_slot, pair_rank = patch_tables(solver_counts, cnn_owner)
    solver_rows = (source * CAP + solver_slot).astype(jnp.int32)
    brick_places = (cnn_owner * MEAN + brick_slot).astype(jnp.int32)
    gather_order = jnp.zeros((NDEV * MEAN,), jnp.int32).at[brick_places].set(solver_rows)
    patches = fields[gather_order]
    whole_grid = patches.reshape(N_GX, N_YZ, BYP, BZ, CIN, P_SIZE, P_SIZE, P_SIZE).transpose(4, 0, 5, 1, 2, 6, 3, 7)
    whole_grid = whole_grid.reshape(CIN, N_GX * P_SIZE, N_YZ * BYP * P_SIZE, BZ * P_SIZE)
    zero_layer = jnp.zeros((CIN, 1, N_YZ * BYP * P_SIZE, BZ * P_SIZE), jnp.bfloat16)
    padded = jnp.concatenate([zero_layer, whole_grid, zero_layer], axis=1)
    padded = jnp.concatenate([padded[:, :, -1:], padded, padded[:, :, :1]], axis=2)

    def one_device(device):
        gx_index = device // N_YZ
        yz_index = device % N_YZ
        starts = (jnp.int32(0), (gx_index * P_SIZE).astype(jnp.int32), (yz_index * (BYP * P_SIZE)).astype(jnp.int32), jnp.int32(0))
        device_block = lax.dynamic_slice(padded, starts, (CIN, P_SIZE + 2, BYP * P_SIZE + 2, BZ * P_SIZE))
        x_position = gx_index * P_SIZE + jnp.arange(P_SIZE + 2, dtype=jnp.int32)
        wall_keep = ((x_position > 0) & (x_position < N_GX * P_SIZE + 1)).astype(jnp.float32)
        first_linear = jnp.einsum('hc,cxyz->hxyz', in_weight.astype(jnp.float32), device_block.astype(jnp.float32))
        first_linear = first_linear + in_bias[:, None, None, None]
        first_hidden = (gelu_tanh(first_linear) * wall_keep[None, :, None, None]).astype(jnp.bfloat16)
        field_out = depth_and_mix(first_hidden, depth_weight, depth_bias, mix_weight, mix_bias, out_weight, out_bias)
        field_out = field_out.reshape(COUT, P_SIZE, BYP, P_SIZE, BZ, P_SIZE).transpose(2, 4, 0, 1, 3, 5)
        return field_out.reshape(MEAN, COUT, CELLS)

    network_out = lax.map(one_device, jnp.arange(NDEV, dtype=jnp.int32)).reshape(NDEV * MEAN, COUT, CELLS)
    closure = jnp.zeros((NDEV * CAP, COUT, CELLS), jnp.bfloat16).at[solver_rows].set(network_out[brick_places])
    return closure
```

```python
import jax
import jax.numpy as jnp
from jax import lax
from jax.experimental import pallas as pl
from jax.experimental.pallas import tpu as pltpu
from jax.sharding import PartitionSpec as P

MESH = pl.DeviceIdType.MESH
NDEV = 128
N_GX = 4
N_YZ = 32
CAP = 192
CIN = 5
HID = 32
COUT = 6
LANES = 128
SLOTS = 2 * NDEV
ROWS = 4 * SLOTS
F32 = jnp.float32
BF16 = jnp.bfloat16
I32 = jnp.int32
GELU_A = 2.0 * 0.7978845608028654
GELU_B = 8.0 * 0.7978845608028654 * 0.044715


def iota(shape, dim):
    return lax.broadcasted_iota(I32, shape, dim)


def dot(a, b):
    return jnp.dot(a, b, preferred_element_type=F32)


def one_hot(condition):
    return jnp.where(condition, 1.0, 0.0).astype(BF16)


def row_to_col(row):
    count = row.shape[1]
    same = iota((count, count), 0) == iota((count, count), 1)
    return jnp.sum(jnp.where(same, row, 0.0), axis=1, keepdims=True)


def col_to_row(col):
    count = col.shape[0]
    same = iota((count, count), 0) == iota((count, count), 1)
    return jnp.sum(jnp.where(same, col, 0.0), axis=0, keepdims=True)


def gelu_half(y):
    return y + y * jnp.tanh(y * (GELU_A + GELU_B * (y * y)))


def run_cumulative(me, counts, owner):
    lower = iota((NDEV, NDEV), 1) <= iota((NDEV, NDEV), 0)
    run_end = jnp.sum(jnp.where(lower, counts, 0.0), axis=1, keepdims=True).astype(I32)
    mine = one_hot(owner == me)
    rows = iota((NDEV, 64), 1)
    whole = dot(one_hot(rows < (run_end >> 7)), mine)
    part = dot(one_hot(rows == (run_end >> 7)), mine)
    inside = iota((NDEV, LANES), 1) < (run_end & 127)
    return jnp.sum(whole + jnp.where(inside, part, 0.0), axis=1, keepdims=True)


def brick_keys(cum_col):
    cum_row = col_to_row(cum_col)
    row = iota((2 * LANES, NDEV), 0)
    patch = (row & 63).astype(F32)
    below = cum_row <= patch
    source = jnp.sum(jnp.where(below, 1.0, 0.0), axis=1, keepdims=True)
    before = jnp.max(jnp.where(below, cum_row, 0.0), axis=1, keepdims=True)
    place = 2.0 * source + ((iota((2 * LANES, 1), 0) & 63).astype(F32) - before)
    row = iota((2 * LANES, 1), 0)
    key_col = 4 * place.astype(I32) + 2 * ((row >> 6) & 1) + (row >> 7)
    lane = iota((NDEV, 2 * LANES), 1)
    patch = (lane & 63).astype(F32)
    below = cum_col <= patch
    source = jnp.sum(jnp.where(below, 1.0, 0.0), axis=0, keepdims=True)
    before = jnp.max(jnp.where(below, cum_col, 0.0), axis=0, keepdims=True)
    lane = iota((1, 2 * LANES), 1)
    place = 2.0 * source + ((lane & 63).astype(F32) - before)
    key_row = 4 * place.astype(I32) + 2 * ((lane >> 6) & 1) + (lane >> 7)
    return key_col, key_row


def slot_keys(me, counts, owner):
    lane = iota((1, NDEV), 1)
    start = jnp.sum(jnp.where(lane < me, counts, 0.0), axis=1, keepdims=True).astype(I32)
    count = jnp.sum(jnp.where(lane == me, counts, 0.0), axis=1, keepdims=True).astype(I32)
    position = iota((CAP, 1), 0) + start
    rows = dot(one_hot(iota((CAP, 64), 1) == (position >> 7)), owner.astype(F32).astype(BF16))
    here = iota((CAP, LANES), 1) == (position & 127)
    owner_col = jnp.sum(jnp.where(here, rows, 0.0), axis=1, keepdims=True)
    owner_row = col_to_row(owner_col)
    same = owner_col == owner_row
    first = iota((CAP, CAP), 0)
    second = iota((CAP, CAP), 1)
    rank_col = jnp.sum(jnp.where(same & (second < first), 1.0, 0.0), axis=1, keepdims=True)
    rank_row = jnp.sum(jnp.where(same & (first < second), 1.0, 0.0), axis=0, keepdims=True)
    key_col = (2.0 * owner_col + rank_col).astype(I32)
    key_row = (2.0 * owner_row + rank_row).astype(I32)
    key_col = jnp.where(iota((CAP, 1), 0) < count, key_col, -1)
    key_row = jnp.where(iota((1, CAP), 1) < count, key_row, -1)
    return key_col, key_row


def split3(value):
    high = value.astype(BF16).astype(F32)
    middle = (value - high).astype(BF16).astype(F32)
    low = value - high - middle
    return high, middle, low


def with_bias(weight, bias_col, width):
    rows, depth = weight.shape
    tail = iota((rows, width - depth), 1)
    high, middle, low = split3(bias_col)
    extra = jnp.where(tail == 0, high, jnp.where(tail == 1, middle, jnp.where(tail == 2, low, 0.0)))
    return jnp.concatenate([weight, extra], axis=1).astype(BF16)


def move_body(
    counts_ref, owner_ref, fields_ref, in_weight_ref, in_bias_ref, depth_weight_ref, depth_bias_ref,
    mix_weight_ref, mix_bias_ref, out_weight_ref, out_bias_ref,
    back_ref, key_ref,
    spread, outgoing, incoming, grid_in, ones_mask, hidden, taps, taps_bias, result, packed,
    x_send, x_recv, y_send, y_recv, c_send, c_recv, leaving,
    send_sem, recv_sem, halo_send, halo_recv, back_send, back_recv,
):
    gx = lax.axis_index("gx")
    yz = lax.axis_index("yz")
    me = gx * N_YZ + yz

    def coords(step):
        other = lax.rem(me + step, NDEV)
        return other, (lax.div(other, N_YZ), lax.rem(other, N_YZ))

    barrier = pltpu.get_barrier_semaphore()

    def greet(step, carry):
        _, where = coords(step)
        pl.semaphore_signal(barrier, inc=1, device_id=where, device_id_type=MESH)
        return carry

    lax.fori_loop(1, NDEV, greet, 0)

    counts = counts_ref[...].astype(F32)
    owner = owner_ref[...]
    key_col, key_row = slot_keys(me, counts, owner)
    key_ref[...] = jnp.broadcast_to(key_col, (CAP, LANES))
    select = one_hot(iota((SLOTS, CAP), 0) == key_row)
    for c in range(CIN):
        rows = dot(select, fields_ref[c])
        for part in range(4):
            spread[c, pl.ds(part, SLOTS, stride=4), :] = rows[:, part * LANES : (part + 1) * LANES]
    for c in range(CIN):
        outgoing[:, :, c * LANES : (c + 1) * LANES] = (
            spread[c].reshape(NDEV, 8, LANES).astype(BF16)
        )

    pl.semaphore_wait(barrier, NDEV - 1)

    def send_out(step, carry):
        other, where = coords(step)
        pltpu.make_async_remote_copy(
            src_ref=outgoing.at[other], dst_ref=incoming.at[me],
            send_sem=send_sem, recv_sem=recv_sem, device_id=where, device_id_type=MESH,
        ).start()
        return carry

    lax.fori_loop(1, NDEV, send_out, 0)
    incoming[me] = outgoing[me]

    cum_col = run_cumulative(me, counts, owner)
    brick_col, brick_row = brick_keys(cum_col)
    gather = one_hot(iota((2 * LANES, ROWS), 1) == brick_col)
    lane = iota((1, LANES), 1)
    high_x = ((lane >> 6) & 1) == 1
    along_y = (lane >> 4) & 3
    along_z = lane & 15
    keep_low = jnp.where(gx > 0, 1.0, 0.0).astype(F32)
    keep_high = jnp.where(gx < N_GX - 1, 1.0, 0.0).astype(F32)
    for x in range(6):
        mask = jnp.ones((1, LANES), F32)
        if x == 0:
            mask = jnp.where(high_x, 1.0, keep_low)
        if x == 5:
            mask = jnp.where(high_x, keep_high, 1.0)
        ones_mask[x] = jnp.broadcast_to(mask, (16, LANES))
    depth_weight = depth_weight_ref[...]
    for tap in range(27):
        taps[tap] = jnp.broadcast_to(depth_weight[:, tap : tap + 1], (HID, LANES))
    taps_bias[...] = jnp.broadcast_to(row_to_col(depth_bias_ref[...]), (HID, LANES))
    in_weight = in_weight_ref[...].astype(F32)
    in_cols = [row_to_col(in_weight[c : c + 1, :]) for c in range(CIN)]
    column = iota((HID, 80), 1)
    base = jnp.zeros((HID, 80), F32)
    for c in range(CIN):
        base = jnp.where((column >> 4) == c, 0.5 * in_cols[c], base)
    in_bias = 0.5 * row_to_col(in_bias_ref[...])
    first_w = jnp.concatenate(
        [with_bias(jnp.where((column & 15) == cell, base, 0.0), in_bias, 96) for cell in range(16)],
        axis=0,
    )
    mix_w = with_bias(0.5 * mix_weight_ref[...].astype(F32), 0.5 * row_to_col(mix_bias_ref[...]), 48)
    out_w = with_bias(out_weight_ref[...].astype(F32), row_to_col(out_bias_ref[...]), 48)
    ones_cells = jnp.ones((16, 8 * LANES), BF16)

    every = pltpu.make_async_copy(
        outgoing.at[pl.ds(0, NDEV - 1)], incoming.at[pl.ds(0, NDEV - 1)], recv_sem
    )
    every.wait()

    bricks = dot(gather, incoming[...].reshape(ROWS, CIN * LANES))
    for c in range(CIN):
        for m in range(2):
            turned = bricks[m * LANES : (m + 1) * LANES, c * LANES : (c + 1) * LANES].T
            for p in range(2):
                grid_in[c, pl.ds((1 + 2 * m + p) * 80 + 8, 64), :] = turned[p * 64 : (p + 1) * 64]

    for c in range(CIN):
        x_send[0, c] = pltpu.roll(grid_in[c, pl.ds(4 * 80 + 8, 64), :], 64, 1).astype(BF16)
        x_send[1, c] = pltpu.roll(grid_in[c, pl.ds(1 * 80 + 8, 64), :], 64, 1).astype(BF16)
        last_y = [grid_in[c, pl.ds(x * 80 + 64, 8), :] for x in range(1, 5)]
        first_y = [grid_in[c, pl.ds(x * 80 + 8, 8), :] for x in range(1, 5)]
        y_send[0, c] = pltpu.roll(jnp.concatenate(last_y, axis=0), 80, 1).astype(BF16)
        y_send[1, c] = pltpu.roll(jnp.concatenate(first_y, axis=0), 48, 1).astype(BF16)
        c_send[0, c] = pltpu.roll(last_y[3], 16, 1).astype(BF16)
        c_send[1, c] = pltpu.roll(first_y[3], 112, 1).astype(BF16)
        c_send[2, c] = pltpu.roll(last_y[0], 16, 1).astype(BF16)
        c_send[3, c] = pltpu.roll(first_y[0], 112, 1).astype(BF16)
    up_x = lax.rem(gx + 1, N_GX)
    down_x = lax.rem(gx + N_GX - 1, N_GX)
    up_y = lax.rem(yz + 1, N_YZ)
    down_y = lax.rem(yz + N_YZ - 1, N_YZ)
    halo = []
    for source, target, where in (
        (x_send.at[0], x_recv.at[0], (up_x, yz)),
        (x_send.at[1], x_recv.at[1], (down_x, yz)),
        (y_send.at[0], y_recv.at[0], (gx, up_y)),
        (y_send.at[1], y_recv.at[1], (gx, down_y)),
        (c_send.at[0], c_recv.at[0], (up_x, up_y)),
        (c_send.at[1], c_recv.at[1], (up_x, down_y)),
        (c_send.at[2], c_recv.at[2], (down_x, up_y)),
        (c_send.at[3], c_recv.at[3], (down_x, down_y)),
    ):
        number = len(halo)
        copy = pltpu.make_async_remote_copy(
            src_ref=source, dst_ref=target, send_sem=halo_send.at[number],
            recv_sem=halo_recv.at[number], device_id=where, device_id_type=MESH,
        )
        copy.start()
        halo.append(copy)
    for copy in halo:
        copy.wait()

    for c in range(CIN):
        low = jnp.where(high_x, x_send[0, c].astype(F32), keep_low * x_recv[0, c].astype(F32))
        high = jnp.where(high_x, keep_high * x_recv[1, c].astype(F32), x_send[1, c].astype(F32))
        grid_in[c, pl.ds(8, 64), :] = low
        grid_in[c, pl.ds(5 * 80 + 8, 64), :] = high
        for side in range(2):
            own = y_recv[side, c].astype(F32)
            corner_low = keep_low * c_recv[0 + side, c].astype(F32)
            corner_high = keep_high * c_recv[2 + side, c].astype(F32)
            edge_lane = along_y == (0 if side == 0 else 3)
            for x in range(6):
                if x == 0:
                    far = jnp.where(high_x, pltpu.roll(own[24:32], 64, 1), corner_low)
                elif x == 5:
                    far = jnp.where(high_x, corner_high, pltpu.roll(own[0:8], 64, 1))
                else:
                    far = own[8 * (x - 1) : 8 * x]
                near = grid_in[c, pl.ds(x * 80 + (64 if side == 0 else 8), 8), :]
                near = pltpu.roll(near, 16 if side == 0 else 112, 1)
                grid_in[c, pl.ds(x * 80 + (0 if side == 0 else 72), 8), :] = jnp.where(
                    edge_lane, far, near
                )

    def first_group(group, carry):
        x = lax.div(group, 5)
        pair = lax.rem(group, 5)
        start = pl.multiple_of(group * 16, 16)
        cells = [grid_in[c, pl.ds(start, 16), :] for c in range(CIN)]
        stacked = jnp.concatenate(cells + [ones_mask[x]], axis=0).astype(BF16)
        value = gelu_half(dot(first_w, stacked)).astype(BF16).astype(F32)
        for cell in range(16):
            y = 2 * pair + cell // 8
            z = cell % 8
            here = value[cell * HID : (cell + 1) * HID]
            hidden[x, y, 1 + z] = here
            if z == 7:
                hidden[x, y, 0] = jnp.where(
                    along_z == 0, pltpu.roll(here, 113, 1), pltpu.roll(here, 1, 1)
                )
            if z == 0:
                hidden[x, y, 9] = jnp.where(
                    along_z == 15, pltpu.roll(here, 15, 1), pltpu.roll(here, 127, 1)
                )
        return carry

    lax.fori_loop(0, 30, first_group, 0)

    def depth_group(group, carry):
        x = lax.div(group, 8)
        y = lax.rem(group, 8)
        columns = [[] for _ in range(8)]
        for part in range(4):
            rows = pl.ds(8 * part, 8)
            total = [taps_bias[rows, :]] * 8
            for a in range(3):
                for b in range(3):
                    cells = [hidden[x + a, y + b, z, rows, :] for z in range(10)]
                    for c in range(3):
                        weight = taps[9 * a + 3 * b + c, rows, :]
                        for z in range(8):
                            total[z] = total[z] + weight * cells[z + c]
            for z in range(8):
                columns[z].append(total[z])
        depth = jnp.concatenate(
            [jnp.concatenate(column, axis=0).astype(BF16) for column in columns], axis=1
        )
        mixed = gelu_half(dot(mix_w, jnp.concatenate([depth, ones_cells], axis=0))).astype(BF16)
        field = dot(out_w, jnp.concatenate([mixed, ones_cells], axis=0))
        for z in range(8):
            start = pl.multiple_of(group * 64 + 8 * z, 8)
            result[pl.ds(start, COUT), :] = field[:, z * LANES : (z + 1) * LANES]
        return carry

    lax.fori_loop(0, 32, depth_group, 0)

    for f in range(COUT):
        for m in range(2):
            cells = result[pl.ds(m * 1024 + f, LANES, stride=8), :]
            packed[m * LANES : (m + 1) * LANES, f * LANES : (f + 1) * LANES] = cells.T.astype(BF16)
    scatter = one_hot(iota((ROWS, 2 * LANES), 0) == brick_row)
    leaving[...] = dot(scatter, packed[...]).reshape(NDEV, 8, COUT * LANES).astype(BF16)

    def send_back(step, carry):
        other, where = coords(step)
        pltpu.make_async_remote_copy(
            src_ref=leaving.at[other], dst_ref=back_ref.at[me],
            send_sem=back_send, recv_sem=back_recv, device_id=where, device_id_type=MESH,
        ).start()
        return carry

    lax.fori_loop(1, NDEV, send_back, 0)
    back_ref[me] = leaving[me]
    pltpu.make_async_copy(
        outgoing.at[pl.ds(0, NDEV - 1)], incoming.at[pl.ds(0, NDEV - 1)], send_sem
    ).wait()
    for semaphore in (back_send, back_recv):
        pltpu.make_async_copy(
            leaving.at[pl.ds(0, NDEV - 1)], back_ref.at[pl.ds(0, NDEV - 1)], semaphore
        ).wait()


def unpack_body(back_ref, key_ref, out_ref):
    key = key_ref[...][:, :1]
    rows = iota((CAP, ROWS), 1)
    arrived = back_ref[...].reshape(ROWS, COUT * LANES)
    for part in range(4):
        wanted = jnp.where(key < 0, -1, 4 * key + part)
        taken = dot(one_hot(rows == wanted), arrived).astype(BF16)
        for f in range(COUT):
            out_ref[f, :, part * LANES : (part + 1) * LANES] = taken[:, f * LANES : (f + 1) * LANES]


VMEM = pl.BlockSpec(memory_space=pltpu.VMEM)


def shards(
    fields, solver_counts, cnn_owner, in_weight, in_bias, depth_weight, depth_bias,
    mix_weight, mix_bias, out_weight, out_bias,
):
    back, key = pl.pallas_call(
        move_body,
        out_shape=(
            jax.ShapeDtypeStruct((NDEV, 8, COUT * LANES), BF16),
            jax.ShapeDtypeStruct((CAP, LANES), I32),
        ),
        in_specs=[VMEM] * 11,
        out_specs=(VMEM, VMEM),
        scratch_shapes=[
            pltpu.VMEM((CIN, ROWS, LANES), F32),
            pltpu.VMEM((NDEV, 8, CIN * LANES), BF16),
            pltpu.VMEM((NDEV, 8, CIN * LANES), BF16),
            pltpu.VMEM((CIN, 480, LANES), F32),
            pltpu.VMEM((6, 16, LANES), F32),
            pltpu.VMEM((6, 10, 10, HID, LANES), F32),
            pltpu.VMEM((27, HID, LANES), F32),
            pltpu.VMEM((HID, LANES), F32),
            pltpu.VMEM((2048, LANES), F32),
            pltpu.VMEM((2 * LANES, COUT * LANES), BF16),
            pltpu.VMEM((2, CIN, 64, LANES), BF16),
            pltpu.VMEM((2, CIN, 64, LANES), BF16),
            pltpu.VMEM((2, CIN, 32, LANES), BF16),
            pltpu.VMEM((2, CIN, 32, LANES), BF16),
            pltpu.VMEM((4, CIN, 8, LANES), BF16),
            pltpu.VMEM((4, CIN, 8, LANES), BF16),
            pltpu.VMEM((NDEV, 8, COUT * LANES), BF16),
            pltpu.SemaphoreType.DMA,
            pltpu.SemaphoreType.DMA,
            pltpu.SemaphoreType.DMA((8,)),
            pltpu.SemaphoreType.DMA((8,)),
            pltpu.SemaphoreType.DMA,
            pltpu.SemaphoreType.DMA,
        ],
        compiler_params=pltpu.CompilerParams(
            collective_id=0, has_side_effects=True, vmem_limit_bytes=60 * 1024 * 1024
        ),
        name="closure",
    )(
        solver_counts.reshape(1, NDEV),
        cnn_owner.reshape(64, LANES),
        jnp.transpose(fields, (1, 0, 2)),
        jnp.transpose(in_weight),
        in_bias.reshape(1, HID),
        depth_weight,
        depth_bias.reshape(1, HID),
        mix_weight,
        mix_bias.reshape(1, HID),
        out_weight,
        out_bias.reshape(1, COUT),
    )
    closure = pl.pallas_call(
        unpack_body,
        out_shape=jax.ShapeDtypeStruct((COUT, CAP, 4 * LANES), BF16),
        in_specs=[VMEM] * 2,
        out_specs=VMEM,
        compiler_params=pltpu.CompilerParams(vmem_limit_bytes=60 * 1024 * 1024),
        name="unpack",
    )(back, key)
    return jnp.transpose(closure, (1, 0, 2))


def solution(mesh):
    return jax.shard_map(
        shards,
        mesh=mesh,
        in_specs=(P(("gx", "yz"), None, None), P(), P(), P(), P(), P(), P(), P(), P(), P(), P()),
        out_specs=P(("gx", "yz"), None, None),
        check_vma=False,
    )
```

```python
import jax
import jax.numpy as jnp
from jax import lax
from jax.experimental import pallas as pl
from jax.experimental.pallas import tpu as pltpu
from jax.sharding import PartitionSpec as P

MESH = pl.DeviceIdType.MESH
NDEV = 128
N_GX = 4
N_YZ = 32
CAP = 192
CIN = 5
HID = 32
COUT = 6
LANES = 128
SLOTS = 2 * NDEV
ROWS = 4 * SLOTS
F32 = jnp.float32
BF16 = jnp.bfloat16
I32 = jnp.int32
GELU_A = 2.0 * 0.7978845608028654
GELU_B = 8.0 * 0.7978845608028654 * 0.044715


STEPS = sorted(
    [(x, y, z, c) for x in range(4) for y in range(4) for z in range(4) for c in range(2)],
    key=lambda step: -sum(min(part, 4 - part) for part in step[:3]),
)[:-2] + [(0, 0, 0, 1)]


def iota(shape, dim):
    return lax.broadcasted_iota(I32, shape, dim)


def dot(a, b):
    return jnp.dot(a, b, preferred_element_type=F32)


def one_hot(condition):
    return jnp.where(condition, 1.0, 0.0).astype(BF16)


def row_to_col(row):
    count = row.shape[1]
    same = iota((count, count), 0) == iota((count, count), 1)
    return jnp.sum(jnp.where(same, row, 0.0), axis=1, keepdims=True)


def col_to_row(col):
    count = col.shape[0]
    same = iota((count, count), 0) == iota((count, count), 1)
    return jnp.sum(jnp.where(same, col, 0.0), axis=0, keepdims=True)


def gelu_half(y):
    return y + y * jnp.tanh(y * (GELU_A + GELU_B * (y * y)))


def run_cumulative(me, counts, owner):
    lower = iota((NDEV, NDEV), 1) <= iota((NDEV, NDEV), 0)
    run_end = jnp.sum(jnp.where(lower, counts, 0.0), axis=1, keepdims=True).astype(I32)
    mine = one_hot(owner == me)
    rows = iota((NDEV, 64), 1)
    whole = dot(one_hot(rows < (run_end >> 7)), mine)
    part = dot(one_hot(rows == (run_end >> 7)), mine)
    inside = iota((NDEV, LANES), 1) < (run_end & 127)
    return jnp.sum(whole + jnp.where(inside, part, 0.0), axis=1, keepdims=True)


def brick_keys(cum_col):
    cum_row = col_to_row(cum_col)
    row = iota((2 * LANES, NDEV), 0)
    patch = (row & 63).astype(F32)
    below = cum_row <= patch
    source = jnp.sum(jnp.where(below, 1.0, 0.0), axis=1, keepdims=True)
    before = jnp.max(jnp.where(below, cum_row, 0.0), axis=1, keepdims=True)
    row = iota((2 * LANES, 1), 0)
    place = 2.0 * source + ((row & 63).astype(F32) - before)
    key_col = 4 * place.astype(I32) + 2 * ((row >> 6) & 1) + (row >> 7)
    patch = (iota((NDEV, LANES), 1) & 63).astype(F32)
    below = cum_col <= patch
    source = jnp.sum(jnp.where(below, 1.0, 0.0), axis=0, keepdims=True)
    before = jnp.max(jnp.where(below, cum_col, 0.0), axis=0, keepdims=True)
    lane = iota((1, LANES), 1)
    place = 2.0 * source + ((lane & 63).astype(F32) - before)
    key_row = 2 * place.astype(I32) + (lane >> 6)
    return key_col, key_row


def slot_keys(me, counts, owner):
    lane = iota((1, NDEV), 1)
    start = jnp.sum(jnp.where(lane < me, counts, 0.0), axis=1, keepdims=True).astype(I32)
    count = jnp.sum(jnp.where(lane == me, counts, 0.0), axis=1, keepdims=True).astype(I32)
    position = iota((CAP, 1), 0) + start
    rows = dot(one_hot(iota((CAP, 64), 1) == (position >> 7)), owner.astype(F32).astype(BF16))
    here = iota((CAP, LANES), 1) == (position & 127)
    owner_col = jnp.sum(jnp.where(here, rows, 0.0), axis=1, keepdims=True)
    owner_row = col_to_row(owner_col)
    same = owner_col == owner_row
    first = iota((CAP, CAP), 0)
    second = iota((CAP, CAP), 1)
    rank_col = jnp.sum(jnp.where(same & (second < first), 1.0, 0.0), axis=1, keepdims=True)
    rank_row = jnp.sum(jnp.where(same & (first < second), 1.0, 0.0), axis=0, keepdims=True)
    key_col = (2.0 * owner_col + rank_col).astype(I32)
    key_row = (2.0 * owner_row + rank_row).astype(I32)
    key_col = jnp.where(iota((CAP, 1), 0) < count, key_col, -1)
    key_row = jnp.where(iota((1, CAP), 1) < count, key_row, -1)
    return key_col, key_row


def split3(value):
    high = value.astype(BF16).astype(F32)
    middle = (value - high).astype(BF16).astype(F32)
    low = value - high - middle
    return high, middle, low


def with_bias(weight, bias_col, width):
    rows, depth = weight.shape
    tail = iota((rows, width - depth), 1)
    high, middle, low = split3(bias_col)
    extra = jnp.where(tail == 0, high, jnp.where(tail == 1, middle, jnp.where(tail == 2, low, 0.0)))
    return jnp.concatenate([weight, extra], axis=1).astype(BF16)


def closure_body(
    counts_ref, owner_ref, fields_ref, in_weight_ref, in_bias_ref, depth_weight_ref, depth_bias_ref,
    mix_weight_ref, mix_bias_ref, out_weight_ref, out_bias_ref,
    out_ref,
    spread, outgoing, incoming, grid_in, ones_mask, hidden, taps, taps_bias, depth, result, scatter,
    place_slots, x_send, x_recv, y_send, y_recv, c_send, c_recv, leaving, arrived,
    send_sem, recv_sem, halo_send, halo_recv, back_send, back_recv,
):
    gx = lax.axis_index("gx")
    yz = lax.axis_index("yz")
    me = gx * N_YZ + yz
    at_x = [lax.rem(gx + step, 4) for step in range(4)]
    at_y = [8 * lax.rem(lax.div(yz, 8) + step, 4) for step in range(4)]
    at_z = [2 * lax.rem(lax.div(yz, 2) + step, 4) for step in range(4)]
    at_core = [lax.rem(yz + step, 2) for step in range(2)]

    def coords(step):
        where = (at_x[step[0]], at_y[step[1]] + at_z[step[2]] + at_core[step[3]])
        return where[0] * N_YZ + where[1], where

    barrier = pltpu.get_barrier_semaphore()
    for step in STEPS:
        pl.semaphore_signal(barrier, inc=1, device_id=coords(step)[1], device_id_type=MESH)

    counts = counts_ref[...].astype(F32)
    owner = owner_ref[...]
    key_col, key_row = slot_keys(me, counts, owner)
    select = one_hot(iota((SLOTS, CAP), 0) == key_row)
    for c in range(CIN):
        rows = dot(select, fields_ref[c])
        for part in range(4):
            spread[c, pl.ds(part, SLOTS, stride=4), :] = rows[:, part * LANES : (part + 1) * LANES]
    for c in range(CIN):
        outgoing[:, :, c * LANES : (c + 1) * LANES] = (
            spread[c].reshape(NDEV, 8, LANES).astype(BF16)
        )

    pl.semaphore_wait(barrier, NDEV - 1)

    for step in STEPS:
        other, where = coords(step)
        pltpu.make_async_remote_copy(
            src_ref=outgoing.at[other], dst_ref=incoming.at[me],
            send_sem=send_sem, recv_sem=recv_sem, device_id=where, device_id_type=MESH,
        ).start()
    incoming[me] = outgoing[me]

    cum_col = run_cumulative(me, counts, owner)
    brick_col, brick_row = brick_keys(cum_col)
    gather = one_hot(iota((2 * LANES, ROWS), 1) == brick_col)
    scatter[...] = one_hot(iota((2 * SLOTS, LANES), 0) == brick_row)
    for half in range(2):
        wanted = jnp.where(key_col < 0, -1, 2 * key_col + half)
        place_slots[half * CAP : (half + 1) * CAP, :] = one_hot(
            iota((CAP, 2 * SLOTS), 1) == wanted
        )
    lane = iota((1, LANES), 1)
    high_x = ((lane >> 6) & 1) == 1
    along_y = (lane >> 4) & 3
    along_z = lane & 15
    keep_low = jnp.where(gx > 0, 1.0, 0.0).astype(F32)
    keep_high = jnp.where(gx < N_GX - 1, 1.0, 0.0).astype(F32)
    for x in range(6):
        mask = jnp.ones((1, LANES), F32)
        if x == 0:
            mask = jnp.where(high_x, 1.0, keep_low)
        if x == 5:
            mask = jnp.where(high_x, keep_high, 1.0)
        ones_mask[x] = jnp.broadcast_to(mask, (16, LANES))
    depth_weight = depth_weight_ref[...]
    for tap in range(27):
        taps[tap] = jnp.broadcast_to(depth_weight[:, tap : tap + 1], (HID, LANES))
    taps_bias[...] = jnp.broadcast_to(row_to_col(depth_bias_ref[...]), (HID, LANES))
    in_weight = in_weight_ref[...].astype(F32)
    in_cols = [row_to_col(in_weight[c : c + 1, :]) for c in range(CIN)]
    column = iota((HID, 80), 1)
    base = jnp.zeros((HID, 80), F32)
    for c in range(CIN):
        base = jnp.where((column >> 4) == c, 0.5 * in_cols[c], base)
    in_bias = 0.5 * row_to_col(in_bias_ref[...])
    first_w = jnp.concatenate(
        [with_bias(jnp.where((column & 15) == cell, base, 0.0), in_bias, 96) for cell in range(16)],
        axis=0,
    )
    mix_w = with_bias(0.5 * mix_weight_ref[...].astype(F32), 0.5 * row_to_col(mix_bias_ref[...]), 48)
    out_w = with_bias(out_weight_ref[...].astype(F32), row_to_col(out_bias_ref[...]), 48)
    ones_cells = jnp.ones((16, 8 * LANES), BF16)

    every = pltpu.make_async_copy(
        outgoing.at[pl.ds(0, NDEV - 1)], incoming.at[pl.ds(0, NDEV - 1)], recv_sem
    )
    every.wait()

    bricks = dot(gather, incoming[...].reshape(ROWS, CIN * LANES))
    for c in range(CIN):
        for m in range(2):
            turned = bricks[m * LANES : (m + 1) * LANES, c * LANES : (c + 1) * LANES].T
            for p in range(2):
                grid_in[c, pl.ds((1 + 2 * m + p) * 80 + 8, 64), :] = turned[p * 64 : (p + 1) * 64]

    for c in range(CIN):
        x_send[0, c] = pltpu.roll(grid_in[c, pl.ds(4 * 80 + 8, 64), :], 64, 1).astype(BF16)
        x_send[1, c] = pltpu.roll(grid_in[c, pl.ds(1 * 80 + 8, 64), :], 64, 1).astype(BF16)
        last_y = [grid_in[c, pl.ds(x * 80 + 64, 8), :] for x in range(1, 5)]
        first_y = [grid_in[c, pl.ds(x * 80 + 8, 8), :] for x in range(1, 5)]
        y_send[0, c] = pltpu.roll(jnp.concatenate(last_y, axis=0), 80, 1).astype(BF16)
        y_send[1, c] = pltpu.roll(jnp.concatenate(first_y, axis=0), 48, 1).astype(BF16)
        c_send[0, c] = pltpu.roll(last_y[3], 16, 1).astype(BF16)
        c_send[1, c] = pltpu.roll(first_y[3], 112, 1).astype(BF16)
        c_send[2, c] = pltpu.roll(last_y[0], 16, 1).astype(BF16)
        c_send[3, c] = pltpu.roll(first_y[0], 112, 1).astype(BF16)
    up_x = lax.rem(gx + 1, N_GX)
    down_x = lax.rem(gx + N_GX - 1, N_GX)
    up_y = lax.rem(yz + 1, N_YZ)
    down_y = lax.rem(yz + N_YZ - 1, N_YZ)
    halo = []
    for source, target, where in (
        (x_send.at[0], x_recv.at[0], (up_x, yz)),
        (x_send.at[1], x_recv.at[1], (down_x, yz)),
        (y_send.at[0], y_recv.at[0], (gx, up_y)),
        (y_send.at[1], y_recv.at[1], (gx, down_y)),
        (c_send.at[0], c_recv.at[0], (up_x, up_y)),
        (c_send.at[1], c_recv.at[1], (up_x, down_y)),
        (c_send.at[2], c_recv.at[2], (down_x, up_y)),
        (c_send.at[3], c_recv.at[3], (down_x, down_y)),
    ):
        number = len(halo)
        copy = pltpu.make_async_remote_copy(
            src_ref=source, dst_ref=target, send_sem=halo_send.at[number],
            recv_sem=halo_recv.at[number], device_id=where, device_id_type=MESH,
        )
        copy.start()
        halo.append(copy)
    def first_group(x, pair):
        start = pl.multiple_of(x * 80 + pair * 16, 16)
        cells = [grid_in[c, pl.ds(start, 16), :] for c in range(CIN)]
        stacked = jnp.concatenate(cells + [ones_mask[x]], axis=0).astype(BF16)
        value = gelu_half(dot(first_w, stacked)).astype(BF16).astype(F32)
        for cell in range(16):
            y = 2 * pair + cell // 8
            z = cell % 8
            here = value[cell * HID : (cell + 1) * HID]
            hidden[x, y, 1 + z] = here
            if z == 7:
                hidden[x, y, 0] = jnp.where(
                    along_z == 0, pltpu.roll(here, 113, 1), pltpu.roll(here, 1, 1)
                )
            if z == 0:
                hidden[x, y, 9] = jnp.where(
                    along_z == 15, pltpu.roll(here, 15, 1), pltpu.roll(here, 127, 1)
                )

    def first_inner(x, carry):
        for pair in range(1, 4):
            first_group(x, pair)
        return carry

    lax.fori_loop(1, 5, first_inner, 0)

    for copy in halo:
        copy.wait()

    for c in range(CIN):
        low = jnp.where(high_x, x_send[0, c].astype(F32), keep_low * x_recv[0, c].astype(F32))
        high = jnp.where(high_x, keep_high * x_recv[1, c].astype(F32), x_send[1, c].astype(F32))
        grid_in[c, pl.ds(8, 64), :] = low
        grid_in[c, pl.ds(5 * 80 + 8, 64), :] = high
        for side in range(2):
            own = y_recv[side, c].astype(F32)
            corner_low = keep_low * c_recv[0 + side, c].astype(F32)
            corner_high = keep_high * c_recv[2 + side, c].astype(F32)
            edge_lane = along_y == (0 if side == 0 else 3)
            for x in range(6):
                if x == 0:
                    far = jnp.where(high_x, pltpu.roll(own[24:32], 64, 1), corner_low)
                elif x == 5:
                    far = jnp.where(high_x, corner_high, pltpu.roll(own[0:8], 64, 1))
                else:
                    far = own[8 * (x - 1) : 8 * x]
                near = grid_in[c, pl.ds(x * 80 + (64 if side == 0 else 8), 8), :]
                near = pltpu.roll(near, 16 if side == 0 else 112, 1)
                grid_in[c, pl.ds(x * 80 + (0 if side == 0 else 72), 8), :] = jnp.where(
                    edge_lane, far, near
                )

    def first_edge_y(x, carry):
        first_group(x, 0)
        first_group(x, 4)
        return carry

    def first_edge_x(pair, carry):
        first_group(0, pair)
        first_group(5, pair)
        return carry

    lax.fori_loop(1, 5, first_edge_y, 0)
    lax.fori_loop(0, 5, first_edge_x, 0)

    def plane(x, carry):
        def depth_part(group, inner):
            y = lax.div(group, 4)
            rows = pl.ds(pl.multiple_of(8 * lax.rem(group, 4), 8), 8)
            total = [taps_bias[rows, :]] * 8
            for a in range(3):
                for b in range(3):
                    cells = [hidden[x + a, y + b, z, rows, :] for z in range(10)]
                    for c in range(3):
                        weight = taps[9 * a + 3 * b + c, rows, :]
                        for z in range(8):
                            total[z] = total[z] + weight * cells[z + c]
            for z in range(8):
                depth[y, z, rows, :] = total[z]
            return inner

        lax.fori_loop(0, 32, depth_part, 0)

        def mix_part(y, inner):
            columns = [depth[y, z].astype(BF16) for z in range(8)]
            stacked = jnp.concatenate([jnp.concatenate(columns, axis=1), ones_cells], axis=0)
            mixed = gelu_half(dot(mix_w, stacked)).astype(BF16)
            field = dot(out_w, jnp.concatenate([mixed, ones_cells], axis=0))
            for z in range(8):
                start = pl.multiple_of(y * 64 + 8 * z, 8)
                result[pl.ds(start, COUT), :] = field[:, z * LANES : (z + 1) * LANES]
            return inner

        lax.fori_loop(0, 8, mix_part, 0)

        odd = lax.rem(x, 2)
        turned = []
        for pair in range(3):
            first = result[pl.ds(2 * pair + odd, 64, stride=8), :]
            second = result[pl.ds(2 * pair + 1 - odd, 64, stride=8), :]
            turned.append(jnp.concatenate([first, second], axis=0).T.astype(BF16))
        packed = jnp.concatenate(turned, axis=1)
        leaving[x] = dot(scatter[...], packed).reshape(NDEV, 4, 3 * LANES).astype(BF16)
        for step in STEPS:
            other, where = coords(step)
            pltpu.make_async_remote_copy(
                src_ref=leaving.at[x, other], dst_ref=arrived.at[x, me],
                send_sem=back_send, recv_sem=back_recv.at[x], device_id=where, device_id_type=MESH,
            ).start()
        arrived[x, me] = leaving[x, me]
        return carry

    lax.fori_loop(0, 4, plane, 0)

    low_half = iota((1, LANES), 1) < 64
    taken = []
    for x in range(4):
        pltpu.make_async_copy(
            leaving.at[x, pl.ds(0, NDEV - 1)], arrived.at[x, pl.ds(0, NDEV - 1)], back_recv.at[x]
        ).wait()
        taken.append(dot(place_slots[...], arrived[x].reshape(2 * SLOTS, 3 * LANES)))
        if x % 2 == 0:
            continue
        for half in range(2):
            rows = slice(half * CAP, (half + 1) * CAP)
            lanes = slice((2 * half + x // 2) * LANES, (2 * half + x // 2 + 1) * LANES)
            for pair in range(3):
                even = taken[x - 1][rows, pair * LANES : (pair + 1) * LANES]
                odd = taken[x][rows, pair * LANES : (pair + 1) * LANES]
                out_ref[2 * pair, :, lanes] = jnp.where(low_half, even, odd).astype(BF16)
                out_ref[2 * pair + 1, :, lanes] = pltpu.roll(
                    jnp.where(low_half, odd, even), 64, 1
                ).astype(BF16)
    pltpu.make_async_copy(
        outgoing.at[pl.ds(0, NDEV - 1)], incoming.at[pl.ds(0, NDEV - 1)], send_sem
    ).wait()
    pltpu.make_async_copy(
        leaving.at[:, pl.ds(0, NDEV - 1)], arrived.at[:, pl.ds(0, NDEV - 1)], back_send
    ).wait()


VMEM = pl.BlockSpec(memory_space=pltpu.VMEM)


def shards(
    fields, solver_counts, cnn_owner, in_weight, in_bias, depth_weight, depth_bias,
    mix_weight, mix_bias, out_weight, out_bias,
):
    closure = pl.pallas_call(
        closure_body,
        out_shape=jax.ShapeDtypeStruct((COUT, CAP, 4 * LANES), BF16),
        in_specs=[VMEM] * 11,
        out_specs=VMEM,
        scratch_shapes=[
            pltpu.VMEM((CIN, ROWS, LANES), F32),
            pltpu.VMEM((NDEV, 8, CIN * LANES), BF16),
            pltpu.VMEM((NDEV, 8, CIN * LANES), BF16),
            pltpu.VMEM((CIN, 480, LANES), F32),
            pltpu.VMEM((6, 16, LANES), F32),
            pltpu.VMEM((6, 10, 10, HID, LANES), F32),
            pltpu.VMEM((27, HID, LANES), F32),
            pltpu.VMEM((HID, LANES), F32),
            pltpu.VMEM((8, 8, HID, LANES), F32),
            pltpu.VMEM((512, LANES), F32),
            pltpu.VMEM((2 * SLOTS, LANES), BF16),
            pltpu.VMEM((2 * CAP, 2 * SLOTS), BF16),
            pltpu.VMEM((2, CIN, 64, LANES), BF16),
            pltpu.VMEM((2, CIN, 64, LANES), BF16),
            pltpu.VMEM((2, CIN, 32, LANES), BF16),
            pltpu.VMEM((2, CIN, 32, LANES), BF16),
            pltpu.VMEM((4, CIN, 8, LANES), BF16),
            pltpu.VMEM((4, CIN, 8, LANES), BF16),
            pltpu.VMEM((4, NDEV, 4, 3 * LANES), BF16),
            pltpu.VMEM((4, NDEV, 4, 3 * LANES), BF16),
            pltpu.SemaphoreType.DMA,
            pltpu.SemaphoreType.DMA,
            pltpu.SemaphoreType.DMA((8,)),
            pltpu.SemaphoreType.DMA((8,)),
            pltpu.SemaphoreType.DMA,
            pltpu.SemaphoreType.DMA((4,)),
        ],
        compiler_params=pltpu.CompilerParams(
            collective_id=0, has_side_effects=True, vmem_limit_bytes=60 * 1024 * 1024
        ),
        name="closure",
    )(
        solver_counts.reshape(1, NDEV),
        cnn_owner.reshape(64, LANES),
        jnp.transpose(fields, (1, 0, 2)),
        jnp.transpose(in_weight),
        in_bias.reshape(1, HID),
        depth_weight,
        depth_bias.reshape(1, HID),
        mix_weight,
        mix_bias.reshape(1, HID),
        out_weight,
        out_bias.reshape(1, COUT),
    )
    return jnp.transpose(closure, (1, 0, 2))


def solution(mesh):
    return jax.shard_map(
        shards,
        mesh=mesh,
        in_specs=(P(("gx", "yz"), None, None), P(), P(), P(), P(), P(), P(), P(), P(), P(), P()),
        out_specs=P(("gx", "yz"), None, None),
        check_vma=False,
    )
```

```python
import jax
import jax.numpy as jnp
from jax import lax
from jax.experimental import pallas as pl
from jax.experimental.pallas import tpu as pltpu
from jax.sharding import PartitionSpec as P

MESH = pl.DeviceIdType.MESH
NDEV = 128
N_GX = 4
N_YZ = 32
CAP = 192
CIN = 5
HID = 32
COUT = 6
LANES = 128
SLOTS = 2 * NDEV
ROWS = 4 * SLOTS
F32 = jnp.float32
BF16 = jnp.bfloat16
I32 = jnp.int32
GELU_A = 2.0 * 0.7978845608028654
GELU_B = 8.0 * 0.7978845608028654 * 0.044715


STEPS = sorted(
    [(x, y, z, c) for x in range(4) for y in range(4) for z in range(4) for c in range(2)],
    key=lambda step: -sum(min(part, 4 - part) for part in step[:3]),
)[:-2] + [(0, 0, 0, 1)]


def iota(shape, dim):
    return lax.broadcasted_iota(I32, shape, dim)


def dot(a, b):
    return jnp.dot(a, b, preferred_element_type=F32)


def one_hot(condition):
    return jnp.where(condition, 1.0, 0.0).astype(BF16)


def row_to_col(row):
    count = row.shape[1]
    same = iota((count, count), 0) == iota((count, count), 1)
    return jnp.sum(jnp.where(same, row, 0.0), axis=1, keepdims=True)


def col_to_row(col):
    count = col.shape[0]
    same = iota((count, count), 0) == iota((count, count), 1)
    return jnp.sum(jnp.where(same, col, 0.0), axis=0, keepdims=True)


def gelu_half(y):
    return y + y * jnp.tanh(y * (GELU_A + GELU_B * (y * y)))


def run_cumulative(me, counts, owner):
    lower = iota((NDEV, NDEV), 1) <= iota((NDEV, NDEV), 0)
    run_end = jnp.sum(jnp.where(lower, counts, 0.0), axis=1, keepdims=True).astype(I32)
    mine = one_hot(owner == me)
    rows = iota((NDEV, 64), 1)
    whole = dot(one_hot(rows < (run_end >> 7)), mine)
    part = dot(one_hot(rows == (run_end >> 7)), mine)
    inside = iota((NDEV, LANES), 1) < (run_end & 127)
    return jnp.sum(whole + jnp.where(inside, part, 0.0), axis=1, keepdims=True)


def brick_keys(cum_col):
    cum_row = col_to_row(cum_col)
    row = iota((2 * LANES, NDEV), 0)
    patch = (row & 63).astype(F32)
    below = cum_row <= patch
    source = jnp.sum(jnp.where(below, 1.0, 0.0), axis=1, keepdims=True)
    before = jnp.max(jnp.where(below, cum_row, 0.0), axis=1, keepdims=True)
    row = iota((2 * LANES, 1), 0)
    place = 2.0 * source + ((row & 63).astype(F32) - before)
    key_col = 4 * place.astype(I32) + 2 * ((row >> 6) & 1) + (row >> 7)
    patch = (iota((NDEV, LANES), 1) & 63).astype(F32)
    below = cum_col <= patch
    source = jnp.sum(jnp.where(below, 1.0, 0.0), axis=0, keepdims=True)
    before = jnp.max(jnp.where(below, cum_col, 0.0), axis=0, keepdims=True)
    lane = iota((1, LANES), 1)
    place = 2.0 * source + ((lane & 63).astype(F32) - before)
    key_row = 2 * place.astype(I32) + (lane >> 6)
    return key_col, key_row


def slot_keys(me, counts, owner):
    lane = iota((1, NDEV), 1)
    start = jnp.sum(jnp.where(lane < me, counts, 0.0), axis=1, keepdims=True).astype(I32)
    count = jnp.sum(jnp.where(lane == me, counts, 0.0), axis=1, keepdims=True).astype(I32)
    position = iota((CAP, 1), 0) + start
    rows = dot(one_hot(iota((CAP, 64), 1) == (position >> 7)), owner.astype(F32).astype(BF16))
    here = iota((CAP, LANES), 1) == (position & 127)
    owner_col = jnp.sum(jnp.where(here, rows, 0.0), axis=1, keepdims=True)
    owner_row = col_to_row(owner_col)
    same = owner_col == owner_row
    first = iota((CAP, CAP), 0)
    second = iota((CAP, CAP), 1)
    rank_col = jnp.sum(jnp.where(same & (second < first), 1.0, 0.0), axis=1, keepdims=True)
    rank_row = jnp.sum(jnp.where(same & (first < second), 1.0, 0.0), axis=0, keepdims=True)
    key_col = (2.0 * owner_col + rank_col).astype(I32)
    key_row = (2.0 * owner_row + rank_row).astype(I32)
    key_col = jnp.where(iota((CAP, 1), 0) < count, key_col, -1)
    key_row = jnp.where(iota((1, CAP), 1) < count, key_row, -1)
    return key_col, key_row


def split3(value):
    high = value.astype(BF16).astype(F32)
    middle = (value - high).astype(BF16).astype(F32)
    low = value - high - middle
    return high, middle, low


def repeat_rows(value, count):
    rows, lanes = value.shape
    return jnp.broadcast_to(value[:, None, :], (rows, count, lanes)).reshape(rows * count, lanes)


def first_weights(in_weight, in_bias, z_halo):
    lane = iota((HID, 96), 1)
    base = jnp.zeros((HID, 96), F32)
    for c in range(CIN):
        base = jnp.where((lane >> 4) == c, 0.5 * row_to_col(in_weight[c : c + 1, :]), base)
    for number, part in enumerate(split3(0.5 * row_to_col(in_bias))):
        for mask in range(3):
            base = jnp.where(lane == 80 + 3 * mask + number, part, base)
    base = repeat_rows(base, 16)
    lane = iota((16 * HID, 96), 1)
    cell = iota((16 * HID, 96), 0) & 15
    first = jnp.where(cell < 2, 83, jnp.where((cell >> 1) == 5, 86, 80)) if z_halo else 80
    own = jnp.where(lane < 80, cell, -1) == (lane & 15)
    keep = own | ((lane >= first) & (lane < first + 3))
    return jnp.where(keep, base, 0.0).astype(BF16)


def over_cells(weight):
    rows, depth = weight.shape
    widen = one_hot(iota((depth, 8 * depth), 0) == (iota((depth, 8 * depth), 1) >> 3))
    wide = repeat_rows(dot(weight, widen), 8)
    keep = (iota(wide.shape, 0) & 7) == (iota(wide.shape, 1) & 7)
    return jnp.where(keep, wide, 0.0).astype(BF16)


def tap_places(x, pair):
    lane = iota((1, 2048), 1)
    z = lane >> 8
    side = (lane >> 7) & 1
    row = lane & 127
    edge = row - 96
    far = edge & 15
    regular = row < 96
    in_x = jnp.where(regular, row >> 4, far >> 1)
    in_y = jnp.where(regular, (row >> 3) & 1, far & 1)
    in_z = jnp.where(regular, row & 7, jnp.where(edge >= 16, 8, -1))
    a = in_x - x
    b = 2 * side + in_y - pair
    c = in_z - z + 1
    valid = (a >= 0) & (a <= 2) & (b >= 0) & (b <= 2) & (c >= 0) & (c <= 2)
    valid = valid & (regular | (far < 12))
    tap = jnp.where(valid, 9 * a + 3 * b + c, -1)
    return one_hot(iota((32, 2048), 0) == tap)


def closure_body(
    counts_ref, owner_ref, fields_ref, in_weight_ref, in_bias_ref, depth_weight_ref, depth_bias_ref,
    mix_weight_ref, mix_bias_ref, out_weight_ref, out_bias_ref,
    out_ref,
    spread, outgoing, incoming, grid_in, ones_mask, hidden, band, depth_bias, mix_bias, depth, result, scatter,
    place_slots, x_send, x_recv, y_send, y_recv, c_send, c_recv, leaving, arrived,
    send_sem, recv_sem, halo_send, halo_recv, back_send, back_recv,
):
    gx = lax.axis_index("gx")
    yz = lax.axis_index("yz")
    me = gx * N_YZ + yz
    at_x = [lax.rem(gx + step, 4) for step in range(4)]
    at_y = [8 * lax.rem(lax.div(yz, 8) + step, 4) for step in range(4)]
    at_z = [2 * lax.rem(lax.div(yz, 2) + step, 4) for step in range(4)]
    at_core = [lax.rem(yz + step, 2) for step in range(2)]

    def coords(step):
        where = (at_x[step[0]], at_y[step[1]] + at_z[step[2]] + at_core[step[3]])
        return where[0] * N_YZ + where[1], where

    barrier = pltpu.get_barrier_semaphore()
    for step in STEPS:
        pl.semaphore_signal(barrier, inc=1, device_id=coords(step)[1], device_id_type=MESH)

    counts = counts_ref[...].astype(F32)
    owner = owner_ref[...]
    key_col, key_row = slot_keys(me, counts, owner)
    select = one_hot(iota((SLOTS, CAP), 0) == key_row)
    for c in range(CIN):
        rows = dot(select, fields_ref[c])
        for part in range(4):
            spread[c, pl.ds(part, SLOTS, stride=4), :] = rows[:, part * LANES : (part + 1) * LANES]
    for c in range(CIN):
        outgoing[:, :, c * LANES : (c + 1) * LANES] = (
            spread[c].reshape(NDEV, 8, LANES).astype(BF16)
        )

    pl.semaphore_wait(barrier, NDEV - 1)

    for step in STEPS:
        other, where = coords(step)
        pltpu.make_async_remote_copy(
            src_ref=outgoing.at[other], dst_ref=incoming.at[me],
            send_sem=send_sem, recv_sem=recv_sem, device_id=where, device_id_type=MESH,
        ).start()
    incoming[me] = outgoing[me]

    cum_col = run_cumulative(me, counts, owner)
    brick_col, brick_row = brick_keys(cum_col)
    gather = one_hot(iota((2 * LANES, ROWS), 1) == brick_col)
    scatter[...] = one_hot(iota((2 * SLOTS, LANES), 0) == brick_row)
    for half in range(2):
        wanted = jnp.where(key_col < 0, -1, 2 * key_col + half)
        place_slots[half * CAP : (half + 1) * CAP, :] = one_hot(
            iota((CAP, 2 * SLOTS), 1) == wanted
        )
    lane = iota((1, LANES), 1)
    high_x = ((lane >> 6) & 1) == 1
    along_y = (lane >> 4) & 3
    along_z = lane & 15
    keep_low = jnp.where(gx > 0, 1.0, 0.0).astype(F32)
    keep_high = jnp.where(gx < N_GX - 1, 1.0, 0.0).astype(F32)
    masks = [jnp.ones((1, LANES), F32)] * 6
    masks[0] = jnp.where(high_x, 1.0, keep_low)
    masks[5] = jnp.where(high_x, keep_high, 1.0)
    for x in range(6):
        ones_mask[x] = jnp.broadcast_to(masks[x], (16, LANES))
    line = iota((16, LANES), 0)
    ones_mask[6] = jnp.where(line < 3, 1.0, jnp.where(line < 6, masks[0], masks[5]))
    in_weight = in_weight_ref[...].astype(F32)
    first_w = [first_weights(in_weight, in_bias_ref[...], z_halo) for z_halo in (False, True)]
    mix_w = over_cells((0.5 * mix_weight_ref[...].astype(F32)).astype(BF16))
    out_w = over_cells(out_weight_ref[...])
    depth_bias[...] = repeat_rows(
        jnp.broadcast_to(row_to_col(depth_bias_ref[...]), (HID, LANES)), 8
    )
    mix_bias[...] = repeat_rows(
        jnp.broadcast_to(0.5 * row_to_col(mix_bias_ref[...]), (HID, LANES)), 8
    )
    out_bias = repeat_rows(jnp.broadcast_to(row_to_col(out_bias_ref[...]), (COUT, LANES)), 8)
    taps = jnp.concatenate([depth_weight_ref[...], jnp.zeros((HID, 5), F32)], axis=1).astype(BF16)

    def band_rows(group, carry):
        rows = dot(taps, tap_places(lax.div(group, 2), lax.rem(group, 2)))
        for z in range(8):
            start = pl.multiple_of((group * 8 + z) * HID, HID)
            for side in range(2):
                first = z * 256 + side * LANES
                band[side, pl.ds(start, HID), :] = rows[:, first : first + LANES]
        return carry

    lax.fori_loop(0, 8, band_rows, 0)
    grid_in[...] = jnp.zeros_like(grid_in)

    every = pltpu.make_async_copy(
        outgoing.at[pl.ds(0, NDEV - 1)], incoming.at[pl.ds(0, NDEV - 1)], recv_sem
    )
    every.wait()

    def place(x, y):
        return (y // 2) * 128 + x * 16 + (y % 2) * 8

    def get(c, x, y):
        return grid_in[c, place(x, y) : place(x, y) + 8, :]

    def put(c, x, y, value):
        grid_in[c, place(x, y) : place(x, y) + 8, :] = value

    bricks = dot(gather, incoming[...].reshape(ROWS, CIN * LANES))
    for c in range(CIN):
        for m in range(2):
            turned = bricks[m * LANES : (m + 1) * LANES, c * LANES : (c + 1) * LANES].T
            for p in range(2):
                for y in range(8):
                    first = p * 64 + y * 8
                    put(c, 1 + 2 * m + p, 1 + y, turned[first : first + 8])

    for c in range(CIN):
        for side, x in enumerate((4, 1)):
            cells = jnp.concatenate([get(c, x, y) for y in range(1, 9)], axis=0)
            x_send[side, c] = pltpu.roll(cells, 64, 1).astype(BF16)
        last_y = [get(c, x, 8) for x in range(1, 5)]
        first_y = [get(c, x, 1) for x in range(1, 5)]
        y_send[0, c] = pltpu.roll(jnp.concatenate(last_y, axis=0), 80, 1).astype(BF16)
        y_send[1, c] = pltpu.roll(jnp.concatenate(first_y, axis=0), 48, 1).astype(BF16)
        c_send[0, c] = pltpu.roll(last_y[3], 16, 1).astype(BF16)
        c_send[1, c] = pltpu.roll(first_y[3], 112, 1).astype(BF16)
        c_send[2, c] = pltpu.roll(last_y[0], 16, 1).astype(BF16)
        c_send[3, c] = pltpu.roll(first_y[0], 112, 1).astype(BF16)
    up_x = lax.rem(gx + 1, N_GX)
    down_x = lax.rem(gx + N_GX - 1, N_GX)
    up_y = lax.rem(yz + 1, N_YZ)
    down_y = lax.rem(yz + N_YZ - 1, N_YZ)
    halo = []
    for source, target, where in (
        (x_send.at[0], x_recv.at[0], (up_x, yz)),
        (x_send.at[1], x_recv.at[1], (down_x, yz)),
        (y_send.at[0], y_recv.at[0], (gx, up_y)),
        (y_send.at[1], y_recv.at[1], (gx, down_y)),
        (c_send.at[0], c_recv.at[0], (up_x, up_y)),
        (c_send.at[1], c_recv.at[1], (up_x, down_y)),
        (c_send.at[2], c_recv.at[2], (down_x, up_y)),
        (c_send.at[3], c_recv.at[3], (down_x, down_y)),
    ):
        number = len(halo)
        copy = pltpu.make_async_remote_copy(
            src_ref=source, dst_ref=target, send_sem=halo_send.at[number],
            recv_sem=halo_recv.at[number], device_id=where, device_id_type=MESH,
        )
        copy.start()
        halo.append(copy)
    def first_group(pair, tile):
        start = pl.multiple_of(pair * 128 + tile * 16, 16)
        cells = [grid_in[c, pl.ds(start, 16), :] for c in range(CIN)]
        stacked = jnp.concatenate(cells + [ones_mask[min(tile, 6)]], axis=0).astype(BF16)
        value = gelu_half(dot(first_w[tile > 5], stacked)).astype(BF16)
        for h in range(HID):
            hidden[h, pl.ds(start, 16), :] = value[16 * h : 16 * h + 16]

    def first_inner(pair, carry):
        for tile in range(1, 5):
            first_group(pair, tile)
        return carry

    lax.fori_loop(1, 4, first_inner, 0)

    for copy in halo:
        copy.wait()

    for c in range(CIN):
        low = jnp.where(high_x, x_send[0, c].astype(F32), keep_low * x_recv[0, c].astype(F32))
        high = jnp.where(high_x, keep_high * x_recv[1, c].astype(F32), x_send[1, c].astype(F32))
        for y in range(8):
            put(c, 0, 1 + y, low[8 * y : 8 * y + 8])
            put(c, 5, 1 + y, high[8 * y : 8 * y + 8])
        for side in range(2):
            own = y_recv[side, c].astype(F32)
            corner_low = keep_low * c_recv[0 + side, c].astype(F32)
            corner_high = keep_high * c_recv[2 + side, c].astype(F32)
            edge_lane = along_y == (0 if side == 0 else 3)
            for x in range(6):
                if x == 0:
                    far = jnp.where(high_x, pltpu.roll(own[24:32], 64, 1), corner_low)
                elif x == 5:
                    far = jnp.where(high_x, corner_high, pltpu.roll(own[0:8], 64, 1))
                else:
                    far = own[8 * (x - 1) : 8 * x]
                near = pltpu.roll(get(c, x, 8 if side == 0 else 1), 16 if side == 0 else 112, 1)
                put(c, x, 0 if side == 0 else 9, jnp.where(edge_lane, far, near))
        for pair in range(5):
            below = grid_in[c, pl.ds(pair * 128 + 7, 12, stride=8), :]
            above = grid_in[c, pl.ds(pair * 128, 12, stride=8), :]
            grid_in[c, pair * 128 + 96 : pair * 128 + 108, :] = jnp.where(
                along_z == 0, pltpu.roll(below, 113, 1), pltpu.roll(below, 1, 1)
            )
            grid_in[c, pair * 128 + 112 : pair * 128 + 124, :] = jnp.where(
                along_z == 15, pltpu.roll(above, 15, 1), pltpu.roll(above, 127, 1)
            )

    def first_edge_y(side, carry):
        for tile in range(1, 5):
            first_group(4 * side, tile)
        return carry

    def first_edge_x(pair, carry):
        for tile in (0, 5, 6, 7):
            first_group(pair, tile)
        return carry

    lax.fori_loop(0, 2, first_edge_y, 0)
    lax.fori_loop(0, 5, first_edge_x, 0)

    def depth_part(group, carry):
        parts = []
        for number in range(2):
            h = 2 * group + number
            weight = jnp.concatenate(
                [band[side, pl.ds(h, 64, stride=HID), :] for side in range(2)], axis=1
            ).astype(BF16)
            cells = [hidden[h, 128 * pair : 128 * pair + 256, :] for pair in range(4)]
            parts.append(dot(weight, jnp.concatenate(cells, axis=1)))
        start = pl.multiple_of(16 * group, 16)
        bias = depth_bias[pl.ds(start, 16), :]
        for x in range(4):
            for y in range(8):
                rows = slice(16 * x + 8 * (y % 2), 16 * x + 8 * (y % 2) + 8)
                lanes = slice((y // 2) * LANES, (y // 2 + 1) * LANES)
                both = jnp.concatenate([part[rows, lanes] for part in parts], axis=0)
                depth[x, y, pl.ds(start, 16), :] = (both + bias).astype(BF16)
        return carry

    lax.fori_loop(0, 16, depth_part, 0)

    def plane(x, carry):
        def mix_part(group, inner):
            for number in range(4):
                y = 4 * group + number
                mixed = dot(mix_w, depth[x, y]) + mix_bias[...]
                field = dot(out_w, gelu_half(mixed).astype(BF16)) + out_bias
                for f in range(COUT):
                    start = pl.multiple_of(f * 64 + 8 * y, 8)
                    result[pl.ds(start, 8), :] = field[8 * f : 8 * f + 8]
            return inner

        lax.fori_loop(0, 2, mix_part, 0)

        odd = lax.rem(x, 2)
        turned = []
        for pair in range(3):
            first = result[pl.ds(pl.multiple_of((2 * pair + odd) * 64, 64), 64), :]
            second = result[pl.ds(pl.multiple_of((2 * pair + 1 - odd) * 64, 64), 64), :]
            turned.append(jnp.concatenate([first, second], axis=0).T.astype(BF16))
        packed = jnp.concatenate(turned, axis=1)
        leaving[x] = dot(scatter[...], packed).reshape(NDEV, 4, 3 * LANES).astype(BF16)
        for step in STEPS:
            other, where = coords(step)
            pltpu.make_async_remote_copy(
                src_ref=leaving.at[x, other], dst_ref=arrived.at[x, me],
                send_sem=back_send, recv_sem=back_recv.at[x], device_id=where, device_id_type=MESH,
            ).start()
        arrived[x, me] = leaving[x, me]
        return carry

    lax.fori_loop(0, 4, plane, 0)

    low_half = iota((1, LANES), 1) < 64
    taken = []
    for x in range(4):
        pltpu.make_async_copy(
            leaving.at[x, pl.ds(0, NDEV - 1)], arrived.at[x, pl.ds(0, NDEV - 1)], back_recv.at[x]
        ).wait()
        taken.append(dot(place_slots[...], arrived[x].reshape(2 * SLOTS, 3 * LANES)))
        if x % 2 == 0:
            continue
        for half in range(2):
            rows = slice(half * CAP, (half + 1) * CAP)
            lanes = slice((2 * half + x // 2) * LANES, (2 * half + x // 2 + 1) * LANES)
            for pair in range(3):
                even = taken[x - 1][rows, pair * LANES : (pair + 1) * LANES]
                odd = taken[x][rows, pair * LANES : (pair + 1) * LANES]
                out_ref[2 * pair, :, lanes] = jnp.where(low_half, even, odd).astype(BF16)
                out_ref[2 * pair + 1, :, lanes] = pltpu.roll(
                    jnp.where(low_half, odd, even), 64, 1
                ).astype(BF16)
    pltpu.make_async_copy(
        outgoing.at[pl.ds(0, NDEV - 1)], incoming.at[pl.ds(0, NDEV - 1)], send_sem
    ).wait()
    pltpu.make_async_copy(
        leaving.at[:, pl.ds(0, NDEV - 1)], arrived.at[:, pl.ds(0, NDEV - 1)], back_send
    ).wait()


VMEM = pl.BlockSpec(memory_space=pltpu.VMEM)


def shards(
    fields, solver_counts, cnn_owner, in_weight, in_bias, depth_weight, depth_bias,
    mix_weight, mix_bias, out_weight, out_bias,
):
    closure = pl.pallas_call(
        closure_body,
        out_shape=jax.ShapeDtypeStruct((COUT, CAP, 4 * LANES), BF16),
        in_specs=[VMEM] * 11,
        out_specs=VMEM,
        scratch_shapes=[
            pltpu.VMEM((CIN, ROWS, LANES), F32),
            pltpu.VMEM((NDEV, 8, CIN * LANES), BF16),
            pltpu.VMEM((NDEV, 8, CIN * LANES), BF16),
            pltpu.VMEM((CIN, 640, LANES), F32),
            pltpu.VMEM((7, 16, LANES), F32),
            pltpu.VMEM((HID, 640, LANES), BF16),
            pltpu.VMEM((2, 64 * HID, LANES), F32),
            pltpu.VMEM((8 * HID, LANES), F32),
            pltpu.VMEM((8 * HID, LANES), F32),
            pltpu.VMEM((4, 8, 8 * HID, LANES), BF16),
            pltpu.VMEM((64 * COUT, LANES), F32),
            pltpu.VMEM((2 * SLOTS, LANES), BF16),
            pltpu.VMEM((2 * CAP, 2 * SLOTS), BF16),
            pltpu.VMEM((2, CIN, 64, LANES), BF16),
            pltpu.VMEM((2, CIN, 64, LANES), BF16),
            pltpu.VMEM((2, CIN, 32, LANES), BF16),
            pltpu.VMEM((2, CIN, 32, LANES), BF16),
            pltpu.VMEM((4, CIN, 8, LANES), BF16),
            pltpu.VMEM((4, CIN, 8, LANES), BF16),
            pltpu.VMEM((4, NDEV, 4, 3 * LANES), BF16),
            pltpu.VMEM((4, NDEV, 4, 3 * LANES), BF16),
            pltpu.SemaphoreType.DMA,
            pltpu.SemaphoreType.DMA,
            pltpu.SemaphoreType.DMA((8,)),
            pltpu.SemaphoreType.DMA((8,)),
            pltpu.SemaphoreType.DMA,
            pltpu.SemaphoreType.DMA((4,)),
        ],
        compiler_params=pltpu.CompilerParams(
            collective_id=0, has_side_effects=True, vmem_limit_bytes=36 * 1024 * 1024
        ),
        name="closure",
    )(
        solver_counts.reshape(1, NDEV),
        cnn_owner.reshape(64, LANES),
        jnp.transpose(fields, (1, 0, 2)),
        jnp.transpose(in_weight),
        in_bias.reshape(1, HID),
        depth_weight,
        depth_bias.reshape(1, HID),
        mix_weight,
        mix_bias.reshape(1, HID),
        out_weight,
        out_bias.reshape(1, COUT),
    )
    return jnp.transpose(closure, (1, 0, 2))


def solution(mesh):
    return jax.shard_map(
        shards,
        mesh=mesh,
        in_specs=(P(("gx", "yz"), None, None), P(), P(), P(), P(), P(), P(), P(), P(), P(), P()),
        out_specs=P(("gx", "yz"), None, None),
        check_vma=False,
    )
```

```python
import jax
import jax.numpy as jnp
from jax import lax
from jax.experimental import pallas as pl
from jax.experimental.pallas import tpu as pltpu
from jax.sharding import PartitionSpec as P

MESH = pl.DeviceIdType.MESH
NDEV = 128
N_GX = 4
N_YZ = 32
CAP = 192
CIN = 5
HID = 32
COUT = 6
LANES = 128
SLOTS = 2 * NDEV
ROWS = 4 * SLOTS
F32 = jnp.float32
BF16 = jnp.bfloat16
I32 = jnp.int32
GELU_A = 2.0 * 0.7978845608028654
GELU_B = 8.0 * 0.7978845608028654 * 0.044715


STEPS = sorted(
    [(x, y, z, c) for x in range(4) for y in range(4) for z in range(4) for c in range(2)],
    key=lambda step: -sum(min(part, 4 - part) for part in step[:3]),
)[:-2] + [(0, 0, 0, 1)]


def iota(shape, dim):
    return lax.broadcasted_iota(I32, shape, dim)


def dot(a, b):
    return jnp.dot(a, b, preferred_element_type=F32)


def one_hot(condition):
    return jnp.where(condition, 1.0, 0.0).astype(BF16)


def row_to_col(row):
    count = row.shape[1]
    same = iota((count, count), 0) == iota((count, count), 1)
    return jnp.sum(jnp.where(same, row, 0.0), axis=1, keepdims=True)


def col_to_row(col):
    count = col.shape[0]
    same = iota((count, count), 0) == iota((count, count), 1)
    return jnp.sum(jnp.where(same, col, 0.0), axis=0, keepdims=True)


def gelu_half(y):
    return y + y * jnp.tanh(y * (GELU_A + GELU_B * (y * y)))


def run_cumulative(me, counts, owner):
    lower = iota((NDEV, NDEV), 1) <= iota((NDEV, NDEV), 0)
    run_end = jnp.sum(jnp.where(lower, counts, 0.0), axis=1, keepdims=True).astype(I32)
    mine = one_hot(owner == me)
    rows = iota((NDEV, 64), 1)
    whole = dot(one_hot(rows < (run_end >> 7)), mine)
    part = dot(one_hot(rows == (run_end >> 7)), mine)
    inside = iota((NDEV, LANES), 1) < (run_end & 127)
    return jnp.sum(whole + jnp.where(inside, part, 0.0), axis=1, keepdims=True)


def brick_keys(cum_col):
    cum_row = col_to_row(cum_col)
    row = iota((2 * LANES, NDEV), 0)
    patch = (row & 63).astype(F32)
    below = cum_row <= patch
    source = jnp.sum(jnp.where(below, 1.0, 0.0), axis=1, keepdims=True)
    before = jnp.max(jnp.where(below, cum_row, 0.0), axis=1, keepdims=True)
    row = iota((2 * LANES, 1), 0)
    place = 2.0 * source + ((row & 63).astype(F32) - before)
    key_col = 4 * place.astype(I32) + 2 * ((row >> 6) & 1) + (row >> 7)
    patch = (iota((NDEV, LANES), 1) & 63).astype(F32)
    below = cum_col <= patch
    source = jnp.sum(jnp.where(below, 1.0, 0.0), axis=0, keepdims=True)
    before = jnp.max(jnp.where(below, cum_col, 0.0), axis=0, keepdims=True)
    lane = iota((1, LANES), 1)
    place = 2.0 * source + ((lane & 63).astype(F32) - before)
    key_row = 2 * place.astype(I32) + (lane >> 6)
    return key_col, key_row


def slot_keys(me, counts, owner):
    lane = iota((1, NDEV), 1)
    start = jnp.sum(jnp.where(lane < me, counts, 0.0), axis=1, keepdims=True).astype(I32)
    count = jnp.sum(jnp.where(lane == me, counts, 0.0), axis=1, keepdims=True).astype(I32)
    position = iota((CAP, 1), 0) + start
    rows = dot(one_hot(iota((CAP, 64), 1) == (position >> 7)), owner.astype(F32).astype(BF16))
    here = iota((CAP, LANES), 1) == (position & 127)
    owner_col = jnp.sum(jnp.where(here, rows, 0.0), axis=1, keepdims=True)
    owner_row = col_to_row(owner_col)
    same = owner_col == owner_row
    first = iota((CAP, CAP), 0)
    second = iota((CAP, CAP), 1)
    rank_col = jnp.sum(jnp.where(same & (second < first), 1.0, 0.0), axis=1, keepdims=True)
    rank_row = jnp.sum(jnp.where(same & (first < second), 1.0, 0.0), axis=0, keepdims=True)
    key_col = (2.0 * owner_col + rank_col).astype(I32)
    key_row = (2.0 * owner_row + rank_row).astype(I32)
    key_col = jnp.where(iota((CAP, 1), 0) < count, key_col, -1)
    key_row = jnp.where(iota((1, CAP), 1) < count, key_row, -1)
    return key_col, key_row


def split3(value):
    high = value.astype(BF16).astype(F32)
    middle = (value - high).astype(BF16).astype(F32)
    low = value - high - middle
    return high, middle, low


def repeat_rows(value, count):
    rows, lanes = value.shape
    return jnp.broadcast_to(value[:, None, :], (rows, count, lanes)).reshape(rows * count, lanes)


def first_weights(in_weight, in_bias, z_halo):
    lane = iota((HID, 96), 1)
    base = jnp.zeros((HID, 96), F32)
    for c in range(CIN):
        base = jnp.where((lane >> 4) == c, 0.5 * row_to_col(in_weight[c : c + 1, :]), base)
    for number, part in enumerate(split3(0.5 * row_to_col(in_bias))):
        for mask in range(3):
            base = jnp.where(lane == 80 + 3 * mask + number, part, base)
    base = repeat_rows(base, 16)
    lane = iota((16 * HID, 96), 1)
    cell = iota((16 * HID, 96), 0) & 15
    first = jnp.where(cell < 2, 83, jnp.where((cell >> 1) == 5, 86, 80)) if z_halo else 80
    own = jnp.where(lane < 80, cell, -1) == (lane & 15)
    keep = own | ((lane >= first) & (lane < first + 3))
    return jnp.where(keep, base, 0.0).astype(BF16)


def over_cells(weight):
    rows, depth = weight.shape
    widen = one_hot(iota((depth, 8 * depth), 0) == (iota((depth, 8 * depth), 1) >> 3))
    wide = repeat_rows(dot(weight, widen), 8)
    keep = (iota(wide.shape, 0) & 7) == (iota(wide.shape, 1) & 7)
    return jnp.where(keep, wide, 0.0).astype(BF16)


def tap_places(x, pair):
    lane = iota((1, 2048), 1)
    z = lane >> 8
    side = (lane >> 7) & 1
    row = lane & 127
    edge = row - 96
    far = edge & 15
    regular = row < 96
    in_x = jnp.where(regular, row >> 4, far >> 1)
    in_y = jnp.where(regular, (row >> 3) & 1, far & 1)
    in_z = jnp.where(regular, row & 7, jnp.where(edge >= 16, 8, -1))
    a = in_x - x
    b = 2 * side + in_y - pair
    c = in_z - z + 1
    valid = (a >= 0) & (a <= 2) & (b >= 0) & (b <= 2) & (c >= 0) & (c <= 2)
    valid = valid & (regular | (far < 12))
    tap = jnp.where(valid, 9 * a + 3 * b + c, -1)
    return one_hot(iota((32, 2048), 0) == tap)


def closure_body(
    counts_in, owner_in, fields_in, in_weight_in, in_bias_in, depth_weight_in, depth_bias_in,
    mix_weight_in, mix_bias_in, out_weight_in, out_bias_in,
    out_ref,
    counts_ref, owner_ref, fields_ref, in_weight_ref, in_bias_ref, depth_weight_ref, depth_bias_ref,
    mix_weight_ref, mix_bias_ref, out_weight_ref, out_bias_ref, mix_w, out_w, out_bias,
    spread, outgoing, incoming, grid_in, ones_mask, hidden, band, depth_bias, mix_bias, depth, result, scatter,
    place_slots, x_send, x_recv, y_send, y_recv, c_send, c_recv, leaving, arrived,
    fetch_sem, send_sem, recv_sem, halo_send, halo_recv, back_send, back_recv,
):
    fetches = [
        pltpu.make_async_copy(source, target, fetch_sem.at[number])
        for number, (source, target) in enumerate((
            (counts_in, counts_ref), (owner_in, owner_ref), (fields_in, fields_ref),
            (in_weight_in, in_weight_ref), (in_bias_in, in_bias_ref),
            (depth_weight_in, depth_weight_ref), (depth_bias_in, depth_bias_ref),
            (mix_weight_in, mix_weight_ref), (mix_bias_in, mix_bias_ref),
            (out_weight_in, out_weight_ref), (out_bias_in, out_bias_ref),
        ))
    ]
    for fetch in fetches:
        fetch.start()
    gx = lax.axis_index("gx")
    yz = lax.axis_index("yz")
    me = gx * N_YZ + yz
    at_x = [lax.rem(gx + step, 4) for step in range(4)]
    at_y = [8 * lax.rem(lax.div(yz, 8) + step, 4) for step in range(4)]
    at_z = [2 * lax.rem(lax.div(yz, 2) + step, 4) for step in range(4)]
    at_core = [lax.rem(yz + step, 2) for step in range(2)]

    def coords(step):
        where = (at_x[step[0]], at_y[step[1]] + at_z[step[2]] + at_core[step[3]])
        return where[0] * N_YZ + where[1], where

    barrier = pltpu.get_barrier_semaphore()
    for step in STEPS:
        pl.semaphore_signal(barrier, inc=1, device_id=coords(step)[1], device_id_type=MESH)

    for fetch in fetches[:3]:
        fetch.wait()
    counts = counts_ref[...].astype(F32)
    owner = owner_ref[...]
    key_col, key_row = slot_keys(me, counts, owner)
    select = one_hot(iota((SLOTS, CAP), 0) == key_row)
    for c in range(CIN):
        rows = dot(select, fields_ref[c])
        for part in range(4):
            spread[c, pl.ds(part, SLOTS, stride=4), :] = rows[:, part * LANES : (part + 1) * LANES]
    for c in range(CIN):
        outgoing[:, :, c * LANES : (c + 1) * LANES] = (
            spread[c].reshape(NDEV, 8, LANES).astype(BF16)
        )

    pl.semaphore_wait(barrier, NDEV - 1)

    for step in STEPS:
        other, where = coords(step)
        pltpu.make_async_remote_copy(
            src_ref=outgoing.at[other], dst_ref=incoming.at[me],
            send_sem=send_sem, recv_sem=recv_sem, device_id=where, device_id_type=MESH,
        ).start()
    incoming[me] = outgoing[me]

    cum_col = run_cumulative(me, counts, owner)
    brick_col, brick_row = brick_keys(cum_col)
    gather = one_hot(iota((2 * LANES, ROWS), 1) == brick_col)
    scatter[...] = one_hot(iota((2 * SLOTS, LANES), 0) == brick_row)
    for half in range(2):
        wanted = jnp.where(key_col < 0, -1, 2 * key_col + half)
        place_slots[half * CAP : (half + 1) * CAP, :] = one_hot(
            iota((CAP, 2 * SLOTS), 1) == wanted
        )
    lane = iota((1, LANES), 1)
    high_x = ((lane >> 6) & 1) == 1
    along_y = (lane >> 4) & 3
    along_z = lane & 15
    keep_low = jnp.where(gx > 0, 1.0, 0.0).astype(F32)
    keep_high = jnp.where(gx < N_GX - 1, 1.0, 0.0).astype(F32)
    masks = [jnp.ones((1, LANES), F32)] * 6
    masks[0] = jnp.where(high_x, 1.0, keep_low)
    masks[5] = jnp.where(high_x, keep_high, 1.0)
    for x in range(6):
        ones_mask[x] = jnp.broadcast_to(masks[x], (16, LANES))
    line = iota((16, LANES), 0)
    ones_mask[6] = jnp.where(line < 3, 1.0, jnp.where(line < 6, masks[0], masks[5]))
    for fetch in fetches[3:]:
        fetch.wait()
    in_weight = in_weight_ref[...].astype(F32)
    first_w = [first_weights(in_weight, in_bias_ref[...], z_halo) for z_halo in (False, True)]
    mix_w[...] = over_cells((0.5 * mix_weight_ref[...].astype(F32)).astype(BF16))
    out_w[...] = over_cells(out_weight_ref[...])
    depth_bias[...] = repeat_rows(
        jnp.broadcast_to(row_to_col(depth_bias_ref[...]), (HID, LANES)), 8
    )
    mix_bias[...] = repeat_rows(
        jnp.broadcast_to(0.5 * row_to_col(mix_bias_ref[...]), (HID, LANES)), 8
    )
    out_bias[...] = repeat_rows(jnp.broadcast_to(row_to_col(out_bias_ref[...]), (COUT, LANES)), 8)
    taps = jnp.concatenate([depth_weight_ref[...], jnp.zeros((HID, 5), F32)], axis=1)
    high = taps.astype(BF16)
    taps = jnp.concatenate([high, (taps - high.astype(F32)).astype(BF16)], axis=0)

    def band_rows(group, carry):
        rows = dot(taps, tap_places(lax.div(group, 2), lax.rem(group, 2)))
        for z in range(8):
            start = pl.multiple_of((group * 8 + z) * 2 * HID, 2 * HID)
            for side in range(2):
                first = z * 256 + side * LANES
                band[side, pl.ds(start, 2 * HID), :] = rows[:, first : first + LANES]
        return carry

    lax.fori_loop(0, 8, band_rows, 0)
    grid_in[...] = jnp.zeros_like(grid_in)
    for pair in range(5):
        for tile in (0, 5):
            first = pair * 128 + tile * 16
            hidden[:, first : first + 16, :] = jnp.zeros((HID, 16, LANES), BF16)

    every = pltpu.make_async_copy(
        outgoing.at[pl.ds(0, NDEV - 1)], incoming.at[pl.ds(0, NDEV - 1)], recv_sem
    )
    every.wait()

    def place(x, y):
        return (y // 2) * 128 + x * 16 + (y % 2) * 8

    def get(c, x, y):
        return grid_in[c, place(x, y) : place(x, y) + 8, :]

    def put(c, x, y, value):
        grid_in[c, place(x, y) : place(x, y) + 8, :] = value

    bricks = dot(gather, incoming[...].reshape(ROWS, CIN * LANES))
    for c in range(CIN):
        for m in range(2):
            turned = bricks[m * LANES : (m + 1) * LANES, c * LANES : (c + 1) * LANES].T
            for p in range(2):
                for y in range(8):
                    first = p * 64 + y * 8
                    put(c, 1 + 2 * m + p, 1 + y, turned[first : first + 8])

    for c in range(CIN):
        for side, x in enumerate((4, 1)):
            cells = jnp.concatenate([get(c, x, y) for y in range(1, 9)], axis=0)
            x_send[side, c] = pltpu.roll(cells, 64, 1).astype(BF16)
        last_y = [get(c, x, 8) for x in range(1, 5)]
        first_y = [get(c, x, 1) for x in range(1, 5)]
        y_send[0, c] = pltpu.roll(jnp.concatenate(last_y, axis=0), 80, 1).astype(BF16)
        y_send[1, c] = pltpu.roll(jnp.concatenate(first_y, axis=0), 48, 1).astype(BF16)
        c_send[0, c] = pltpu.roll(last_y[3], 16, 1).astype(BF16)
        c_send[1, c] = pltpu.roll(first_y[3], 112, 1).astype(BF16)
        c_send[2, c] = pltpu.roll(last_y[0], 16, 1).astype(BF16)
        c_send[3, c] = pltpu.roll(first_y[0], 112, 1).astype(BF16)
    up_x = lax.rem(gx + 1, N_GX)
    down_x = lax.rem(gx + N_GX - 1, N_GX)
    up_y = lax.rem(yz + 1, N_YZ)
    down_y = lax.rem(yz + N_YZ - 1, N_YZ)
    halo = []
    for source, target, where in (
        (x_send.at[0], x_recv.at[0], (up_x, yz)),
        (x_send.at[1], x_recv.at[1], (down_x, yz)),
        (y_send.at[0], y_recv.at[0], (gx, up_y)),
        (y_send.at[1], y_recv.at[1], (gx, down_y)),
        (c_send.at[0], c_recv.at[0], (up_x, up_y)),
        (c_send.at[1], c_recv.at[1], (up_x, down_y)),
        (c_send.at[2], c_recv.at[2], (down_x, up_y)),
        (c_send.at[3], c_recv.at[3], (down_x, down_y)),
    ):
        number = len(halo)
        copy = pltpu.make_async_remote_copy(
            src_ref=source, dst_ref=target, send_sem=halo_send.at[number],
            recv_sem=halo_recv.at[number], device_id=where, device_id_type=MESH,
        )
        copy.start()
        halo.append(copy)
    def first_group(pair, tile):
        start = pl.multiple_of(pair * 128 + tile * 16, 16)
        cells = [grid_in[c, pl.ds(start, 16), :] for c in range(CIN)]
        stacked = jnp.concatenate(cells + [ones_mask[min(tile, 6)]], axis=0).astype(BF16)
        value = gelu_half(dot(first_w[tile > 5], stacked)).astype(BF16)
        for h in range(HID):
            hidden[h, pl.ds(start, 16), :] = value[16 * h : 16 * h + 16]

    def first_inner(pair, carry):
        for tile in range(1, 5):
            first_group(pair, tile)
        return carry

    lax.fori_loop(1, 4, first_inner, 0)

    for copy in halo:
        copy.wait()

    for c in range(CIN):
        low = jnp.where(high_x, x_send[0, c].astype(F32), keep_low * x_recv[0, c].astype(F32))
        high = jnp.where(high_x, keep_high * x_recv[1, c].astype(F32), x_send[1, c].astype(F32))
        for y in range(8):
            put(c, 0, 1 + y, low[8 * y : 8 * y + 8])
            put(c, 5, 1 + y, high[8 * y : 8 * y + 8])
        for side in range(2):
            own = y_recv[side, c].astype(F32)
            corner_low = keep_low * c_recv[0 + side, c].astype(F32)
            corner_high = keep_high * c_recv[2 + side, c].astype(F32)
            edge_lane = along_y == (0 if side == 0 else 3)
            for x in range(6):
                if x == 0:
                    far = jnp.where(high_x, pltpu.roll(own[24:32], 64, 1), corner_low)
                elif x == 5:
                    far = jnp.where(high_x, corner_high, pltpu.roll(own[0:8], 64, 1))
                else:
                    far = own[8 * (x - 1) : 8 * x]
                near = pltpu.roll(get(c, x, 8 if side == 0 else 1), 16 if side == 0 else 112, 1)
                put(c, x, 0 if side == 0 else 9, jnp.where(edge_lane, far, near))
        for pair in range(5):
            below = grid_in[c, pl.ds(pair * 128 + 7, 12, stride=8), :]
            above = grid_in[c, pl.ds(pair * 128, 12, stride=8), :]
            grid_in[c, pair * 128 + 96 : pair * 128 + 108, :] = jnp.where(
                along_z == 0, pltpu.roll(below, 113, 1), pltpu.roll(below, 1, 1)
            )
            grid_in[c, pair * 128 + 112 : pair * 128 + 124, :] = jnp.where(
                along_z == 15, pltpu.roll(above, 15, 1), pltpu.roll(above, 127, 1)
            )

    def first_edge_y(side, carry):
        for tile in range(1, 5):
            first_group(4 * side, tile)
        return carry

    def first_z(pair, carry):
        for tile in (6, 7):
            first_group(pair, tile)
        return carry

    def first_edge_x(pair, carry):
        for tile in (0, 5):
            first_group(pair, tile)
        return carry

    def depth_planes(planes):
        def depth_part(group, carry):
            parts = []
            for number in range(2):
                h = 2 * group + number
                weight = jnp.concatenate(
                    [
                        jnp.concatenate(
                            [
                                band[side, pl.ds(x * 16 * 2 * HID + part * HID + h, 16, stride=2 * HID), :]
                                for side in range(2)
                            ],
                            axis=1,
                        )
                        for part in range(2)
                        for x in planes
                    ],
                    axis=0,
                ).astype(BF16)
                cells = [hidden[h, 128 * pair : 128 * pair + 256, :] for pair in range(4)]
                both = dot(weight, jnp.concatenate(cells, axis=1))
                parts.append(both[:32] + both[32:])
            start = pl.multiple_of(16 * group, 16)
            bias = depth_bias[pl.ds(start, 16), :]
            for number, x in enumerate(planes):
                for y in range(8):
                    first = 16 * number + 8 * (y % 2)
                    lanes = slice((y // 2) * LANES, (y // 2 + 1) * LANES)
                    both = jnp.concatenate([part[first : first + 8, lanes] for part in parts], axis=0)
                    depth[x, y, pl.ds(start, 16), :] = (both + bias).astype(BF16)
            return carry

        lax.fori_loop(0, 16, depth_part, 0)

    def plane(x, carry):
        def mix_part(group, inner):
            for number in range(4):
                y = 4 * group + number
                mixed = dot(mix_w[...], depth[x, y]) + mix_bias[...]
                field = dot(out_w[...], gelu_half(mixed).astype(BF16)) + out_bias[...]
                for f in range(COUT):
                    start = pl.multiple_of(f * 64 + 8 * y, 8)
                    result[pl.ds(start, 8), :] = field[8 * f : 8 * f + 8]
            return inner

        lax.fori_loop(0, 2, mix_part, 0)

        odd = lax.rem(x, 2)
        turned = []
        for pair in range(3):
            first = result[pl.ds(pl.multiple_of((2 * pair + odd) * 64, 64), 64), :]
            second = result[pl.ds(pl.multiple_of((2 * pair + 1 - odd) * 64, 64), 64), :]
            turned.append(jnp.concatenate([first, second], axis=0).T.astype(BF16))
        packed = jnp.concatenate(turned, axis=1)
        leaving[x] = dot(scatter[...], packed).reshape(NDEV, 4, 3 * LANES).astype(BF16)
        for step in STEPS:
            other, where = coords(step)
            pltpu.make_async_remote_copy(
                src_ref=leaving.at[x, other], dst_ref=arrived.at[x, me],
                send_sem=back_send, recv_sem=back_recv.at[x], device_id=where, device_id_type=MESH,
            ).start()
        arrived[x, me] = leaving[x, me]
        return carry

    lax.fori_loop(0, 2, first_edge_y, 0)
    lax.fori_loop(0, 5, first_z, 0)
    depth_planes((1, 2))
    lax.fori_loop(1, 3, plane, 0)
    lax.fori_loop(0, 5, first_edge_x, 0)
    depth_planes((0, 3))
    lax.fori_loop(0, 2, lambda number, carry: plane(3 * number, carry), 0)

    low_half = iota((1, LANES), 1) < 64
    taken = {}
    for x in (1, 2, 0, 3):
        pltpu.make_async_copy(
            leaving.at[x, pl.ds(0, NDEV - 1)], arrived.at[x, pl.ds(0, NDEV - 1)], back_recv.at[x]
        ).wait()
        taken[x] = dot(place_slots[...], arrived[x].reshape(2 * SLOTS, 3 * LANES))
        if x in (1, 2):
            continue
        for half in range(2):
            rows = slice(half * CAP, (half + 1) * CAP)
            lanes = slice((2 * half + x // 2) * LANES, (2 * half + x // 2 + 1) * LANES)
            for pair in range(3):
                even = taken[x - x % 2][rows, pair * LANES : (pair + 1) * LANES]
                odd = taken[x - x % 2 + 1][rows, pair * LANES : (pair + 1) * LANES]
                out_ref[2 * pair, :, lanes] = jnp.where(low_half, even, odd).astype(BF16)
                out_ref[2 * pair + 1, :, lanes] = pltpu.roll(
                    jnp.where(low_half, odd, even), 64, 1
                ).astype(BF16)
    pltpu.make_async_copy(
        outgoing.at[pl.ds(0, NDEV - 1)], incoming.at[pl.ds(0, NDEV - 1)], send_sem
    ).wait()
    pltpu.make_async_copy(
        leaving.at[:, pl.ds(0, NDEV - 1)], arrived.at[:, pl.ds(0, NDEV - 1)], back_send
    ).wait()


VMEM = pl.BlockSpec(memory_space=pltpu.VMEM)
HBM = pl.BlockSpec(memory_space=pltpu.HBM)


def shards(
    fields, solver_counts, cnn_owner, in_weight, in_bias, depth_weight, depth_bias,
    mix_weight, mix_bias, out_weight, out_bias,
):
    closure = pl.pallas_call(
        closure_body,
        out_shape=jax.ShapeDtypeStruct((COUT, CAP, 4 * LANES), BF16),
        in_specs=[HBM] * 11,
        out_specs=VMEM,
        scratch_shapes=[
            pltpu.VMEM((1, NDEV), I32),
            pltpu.VMEM((64, LANES), I32),
            pltpu.VMEM((CIN, CAP, 4 * LANES), BF16),
            pltpu.VMEM((CIN, HID), BF16),
            pltpu.VMEM((1, HID), F32),
            pltpu.VMEM((HID, 27), F32),
            pltpu.VMEM((1, HID), F32),
            pltpu.VMEM((HID, HID), BF16),
            pltpu.VMEM((1, HID), F32),
            pltpu.VMEM((COUT, HID), BF16),
            pltpu.VMEM((1, COUT), F32),
            pltpu.VMEM((8 * HID, 8 * HID), BF16),
            pltpu.VMEM((8 * COUT, 8 * HID), BF16),
            pltpu.VMEM((8 * COUT, LANES), F32),
            pltpu.VMEM((CIN, ROWS, LANES), F32),
            pltpu.VMEM((NDEV, 8, CIN * LANES), BF16),
            pltpu.VMEM((NDEV, 8, CIN * LANES), BF16),
            pltpu.VMEM((CIN, 640, LANES), F32),
            pltpu.VMEM((7, 16, LANES), F32),
            pltpu.VMEM((HID, 640, LANES), BF16),
            pltpu.VMEM((2, 128 * HID, LANES), F32),
            pltpu.VMEM((8 * HID, LANES), F32),
            pltpu.VMEM((8 * HID, LANES), F32),
            pltpu.VMEM((4, 8, 8 * HID, LANES), BF16),
            pltpu.VMEM((64 * COUT, LANES), F32),
            pltpu.VMEM((2 * SLOTS, LANES), BF16),
            pltpu.VMEM((2 * CAP, 2 * SLOTS), BF16),
            pltpu.VMEM((2, CIN, 64, LANES), BF16),
            pltpu.VMEM((2, CIN, 64, LANES), BF16),
            pltpu.VMEM((2, CIN, 32, LANES), BF16),
            pltpu.VMEM((2, CIN, 32, LANES), BF16),
            pltpu.VMEM((4, CIN, 8, LANES), BF16),
            pltpu.VMEM((4, CIN, 8, LANES), BF16),
            pltpu.VMEM((4, NDEV, 4, 3 * LANES), BF16),
            pltpu.VMEM((4, NDEV, 4, 3 * LANES), BF16),
            pltpu.SemaphoreType.DMA((11,)),
            pltpu.SemaphoreType.DMA,
            pltpu.SemaphoreType.DMA,
            pltpu.SemaphoreType.DMA((8,)),
            pltpu.SemaphoreType.DMA((8,)),
            pltpu.SemaphoreType.DMA,
            pltpu.SemaphoreType.DMA((4,)),
        ],
        compiler_params=pltpu.CompilerParams(
            collective_id=0, has_side_effects=True, vmem_limit_bytes=36 * 1024 * 1024
        ),
        name="closure",
    )(*(
        pltpu.with_memory_space_constraint(operand, pltpu.HBM)
        for operand in (
            solver_counts.reshape(1, NDEV),
            cnn_owner.reshape(64, LANES),
            jnp.transpose(fields, (1, 0, 2)),
            jnp.transpose(in_weight),
            in_bias.reshape(1, HID),
            depth_weight,
            depth_bias.reshape(1, HID),
            mix_weight,
            mix_bias.reshape(1, HID),
            out_weight,
            out_bias.reshape(1, COUT),
        )
    ))
    return jnp.transpose(closure, (1, 0, 2))


def solution(mesh):
    return jax.shard_map(
        shards,
        mesh=mesh,
        in_specs=(P(("gx", "yz"), None, None), P(), P(), P(), P(), P(), P(), P(), P(), P(), P()),
        out_specs=P(("gx", "yz"), None, None),
        check_vma=False,
    )
```

```python
import jax
import jax.numpy as jnp
from jax import lax
from jax.experimental import pallas as pl
from jax.experimental.pallas import tpu as pltpu
from jax.sharding import PartitionSpec as P

MESH = pl.DeviceIdType.MESH
NDEV = 128
N_GX = 4
N_YZ = 32
CAP = 192
CIN = 5
HID = 32
COUT = 6
LANES = 128
SLOTS = 2 * NDEV
ROWS = 4 * SLOTS
F32 = jnp.float32
BF16 = jnp.bfloat16
I32 = jnp.int32
GELU_A = 2.0 * 0.7978845608028654
GELU_B = 8.0 * 0.7978845608028654 * 0.044715


STEPS = sorted(
    [(x, y, z, c) for x in range(4) for y in range(4) for z in range(4) for c in range(2)],
    key=lambda step: -sum(min(part, 4 - part) for part in step[:3]),
)[:-2] + [(0, 0, 0, 1)]


def iota(shape, dim):
    return lax.broadcasted_iota(I32, shape, dim)


def dot(a, b):
    return jnp.dot(a, b, preferred_element_type=F32)


def one_hot(condition):
    return jnp.where(condition, 1.0, 0.0).astype(BF16)


def row_to_col(row):
    count = row.shape[1]
    same = iota((count, count), 0) == iota((count, count), 1)
    return jnp.sum(jnp.where(same, row, 0.0), axis=1, keepdims=True)


def col_to_row(col):
    count = col.shape[0]
    same = iota((count, count), 0) == iota((count, count), 1)
    return jnp.sum(jnp.where(same, col, 0.0), axis=0, keepdims=True)


def gelu_half(y):
    return y + y * jnp.tanh(y * (GELU_A + GELU_B * (y * y)))


def run_cumulative(me, counts, owner):
    lower = iota((NDEV, NDEV), 1) <= iota((NDEV, NDEV), 0)
    run_end = jnp.sum(jnp.where(lower, counts, 0.0), axis=1, keepdims=True).astype(I32)
    mine = one_hot(owner == me)
    rows = iota((NDEV, 64), 1)
    whole = dot(one_hot(rows < (run_end >> 7)), mine)
    part = dot(one_hot(rows == (run_end >> 7)), mine)
    inside = iota((NDEV, LANES), 1) < (run_end & 127)
    return jnp.sum(whole + jnp.where(inside, part, 0.0), axis=1, keepdims=True)


def brick_keys(cum_col):
    cum_row = col_to_row(cum_col)
    row = iota((2 * LANES, NDEV), 0)
    patch = (row & 63).astype(F32)
    below = cum_row <= patch
    source = jnp.sum(jnp.where(below, 1.0, 0.0), axis=1, keepdims=True)
    before = jnp.max(jnp.where(below, cum_row, 0.0), axis=1, keepdims=True)
    row = iota((2 * LANES, 1), 0)
    place = 2.0 * source + ((row & 63).astype(F32) - before)
    key_col = 4 * place.astype(I32) + 2 * ((row >> 6) & 1) + (row >> 7)
    patch = (iota((NDEV, LANES), 1) & 63).astype(F32)
    below = cum_col <= patch
    source = jnp.sum(jnp.where(below, 1.0, 0.0), axis=0, keepdims=True)
    before = jnp.max(jnp.where(below, cum_col, 0.0), axis=0, keepdims=True)
    lane = iota((1, LANES), 1)
    place = 2.0 * source + ((lane & 63).astype(F32) - before)
    key_row = 2 * place.astype(I32) + (lane >> 6)
    return key_col, key_row


def slot_keys(me, counts, owner):
    lane = iota((1, NDEV), 1)
    start = jnp.sum(jnp.where(lane < me, counts, 0.0), axis=1, keepdims=True).astype(I32)
    count = jnp.sum(jnp.where(lane == me, counts, 0.0), axis=1, keepdims=True).astype(I32)
    position = iota((CAP, 1), 0) + start
    rows = dot(one_hot(iota((CAP, 64), 1) == (position >> 7)), owner.astype(F32).astype(BF16))
    here = iota((CAP, LANES), 1) == (position & 127)
    owner_col = jnp.sum(jnp.where(here, rows, 0.0), axis=1, keepdims=True)
    owner_row = col_to_row(owner_col)
    same = owner_col == owner_row
    first = iota((CAP, CAP), 0)
    second = iota((CAP, CAP), 1)
    rank_col = jnp.sum(jnp.where(same & (second < first), 1.0, 0.0), axis=1, keepdims=True)
    rank_row = jnp.sum(jnp.where(same & (first < second), 1.0, 0.0), axis=0, keepdims=True)
    key_col = (2.0 * owner_col + rank_col).astype(I32)
    key_row = (2.0 * owner_row + rank_row).astype(I32)
    key_col = jnp.where(iota((CAP, 1), 0) < count, key_col, -1)
    key_row = jnp.where(iota((1, CAP), 1) < count, key_row, -1)
    return key_col, key_row


def split3(value):
    high = value.astype(BF16).astype(F32)
    middle = (value - high).astype(BF16).astype(F32)
    low = value - high - middle
    return high, middle, low


def repeat_rows(value, count):
    rows, lanes = value.shape
    return jnp.broadcast_to(value[:, None, :], (rows, count, lanes)).reshape(rows * count, lanes)


def first_weights(in_weight, in_bias, z_halo):
    lane = iota((HID, 96), 1)
    base = jnp.zeros((HID, 96), F32)
    for c in range(CIN):
        base = jnp.where((lane >> 4) == c, 0.5 * row_to_col(in_weight[c : c + 1, :]), base)
    for number, part in enumerate(split3(0.5 * row_to_col(in_bias))):
        for mask in range(3):
            base = jnp.where(lane == 80 + 3 * mask + number, part, base)
    base = repeat_rows(base, 16)
    lane = iota((16 * HID, 96), 1)
    cell = iota((16 * HID, 96), 0) & 15
    first = jnp.where(cell < 2, 83, jnp.where((cell >> 1) == 5, 86, 80)) if z_halo else 80
    own = jnp.where(lane < 80, cell, -1) == (lane & 15)
    keep = own | ((lane >= first) & (lane < first + 3))
    return jnp.where(keep, base, 0.0).astype(BF16)


def over_cells(weight):
    rows, depth = weight.shape
    widen = one_hot(iota((depth, 8 * depth), 0) == (iota((depth, 8 * depth), 1) >> 3))
    wide = repeat_rows(dot(weight, widen), 8)
    keep = (iota(wide.shape, 0) & 7) == (iota(wide.shape, 1) & 7)
    return jnp.where(keep, wide, 0.0).astype(BF16)


def tap_places(x, pair):
    lane = iota((1, 2048), 1)
    z = lane >> 8
    side = (lane >> 7) & 1
    row = lane & 127
    edge = row - 96
    far = edge & 15
    regular = row < 96
    in_x = jnp.where(regular, row >> 4, far >> 1)
    in_y = jnp.where(regular, (row >> 3) & 1, far & 1)
    in_z = jnp.where(regular, row & 7, jnp.where(edge >= 16, 8, -1))
    a = in_x - x
    b = 2 * side + in_y - pair
    c = in_z - z + 1
    valid = (a >= 0) & (a <= 2) & (b >= 0) & (b <= 2) & (c >= 0) & (c <= 2)
    valid = valid & (regular | (far < 12))
    tap = jnp.where(valid, 9 * a + 3 * b + c, -1)
    return one_hot(iota((32, 2048), 0) == tap)


def closure_body(
    counts_in, owner_in, fields_in, in_weight_in, in_bias_in, depth_weight_in, depth_bias_in,
    mix_weight_in, mix_bias_in, out_weight_in, out_bias_in,
    out_ref,
    counts_ref, owner_ref, fields_ref, in_weight_ref, in_bias_ref, depth_weight_ref, depth_bias_ref,
    mix_weight_ref, mix_bias_ref, out_weight_ref, out_bias_ref, mix_w, out_w, out_bias,
    spread, outgoing, incoming, grid_in, ones_mask, hidden, band, tap_w, depth_bias, mix_bias, depth, result, scatter,
    place_slots, x_send, x_recv, y_send, y_recv, c_send, c_recv, leaving, arrived,
    fetch_sem, send_sem, recv_sem, halo_send, halo_recv, back_send, back_recv,
):
    fetches = [
        pltpu.make_async_copy(source, target, fetch_sem.at[number])
        for number, (source, target) in enumerate((
            (counts_in, counts_ref), (owner_in, owner_ref), (fields_in, fields_ref),
            (in_weight_in, in_weight_ref), (in_bias_in, in_bias_ref),
            (depth_weight_in, depth_weight_ref), (depth_bias_in, depth_bias_ref),
            (mix_weight_in, mix_weight_ref), (mix_bias_in, mix_bias_ref),
            (out_weight_in, out_weight_ref), (out_bias_in, out_bias_ref),
        ))
    ]
    for fetch in fetches:
        fetch.start()
    gx = lax.axis_index("gx")
    yz = lax.axis_index("yz")
    me = gx * N_YZ + yz
    at_x = [lax.rem(gx + step, 4) for step in range(4)]
    at_y = [8 * lax.rem(lax.div(yz, 8) + step, 4) for step in range(4)]
    at_z = [2 * lax.rem(lax.div(yz, 2) + step, 4) for step in range(4)]
    at_core = [lax.rem(yz + step, 2) for step in range(2)]

    def coords(step):
        where = (at_x[step[0]], at_y[step[1]] + at_z[step[2]] + at_core[step[3]])
        return where[0] * N_YZ + where[1], where

    barrier = pltpu.get_barrier_semaphore()
    for step in STEPS:
        pl.semaphore_signal(barrier, inc=1, device_id=coords(step)[1], device_id_type=MESH)

    for fetch in fetches[:3]:
        fetch.wait()
    counts = counts_ref[...].astype(F32)
    owner = owner_ref[...]
    key_col, key_row = slot_keys(me, counts, owner)
    select = one_hot(iota((SLOTS, CAP), 0) == key_row)
    for c in range(CIN):
        rows = dot(select, fields_ref[c])
        for part in range(4):
            spread[c, pl.ds(part, SLOTS, stride=4), :] = rows[:, part * LANES : (part + 1) * LANES]
    for c in range(CIN):
        outgoing[:, :, c * LANES : (c + 1) * LANES] = (
            spread[c].reshape(NDEV, 8, LANES).astype(BF16)
        )

    pl.semaphore_wait(barrier, NDEV - 1)

    for step in STEPS:
        other, where = coords(step)
        pltpu.make_async_remote_copy(
            src_ref=outgoing.at[other], dst_ref=incoming.at[me],
            send_sem=send_sem, recv_sem=recv_sem, device_id=where, device_id_type=MESH,
        ).start()
    incoming[me] = outgoing[me]

    cum_col = run_cumulative(me, counts, owner)
    brick_col, brick_row = brick_keys(cum_col)
    gather = one_hot(iota((2 * LANES, ROWS), 1) == brick_col)
    scatter[...] = one_hot(iota((2 * SLOTS, LANES), 0) == brick_row)
    for half in range(2):
        wanted = jnp.where(key_col < 0, -1, 2 * key_col + half)
        place_slots[half * CAP : (half + 1) * CAP, :] = one_hot(
            iota((CAP, 2 * SLOTS), 1) == wanted
        )
    lane = iota((1, LANES), 1)
    high_x = ((lane >> 6) & 1) == 1
    along_y = (lane >> 4) & 3
    along_z = lane & 15
    keep_low = jnp.where(gx > 0, 1.0, 0.0).astype(F32)
    keep_high = jnp.where(gx < N_GX - 1, 1.0, 0.0).astype(F32)
    masks = [jnp.ones((1, LANES), F32)] * 6
    masks[0] = jnp.where(high_x, 1.0, keep_low)
    masks[5] = jnp.where(high_x, keep_high, 1.0)
    for x in range(6):
        ones_mask[x] = jnp.broadcast_to(masks[x], (16, LANES))
    line = iota((16, LANES), 0)
    ones_mask[6] = jnp.where(line < 3, 1.0, jnp.where(line < 6, masks[0], masks[5]))
    for fetch in fetches[3:]:
        fetch.wait()
    in_weight = in_weight_ref[...].astype(F32)
    first_w = [first_weights(in_weight, in_bias_ref[...], z_halo) for z_halo in (False, True)]
    mix_w[...] = over_cells((0.5 * mix_weight_ref[...].astype(F32)).astype(BF16))
    out_w[...] = over_cells(out_weight_ref[...])
    depth_bias[...] = repeat_rows(
        jnp.broadcast_to(row_to_col(depth_bias_ref[...]), (HID, LANES)), 8
    )
    mix_bias[...] = repeat_rows(
        jnp.broadcast_to(0.5 * row_to_col(mix_bias_ref[...]), (HID, LANES)), 8
    )
    out_bias[...] = repeat_rows(jnp.broadcast_to(row_to_col(out_bias_ref[...]), (COUT, LANES)), 8)
    taps = jnp.concatenate([depth_weight_ref[...], jnp.zeros((HID, 5), F32)], axis=1)
    high = taps.astype(BF16)
    taps = jnp.concatenate([high, (taps - high.astype(F32)).astype(BF16)], axis=0)

    def band_rows(group, carry):
        rows = dot(taps, tap_places(lax.div(group, 2), lax.rem(group, 2)))
        for z in range(8):
            start = pl.multiple_of((group * 8 + z) * 2 * HID, 2 * HID)
            for side in range(2):
                first = z * 256 + side * LANES
                band[side, pl.ds(start, 2 * HID), :] = rows[:, first : first + LANES]
        return carry

    lax.fori_loop(0, 8, band_rows, 0)

    def band_channel(h, carry):
        row = 0
        for planes in ((1, 2), (0, 3)):
            for part in range(2):
                for x in planes:
                    for side in range(2):
                        rows = band[side, pl.ds(x * 32 * HID + part * HID + h, 16, stride=2 * HID), :]
                        tap_w[h, row : row + 16, side * LANES : (side + 1) * LANES] = rows.astype(BF16)
                    row += 16
        return carry

    lax.fori_loop(0, HID, band_channel, 0)
    grid_in[...] = jnp.zeros_like(grid_in)
    for pair in range(5):
        for tile in (0, 5):
            first = pair * 128 + tile * 16
            hidden[:, first : first + 16, :] = jnp.zeros((HID, 16, LANES), BF16)

    every = pltpu.make_async_copy(
        outgoing.at[pl.ds(0, NDEV - 1)], incoming.at[pl.ds(0, NDEV - 1)], recv_sem
    )
    every.wait()

    def place(x, y):
        return (y // 2) * 128 + x * 16 + (y % 2) * 8

    def get(c, x, y):
        return grid_in[c, place(x, y) : place(x, y) + 8, :]

    def put(c, x, y, value):
        grid_in[c, place(x, y) : place(x, y) + 8, :] = value

    bricks = dot(gather, incoming[...].reshape(ROWS, CIN * LANES))
    for c in range(CIN):
        for m in range(2):
            turned = bricks[m * LANES : (m + 1) * LANES, c * LANES : (c + 1) * LANES].T
            for p in range(2):
                for y in range(8):
                    first = p * 64 + y * 8
                    put(c, 1 + 2 * m + p, 1 + y, turned[first : first + 8])

    for c in range(CIN):
        for side, x in enumerate((4, 1)):
            cells = jnp.concatenate([get(c, x, y) for y in range(1, 9)], axis=0)
            x_send[side, c] = pltpu.roll(cells, 64, 1).astype(BF16)
        last_y = [get(c, x, 8) for x in range(1, 5)]
        first_y = [get(c, x, 1) for x in range(1, 5)]
        y_send[0, c] = pltpu.roll(jnp.concatenate(last_y, axis=0), 80, 1).astype(BF16)
        y_send[1, c] = pltpu.roll(jnp.concatenate(first_y, axis=0), 48, 1).astype(BF16)
        c_send[0, c] = pltpu.roll(last_y[3], 16, 1).astype(BF16)
        c_send[1, c] = pltpu.roll(first_y[3], 112, 1).astype(BF16)
        c_send[2, c] = pltpu.roll(last_y[0], 16, 1).astype(BF16)
        c_send[3, c] = pltpu.roll(first_y[0], 112, 1).astype(BF16)
    up_x = lax.rem(gx + 1, N_GX)
    down_x = lax.rem(gx + N_GX - 1, N_GX)
    up_y = lax.rem(yz + 1, N_YZ)
    down_y = lax.rem(yz + N_YZ - 1, N_YZ)
    halo = []
    for source, target, where in (
        (x_send.at[0], x_recv.at[0], (up_x, yz)),
        (x_send.at[1], x_recv.at[1], (down_x, yz)),
        (y_send.at[0], y_recv.at[0], (gx, up_y)),
        (y_send.at[1], y_recv.at[1], (gx, down_y)),
        (c_send.at[0], c_recv.at[0], (up_x, up_y)),
        (c_send.at[1], c_recv.at[1], (up_x, down_y)),
        (c_send.at[2], c_recv.at[2], (down_x, up_y)),
        (c_send.at[3], c_recv.at[3], (down_x, down_y)),
    ):
        number = len(halo)
        copy = pltpu.make_async_remote_copy(
            src_ref=source, dst_ref=target, send_sem=halo_send.at[number],
            recv_sem=halo_recv.at[number], device_id=where, device_id_type=MESH,
        )
        copy.start()
        halo.append(copy)
    def first_group(pair, tile):
        start = pl.multiple_of(pair * 128 + tile * 16, 16)
        cells = [grid_in[c, pl.ds(start, 16), :] for c in range(CIN)]
        stacked = jnp.concatenate(cells + [ones_mask[min(tile, 6)]], axis=0).astype(BF16)
        value = gelu_half(dot(first_w[tile > 5], stacked)).astype(BF16)
        for h in range(HID):
            hidden[h, pl.ds(start, 16), :] = value[16 * h : 16 * h + 16]

    def first_inner(pair, carry):
        for tile in range(1, 5):
            first_group(pair, tile)
        return carry

    lax.fori_loop(1, 4, first_inner, 0)

    for copy in halo:
        copy.wait()

    for c in range(CIN):
        low = jnp.where(high_x, x_send[0, c].astype(F32), keep_low * x_recv[0, c].astype(F32))
        high = jnp.where(high_x, keep_high * x_recv[1, c].astype(F32), x_send[1, c].astype(F32))
        for y in range(8):
            put(c, 0, 1 + y, low[8 * y : 8 * y + 8])
            put(c, 5, 1 + y, high[8 * y : 8 * y + 8])
        for side in range(2):
            own = y_recv[side, c].astype(F32)
            corner_low = keep_low * c_recv[0 + side, c].astype(F32)
            corner_high = keep_high * c_recv[2 + side, c].astype(F32)
            edge_lane = along_y == (0 if side == 0 else 3)
            for x in range(6):
                if x == 0:
                    far = jnp.where(high_x, pltpu.roll(own[24:32], 64, 1), corner_low)
                elif x == 5:
                    far = jnp.where(high_x, corner_high, pltpu.roll(own[0:8], 64, 1))
                else:
                    far = own[8 * (x - 1) : 8 * x]
                near = pltpu.roll(get(c, x, 8 if side == 0 else 1), 16 if side == 0 else 112, 1)
                put(c, x, 0 if side == 0 else 9, jnp.where(edge_lane, far, near))
        for pair in range(5):
            below = grid_in[c, pl.ds(pair * 128 + 7, 12, stride=8), :]
            above = grid_in[c, pl.ds(pair * 128, 12, stride=8), :]
            grid_in[c, pair * 128 + 96 : pair * 128 + 108, :] = jnp.where(
                along_z == 0, pltpu.roll(below, 113, 1), pltpu.roll(below, 1, 1)
            )
            grid_in[c, pair * 128 + 112 : pair * 128 + 124, :] = jnp.where(
                along_z == 15, pltpu.roll(above, 15, 1), pltpu.roll(above, 127, 1)
            )

    def first_edge_y(side, carry):
        for tile in range(1, 5):
            first_group(4 * side, tile)
        return carry

    def first_z(pair, carry):
        for tile in (6, 7):
            first_group(pair, tile)
        return carry

    def first_edge_x(pair, carry):
        for tile in (0, 5):
            first_group(pair, tile)
        return carry

    def depth_planes(planes):
        def depth_part(group, carry):
            parts = []
            for number in range(2):
                h = 2 * group + number
                weight = tap_w[h, 64 * (planes[0] == 0) : 64 * (planes[0] == 0) + 64, :]
                cells = [hidden[h, 128 * pair : 128 * pair + 256, :] for pair in range(4)]
                both = dot(weight, jnp.concatenate(cells, axis=1))
                parts.append(both[:32] + both[32:])
            start = pl.multiple_of(16 * group, 16)
            bias = depth_bias[pl.ds(start, 16), :]
            for number, x in enumerate(planes):
                for y in range(8):
                    first = 16 * number + 8 * (y % 2)
                    lanes = slice((y // 2) * LANES, (y // 2 + 1) * LANES)
                    both = jnp.concatenate([part[first : first + 8, lanes] for part in parts], axis=0)
                    depth[x, y, pl.ds(start, 16), :] = (both + bias).astype(BF16)
            return carry

        lax.fori_loop(0, 16, depth_part, 0)

    def plane(x, carry):
        def mix_part(group, inner):
            for number in range(2):
                y = 4 * group + 2 * number
                cells = jnp.concatenate([depth[x, y], depth[x, y + 1]], axis=1)
                bias = jnp.concatenate([mix_bias[...]] * 2, axis=1)
                mixed = gelu_half(dot(mix_w[...], cells) + bias).astype(BF16)
                field = dot(out_w[...], mixed)
                for side in range(2):
                    part = field[:, side * LANES : (side + 1) * LANES] + out_bias[...]
                    for f in range(COUT):
                        start = pl.multiple_of(f * 64 + 8 * (y + side), 8)
                        result[pl.ds(start, 8), :] = part[8 * f : 8 * f + 8]
            return inner

        lax.fori_loop(0, 2, mix_part, 0)

        odd = lax.rem(x, 2)
        turned = []
        for pair in range(3):
            first = result[pl.ds(pl.multiple_of((2 * pair + odd) * 64, 64), 64), :]
            second = result[pl.ds(pl.multiple_of((2 * pair + 1 - odd) * 64, 64), 64), :]
            turned.append(jnp.concatenate([first, second], axis=0).T.astype(BF16))
        packed = jnp.concatenate(turned, axis=1)
        leaving[x] = dot(scatter[...], packed).reshape(NDEV, 4, 3 * LANES).astype(BF16)
        for step in STEPS:
            other, where = coords(step)
            pltpu.make_async_remote_copy(
                src_ref=leaving.at[x, other], dst_ref=arrived.at[x, me],
                send_sem=back_send, recv_sem=back_recv.at[x], device_id=where, device_id_type=MESH,
            ).start()
        arrived[x, me] = leaving[x, me]
        return carry

    lax.fori_loop(0, 2, first_edge_y, 0)
    lax.fori_loop(0, 5, first_z, 0)
    depth_planes((1, 2))
    lax.fori_loop(1, 3, plane, 0)
    lax.fori_loop(0, 5, first_edge_x, 0)
    depth_planes((0, 3))
    lax.fori_loop(0, 2, lambda number, carry: plane(3 * number, carry), 0)

    low_half = iota((1, LANES), 1) < 64
    taken = {}
    for x in (1, 2, 0, 3):
        pltpu.make_async_copy(
            leaving.at[x, pl.ds(0, NDEV - 1)], arrived.at[x, pl.ds(0, NDEV - 1)], back_recv.at[x]
        ).wait()
        taken[x] = dot(place_slots[...], arrived[x].reshape(2 * SLOTS, 3 * LANES))
        if x in (1, 2):
            continue
        for half in range(2):
            rows = slice(half * CAP, (half + 1) * CAP)
            lanes = slice((2 * half + x // 2) * LANES, (2 * half + x // 2 + 1) * LANES)
            for pair in range(3):
                even = taken[x - x % 2][rows, pair * LANES : (pair + 1) * LANES]
                odd = taken[x - x % 2 + 1][rows, pair * LANES : (pair + 1) * LANES]
                out_ref[2 * pair, :, lanes] = jnp.where(low_half, even, odd).astype(BF16)
                out_ref[2 * pair + 1, :, lanes] = pltpu.roll(
                    jnp.where(low_half, odd, even), 64, 1
                ).astype(BF16)
    pltpu.make_async_copy(
        outgoing.at[pl.ds(0, NDEV - 1)], incoming.at[pl.ds(0, NDEV - 1)], send_sem
    ).wait()
    pltpu.make_async_copy(
        leaving.at[:, pl.ds(0, NDEV - 1)], arrived.at[:, pl.ds(0, NDEV - 1)], back_send
    ).wait()


VMEM = pl.BlockSpec(memory_space=pltpu.VMEM)
HBM = pl.BlockSpec(memory_space=pltpu.HBM)


def shards(
    fields, solver_counts, cnn_owner, in_weight, in_bias, depth_weight, depth_bias,
    mix_weight, mix_bias, out_weight, out_bias,
):
    closure = pl.pallas_call(
        closure_body,
        out_shape=jax.ShapeDtypeStruct((COUT, CAP, 4 * LANES), BF16),
        in_specs=[HBM] * 11,
        out_specs=VMEM,
        scratch_shapes=[
            pltpu.VMEM((1, NDEV), I32),
            pltpu.VMEM((64, LANES), I32),
            pltpu.VMEM((CIN, CAP, 4 * LANES), BF16),
            pltpu.VMEM((CIN, HID), BF16),
            pltpu.VMEM((1, HID), F32),
            pltpu.VMEM((HID, 27), F32),
            pltpu.VMEM((1, HID), F32),
            pltpu.VMEM((HID, HID), BF16),
            pltpu.VMEM((1, HID), F32),
            pltpu.VMEM((COUT, HID), BF16),
            pltpu.VMEM((1, COUT), F32),
            pltpu.VMEM((8 * HID, 8 * HID), BF16),
            pltpu.VMEM((8 * COUT, 8 * HID), BF16),
            pltpu.VMEM((8 * COUT, LANES), F32),
            pltpu.VMEM((CIN, ROWS, LANES), F32),
            pltpu.VMEM((NDEV, 8, CIN * LANES), BF16),
            pltpu.VMEM((NDEV, 8, CIN * LANES), BF16),
            pltpu.VMEM((CIN, 640, LANES), F32),
            pltpu.VMEM((7, 16, LANES), F32),
            pltpu.VMEM((HID, 640, LANES), BF16),
            pltpu.VMEM((2, 128 * HID, LANES), F32),
            pltpu.VMEM((HID, 128, 2 * LANES), BF16),
            pltpu.VMEM((8 * HID, LANES), F32),
            pltpu.VMEM((8 * HID, LANES), F32),
            pltpu.VMEM((4, 8, 8 * HID, LANES), BF16),
            pltpu.VMEM((64 * COUT, LANES), F32),
            pltpu.VMEM((2 * SLOTS, LANES), BF16),
            pltpu.VMEM((2 * CAP, 2 * SLOTS), BF16),
            pltpu.VMEM((2, CIN, 64, LANES), BF16),
            pltpu.VMEM((2, CIN, 64, LANES), BF16),
            pltpu.VMEM((2, CIN, 32, LANES), BF16),
            pltpu.VMEM((2, CIN, 32, LANES), BF16),
            pltpu.VMEM((4, CIN, 8, LANES), BF16),
            pltpu.VMEM((4, CIN, 8, LANES), BF16),
            pltpu.VMEM((4, NDEV, 4, 3 * LANES), BF16),
            pltpu.VMEM((4, NDEV, 4, 3 * LANES), BF16),
            pltpu.SemaphoreType.DMA((11,)),
            pltpu.SemaphoreType.DMA,
            pltpu.SemaphoreType.DMA,
            pltpu.SemaphoreType.DMA((8,)),
            pltpu.SemaphoreType.DMA((8,)),
            pltpu.SemaphoreType.DMA,
            pltpu.SemaphoreType.DMA((4,)),
        ],
        compiler_params=pltpu.CompilerParams(
            collective_id=0, has_side_effects=True, vmem_limit_bytes=36 * 1024 * 1024
        ),
        name="closure",
    )(*(
        pltpu.with_memory_space_constraint(operand, pltpu.HBM)
        for operand in (
            solver_counts.reshape(1, NDEV),
            cnn_owner.reshape(64, LANES),
            jnp.transpose(fields, (1, 0, 2)),
            jnp.transpose(in_weight),
            in_bias.reshape(1, HID),
            depth_weight,
            depth_bias.reshape(1, HID),
            mix_weight,
            mix_bias.reshape(1, HID),
            out_weight,
            out_bias.reshape(1, COUT),
        )
    ))
    return jnp.transpose(closure, (1, 0, 2))


def solution(mesh):
    return jax.shard_map(
        shards,
        mesh=mesh,
        in_specs=(P(("gx", "yz"), None, None), P(), P(), P(), P(), P(), P(), P(), P(), P(), P()),
        out_specs=P(("gx", "yz"), None, None),
        check_vma=False,
    )
```

```python
import jax
import jax.numpy as jnp
from jax import lax
from jax.experimental import pallas as pl
from jax.experimental.pallas import tpu as pltpu
from jax.sharding import PartitionSpec as P

MESH = pl.DeviceIdType.MESH
NDEV = 128
N_GX = 4
N_YZ = 32
CAP = 192
CIN = 5
HID = 32
COUT = 6
LANES = 128
SLOTS = 2 * NDEV
ROWS = 4 * SLOTS
F32 = jnp.float32
BF16 = jnp.bfloat16
I32 = jnp.int32
GELU_A = 2.0 * 0.7978845608028654
GELU_B = 8.0 * 0.7978845608028654 * 0.044715


STEPS = sorted(
    [(x, y, z, c) for x in range(4) for y in range(4) for z in range(4) for c in range(2)],
    key=lambda step: -sum(min(part, 4 - part) for part in step[:3]),
)[:-2] + [(0, 0, 0, 1)]


def iota(shape, dim):
    return lax.broadcasted_iota(I32, shape, dim)


def dot(a, b):
    return jnp.dot(a, b, preferred_element_type=F32)


def one_hot(condition):
    return jnp.where(condition, 1.0, 0.0).astype(BF16)


def row_to_col(row):
    count = row.shape[1]
    same = iota((count, count), 0) == iota((count, count), 1)
    return jnp.sum(jnp.where(same, row, 0.0), axis=1, keepdims=True)


def col_to_row(col):
    count = col.shape[0]
    same = iota((count, count), 0) == iota((count, count), 1)
    return jnp.sum(jnp.where(same, col, 0.0), axis=0, keepdims=True)


def gelu_half(y):
    return y + y * jnp.tanh(y * (GELU_A + GELU_B * (y * y)))


def run_cumulative(me, counts, owner):
    lower = iota((NDEV, NDEV), 1) <= iota((NDEV, NDEV), 0)
    run_end = jnp.sum(jnp.where(lower, counts, 0.0), axis=1, keepdims=True).astype(I32)
    mine = one_hot(owner == me)
    rows = iota((NDEV, 64), 1)
    whole = dot(one_hot(rows < (run_end >> 7)), mine)
    part = dot(one_hot(rows == (run_end >> 7)), mine)
    inside = iota((NDEV, LANES), 1) < (run_end & 127)
    return jnp.sum(whole + jnp.where(inside, part, 0.0), axis=1, keepdims=True)


def brick_keys(cum_col):
    cum_row = col_to_row(cum_col)
    row = iota((2 * LANES, NDEV), 0)
    patch = (row & 63).astype(F32)
    below = cum_row <= patch
    source = jnp.sum(jnp.where(below, 1.0, 0.0), axis=1, keepdims=True)
    before = jnp.max(jnp.where(below, cum_row, 0.0), axis=1, keepdims=True)
    row = iota((2 * LANES, 1), 0)
    place = 2.0 * source + ((row & 63).astype(F32) - before)
    key_col = 4 * place.astype(I32) + 2 * ((row >> 6) & 1) + (row >> 7)
    patch = (iota((NDEV, LANES), 1) & 63).astype(F32)
    below = cum_col <= patch
    source = jnp.sum(jnp.where(below, 1.0, 0.0), axis=0, keepdims=True)
    before = jnp.max(jnp.where(below, cum_col, 0.0), axis=0, keepdims=True)
    lane = iota((1, LANES), 1)
    place = 2.0 * source + ((lane & 63).astype(F32) - before)
    key_row = 2 * place.astype(I32) + (lane >> 6)
    return key_col, key_row


def slot_keys(me, counts, owner):
    lane = iota((1, NDEV), 1)
    start = jnp.sum(jnp.where(lane < me, counts, 0.0), axis=1, keepdims=True).astype(I32)
    count = jnp.sum(jnp.where(lane == me, counts, 0.0), axis=1, keepdims=True).astype(I32)
    position = iota((CAP, 1), 0) + start
    rows = dot(one_hot(iota((CAP, 64), 1) == (position >> 7)), owner.astype(F32).astype(BF16))
    here = iota((CAP, LANES), 1) == (position & 127)
    owner_col = jnp.sum(jnp.where(here, rows, 0.0), axis=1, keepdims=True)
    owner_row = col_to_row(owner_col)
    same = owner_col == owner_row
    first = iota((CAP, CAP), 0)
    second = iota((CAP, CAP), 1)
    rank_col = jnp.sum(jnp.where(same & (second < first), 1.0, 0.0), axis=1, keepdims=True)
    rank_row = jnp.sum(jnp.where(same & (first < second), 1.0, 0.0), axis=0, keepdims=True)
    key_col = (2.0 * owner_col + rank_col).astype(I32)
    key_row = (2.0 * owner_row + rank_row).astype(I32)
    key_col = jnp.where(iota((CAP, 1), 0) < count, key_col, -1)
    key_row = jnp.where(iota((1, CAP), 1) < count, key_row, -1)
    return key_col, key_row


def split3(value):
    high = value.astype(BF16).astype(F32)
    middle = (value - high).astype(BF16).astype(F32)
    low = value - high - middle
    return high, middle, low


def repeat_rows(value, count):
    rows, lanes = value.shape
    return jnp.broadcast_to(value[:, None, :], (rows, count, lanes)).reshape(rows * count, lanes)


def first_weights(in_weight, in_bias, z_halo):
    lane = iota((HID, 96), 1)
    base = jnp.zeros((HID, 96), F32)
    for c in range(CIN):
        base = jnp.where((lane >> 4) == c, 0.5 * row_to_col(in_weight[c : c + 1, :]), base)
    for number, part in enumerate(split3(0.5 * row_to_col(in_bias))):
        for mask in range(3):
            base = jnp.where(lane == 80 + 3 * mask + number, part, base)
    base = repeat_rows(base, 16)
    lane = iota((16 * HID, 96), 1)
    cell = iota((16 * HID, 96), 0) & 15
    first = jnp.where(cell < 2, 83, jnp.where((cell >> 1) == 5, 86, 80)) if z_halo else 80
    own = jnp.where(lane < 80, cell, -1) == (lane & 15)
    keep = own | ((lane >= first) & (lane < first + 3))
    return jnp.where(keep, base, 0.0).astype(BF16)


def over_cells(weight):
    rows, depth = weight.shape
    widen = one_hot(iota((depth, 8 * depth), 0) == (iota((depth, 8 * depth), 1) >> 3))
    wide = repeat_rows(dot(weight, widen), 8)
    keep = (iota(wide.shape, 0) & 7) == (iota(wide.shape, 1) & 7)
    return jnp.where(keep, wide, 0.0).astype(BF16)


def tap_places(x, pair):
    lane = iota((1, 2048), 1)
    z = lane >> 8
    side = (lane >> 7) & 1
    row = lane & 127
    edge = row - 96
    far = edge & 15
    regular = row < 96
    in_x = jnp.where(regular, row >> 4, far >> 1)
    in_y = jnp.where(regular, (row >> 3) & 1, far & 1)
    in_z = jnp.where(regular, row & 7, jnp.where(edge >= 16, 8, -1))
    a = in_x - x
    b = 2 * side + in_y - pair
    c = in_z - z + 1
    valid = (a >= 0) & (a <= 2) & (b >= 0) & (b <= 2) & (c >= 0) & (c <= 2)
    valid = valid & (regular | (far < 12))
    tap = jnp.where(valid, 9 * a + 3 * b + c, -1)
    return one_hot(iota((32, 2048), 0) == tap)


def closure_body(
    counts_in, owner_in, fields_in, in_weight_in, in_bias_in, depth_weight_in, depth_bias_in,
    mix_weight_in, mix_bias_in, out_weight_in, out_bias_in,
    out_ref,
    counts_ref, owner_ref, fields_ref, in_weight_ref, in_bias_ref, depth_weight_ref, depth_bias_ref,
    mix_weight_ref, mix_bias_ref, out_weight_ref, out_bias_ref, mix_w, out_w, out_bias,
    spread, outgoing, incoming, grid_in, ones_mask, hidden, band, tap_w, depth_bias, mix_bias, depth, result, scatter,
    place_slots, x_send, x_recv, y_send, y_recv, c_send, c_recv, leaving, arrived,
    fetch_sem, send_sem, recv_sem, halo_send, halo_recv, back_send, back_recv,
):
    fetches = [
        pltpu.make_async_copy(source, target, fetch_sem.at[number])
        for number, (source, target) in enumerate((
            (counts_in, counts_ref), (owner_in, owner_ref), (fields_in, fields_ref),
            (in_weight_in, in_weight_ref), (in_bias_in, in_bias_ref),
            (depth_weight_in, depth_weight_ref), (depth_bias_in, depth_bias_ref),
            (mix_weight_in, mix_weight_ref), (mix_bias_in, mix_bias_ref),
            (out_weight_in, out_weight_ref), (out_bias_in, out_bias_ref),
        ))
    ]
    for fetch in fetches:
        fetch.start()
    gx = lax.axis_index("gx")
    yz = lax.axis_index("yz")
    me = gx * N_YZ + yz
    at_x = [lax.rem(gx + step, 4) for step in range(4)]
    at_y = [8 * lax.rem(lax.div(yz, 8) + step, 4) for step in range(4)]
    at_z = [2 * lax.rem(lax.div(yz, 2) + step, 4) for step in range(4)]
    at_core = [lax.rem(yz + step, 2) for step in range(2)]

    def coords(step):
        where = (at_x[step[0]], at_y[step[1]] + at_z[step[2]] + at_core[step[3]])
        return where[0] * N_YZ + where[1], where

    barrier = pltpu.get_barrier_semaphore()
    for step in STEPS:
        pl.semaphore_signal(barrier, inc=1, device_id=coords(step)[1], device_id_type=MESH)

    for fetch in fetches[:3]:
        fetch.wait()
    counts = counts_ref[...].astype(F32)
    owner = owner_ref[...]
    key_col, key_row = slot_keys(me, counts, owner)
    select = one_hot(iota((SLOTS, CAP), 0) == key_row)
    for c in range(CIN):
        rows = dot(select, fields_ref[c])
        for part in range(4):
            spread[c, pl.ds(part, SLOTS, stride=4), :] = rows[:, part * LANES : (part + 1) * LANES]
    for c in range(CIN):
        outgoing[:, :, c * LANES : (c + 1) * LANES] = (
            spread[c].reshape(NDEV, 8, LANES).astype(BF16)
        )

    pl.semaphore_wait(barrier, NDEV - 1)

    for step in STEPS:
        other, where = coords(step)
        pltpu.make_async_remote_copy(
            src_ref=outgoing.at[other], dst_ref=incoming.at[me],
            send_sem=send_sem, recv_sem=recv_sem, device_id=where, device_id_type=MESH,
        ).start()
    incoming[me] = outgoing[me]

    cum_col = run_cumulative(me, counts, owner)
    brick_col, brick_row = brick_keys(cum_col)
    gather = one_hot(iota((2 * LANES, ROWS), 1) == brick_col)
    scatter[...] = one_hot(iota((2 * SLOTS, LANES), 0) == brick_row)
    for half in range(2):
        wanted = jnp.where(key_col < 0, -1, 2 * key_col + half)
        place_slots[half * CAP : (half + 1) * CAP, :] = one_hot(
            iota((CAP, 2 * SLOTS), 1) == wanted
        )
    lane = iota((1, LANES), 1)
    high_x = ((lane >> 6) & 1) == 1
    along_y = (lane >> 4) & 3
    along_z = lane & 15
    keep_low = jnp.where(gx > 0, 1.0, 0.0).astype(F32)
    keep_high = jnp.where(gx < N_GX - 1, 1.0, 0.0).astype(F32)
    masks = [jnp.ones((1, LANES), F32)] * 6
    masks[0] = jnp.where(high_x, 1.0, keep_low)
    masks[5] = jnp.where(high_x, keep_high, 1.0)
    for x in range(6):
        ones_mask[x] = jnp.broadcast_to(masks[x], (16, LANES))
    line = iota((16, LANES), 0)
    ones_mask[6] = jnp.where(line < 3, 1.0, jnp.where(line < 6, masks[0], masks[5]))
    for fetch in fetches[3:]:
        fetch.wait()
    in_weight = in_weight_ref[...].astype(F32)
    first_w = [first_weights(in_weight, in_bias_ref[...], z_halo) for z_halo in (False, True)]
    mix_w[...] = over_cells((0.5 * mix_weight_ref[...].astype(F32)).astype(BF16))
    out_w[...] = over_cells(out_weight_ref[...])
    depth_bias[...] = repeat_rows(
        jnp.broadcast_to(row_to_col(depth_bias_ref[...]), (HID, LANES)), 8
    )
    mix_bias[...] = repeat_rows(
        jnp.broadcast_to(0.5 * row_to_col(mix_bias_ref[...]), (HID, LANES)), 8
    )
    out_bias[...] = repeat_rows(jnp.broadcast_to(row_to_col(out_bias_ref[...]), (COUT, LANES)), 8)
    taps = jnp.concatenate([depth_weight_ref[...], jnp.zeros((HID, 5), F32)], axis=1)
    high = taps.astype(BF16)
    taps = jnp.concatenate([high, (taps - high.astype(F32)).astype(BF16)], axis=0)

    def band_rows(group, carry):
        rows = dot(taps, tap_places(lax.div(group, 2), lax.rem(group, 2)))
        for z in range(8):
            start = pl.multiple_of((group * 8 + z) * 2 * HID, 2 * HID)
            for side in range(2):
                first = z * 256 + side * LANES
                band[side, pl.ds(start, 2 * HID), :] = rows[:, first : first + LANES]
        return carry

    lax.fori_loop(0, 8, band_rows, 0)

    def band_channel(h, carry):
        row = 0
        for planes in ((1, 2), (0, 3)):
            for part in range(2):
                for x in planes:
                    for side in range(2):
                        rows = band[side, pl.ds(x * 32 * HID + part * HID + h, 16, stride=2 * HID), :]
                        tap_w[h, row : row + 16, side * LANES : (side + 1) * LANES] = rows.astype(BF16)
                    row += 16
        return carry

    lax.fori_loop(0, HID, band_channel, 0)
    grid_in[...] = jnp.zeros_like(grid_in)
    for pair in range(5):
        for tile in (0, 5):
            first = pair * 128 + tile * 16
            hidden[:, first : first + 16, :] = jnp.zeros((HID, 16, LANES), BF16)

    every = pltpu.make_async_copy(
        outgoing.at[pl.ds(0, NDEV - 1)], incoming.at[pl.ds(0, NDEV - 1)], recv_sem
    )
    every.wait()

    def place(x, y):
        return (y // 2) * 128 + x * 16 + (y % 2) * 8

    def get(c, x, y):
        return grid_in[c, place(x, y) : place(x, y) + 8, :]

    def put(c, x, y, value):
        grid_in[c, place(x, y) : place(x, y) + 8, :] = value

    bricks = dot(gather, incoming[...].reshape(ROWS, CIN * LANES))
    for c in range(CIN):
        for m in range(2):
            turned = bricks[m * LANES : (m + 1) * LANES, c * LANES : (c + 1) * LANES].T
            for p in range(2):
                for y in range(8):
                    first = p * 64 + y * 8
                    put(c, 1 + 2 * m + p, 1 + y, turned[first : first + 8])

    for c in range(CIN):
        for side, x in enumerate((4, 1)):
            cells = jnp.concatenate([get(c, x, y) for y in range(1, 9)], axis=0)
            x_send[side, c] = pltpu.roll(cells, 64, 1).astype(BF16)
        last_y = [get(c, x, 8) for x in range(1, 5)]
        first_y = [get(c, x, 1) for x in range(1, 5)]
        y_send[0, c] = pltpu.roll(jnp.concatenate(last_y, axis=0), 80, 1).astype(BF16)
        y_send[1, c] = pltpu.roll(jnp.concatenate(first_y, axis=0), 48, 1).astype(BF16)
        c_send[0, c] = pltpu.roll(last_y[3], 16, 1).astype(BF16)
        c_send[1, c] = pltpu.roll(first_y[3], 112, 1).astype(BF16)
        c_send[2, c] = pltpu.roll(last_y[0], 16, 1).astype(BF16)
        c_send[3, c] = pltpu.roll(first_y[0], 112, 1).astype(BF16)
    up_x = lax.rem(gx + 1, N_GX)
    down_x = lax.rem(gx + N_GX - 1, N_GX)
    up_y = lax.rem(yz + 1, N_YZ)
    down_y = lax.rem(yz + N_YZ - 1, N_YZ)
    halo = []
    for source, target, where in (
        (x_send.at[0], x_recv.at[0], (up_x, yz)),
        (x_send.at[1], x_recv.at[1], (down_x, yz)),
        (y_send.at[0], y_recv.at[0], (gx, up_y)),
        (y_send.at[1], y_recv.at[1], (gx, down_y)),
        (c_send.at[0], c_recv.at[0], (up_x, up_y)),
        (c_send.at[1], c_recv.at[1], (up_x, down_y)),
        (c_send.at[2], c_recv.at[2], (down_x, up_y)),
        (c_send.at[3], c_recv.at[3], (down_x, down_y)),
    ):
        number = len(halo)
        copy = pltpu.make_async_remote_copy(
            src_ref=source, dst_ref=target, send_sem=halo_send.at[number],
            recv_sem=halo_recv.at[number], device_id=where, device_id_type=MESH,
        )
        copy.start()
        halo.append(copy)
    def first_group(pair, tile):
        start = pl.multiple_of(pair * 128 + tile * 16, 16)
        cells = [grid_in[c, pl.ds(start, 16), :] for c in range(CIN)]
        stacked = jnp.concatenate(cells + [ones_mask[min(tile, 6)]], axis=0).astype(BF16)
        value = gelu_half(dot(first_w[tile > 5], stacked)).astype(BF16)
        for h in range(HID):
            hidden[h, pl.ds(start, 16), :] = value[16 * h : 16 * h + 16]

    def first_pairs(pairs, tiles):
        def pair_tiles(number, carry):
            for tile in tiles:
                first_group(pairs[0] + (pairs[1] - pairs[0]) * number, tile)
            return carry

        lax.fori_loop(0, len(pairs), pair_tiles, 0)

    def z_halo(pairs):
        for c in range(CIN):
            for pair in pairs:
                below = grid_in[c, pl.ds(pair * 128 + 7, 12, stride=8), :]
                above = grid_in[c, pl.ds(pair * 128, 12, stride=8), :]
                grid_in[c, pair * 128 + 96 : pair * 128 + 108, :] = jnp.where(
                    along_z == 0, pltpu.roll(below, 113, 1), pltpu.roll(below, 1, 1)
                )
                grid_in[c, pair * 128 + 112 : pair * 128 + 124, :] = jnp.where(
                    along_z == 15, pltpu.roll(above, 15, 1), pltpu.roll(above, 127, 1)
                )

    def finish(chunk, planes, pairs):
        tap_rows = slice(64 * (planes[0] == 0), 64 * (planes[0] == 0) + 64)

        def depth_part(group, carry):
            parts = []
            for number in range(2):
                h = 2 * group + number
                cells = [hidden[h, 128 * pair : 128 * pair + 256, :] for pair in pairs]
                both = dot(tap_w[h, tap_rows, :], jnp.concatenate(cells, axis=1))
                parts.append(both[:32] + both[32:])
            start = pl.multiple_of(16 * group, 16)
            bias = depth_bias[pl.ds(start, 16), :]
            for x in range(2):
                for y in range(4):
                    first = 16 * x + 8 * (y % 2)
                    lanes = slice((y // 2) * LANES, (y // 2 + 1) * LANES)
                    both = jnp.concatenate([part[first : first + 8, lanes] for part in parts], axis=0)
                    depth[4 * x + y, pl.ds(start, 16), :] = (both + bias).astype(BF16)
            return carry

        lax.fori_loop(0, 16, depth_part, 0)

        def mix_part(group, carry):
            for number in range(2):
                row = 4 * group + 2 * number
                cells = jnp.concatenate([depth[row], depth[row + 1]], axis=1)
                bias = jnp.concatenate([mix_bias[...]] * 2, axis=1)
                mixed = gelu_half(dot(mix_w[...], cells) + bias).astype(BF16)
                field = dot(out_w[...], mixed)
                for side in range(2):
                    part = field[:, side * LANES : (side + 1) * LANES] + out_bias[...]
                    for f in range(COUT):
                        start = pl.multiple_of(f * 64 + 8 * (row + side), 8)
                        result[pl.ds(start, 8), :] = part[8 * f : 8 * f + 8]
            return carry

        lax.fori_loop(0, 2, mix_part, 0)

        turned = []
        for pair in range(3):
            blocks = [None] * 16
            for x, plane in enumerate(planes):
                for y in range(4):
                    to = 8 * (plane % 2) + 2 * pairs[y // 2] + y % 2
                    for f in range(2):
                        start = (2 * pair + f) * 64 + x * 32 + y * 8
                        blocks[(to + 4 * f) % 16] = result[start : start + 8, :]
            turned.append(jnp.concatenate(blocks, axis=0).T.astype(BF16))
        packed = jnp.concatenate(turned, axis=1)
        leaving[chunk] = dot(scatter[...], packed).reshape(NDEV, 4, 3 * LANES).astype(BF16)
        for step in STEPS:
            other, where = coords(step)
            pltpu.make_async_remote_copy(
                src_ref=leaving.at[chunk, other], dst_ref=arrived.at[chunk, me],
                send_sem=back_send, recv_sem=back_recv.at[chunk], device_id=where,
                device_id_type=MESH,
            ).start()
        arrived[chunk, me] = leaving[chunk, me]

    z_halo((1, 2, 3))
    first_pairs((1, 2, 3), (1, 2, 3, 4, 6, 7))
    finish(0, (1, 2), (1, 2))

    for copy in halo:
        copy.wait()

    for c in range(CIN):
        low = jnp.where(high_x, x_send[0, c].astype(F32), keep_low * x_recv[0, c].astype(F32))
        high = jnp.where(high_x, keep_high * x_recv[1, c].astype(F32), x_send[1, c].astype(F32))
        for y in range(8):
            put(c, 0, 1 + y, low[8 * y : 8 * y + 8])
            put(c, 5, 1 + y, high[8 * y : 8 * y + 8])
        for side in range(2):
            own = y_recv[side, c].astype(F32)
            corner_low = keep_low * c_recv[0 + side, c].astype(F32)
            corner_high = keep_high * c_recv[2 + side, c].astype(F32)
            edge_lane = along_y == (0 if side == 0 else 3)
            for x in range(6):
                if x == 0:
                    far = jnp.where(high_x, pltpu.roll(own[24:32], 64, 1), corner_low)
                elif x == 5:
                    far = jnp.where(high_x, corner_high, pltpu.roll(own[0:8], 64, 1))
                else:
                    far = own[8 * (x - 1) : 8 * x]
                near = pltpu.roll(get(c, x, 8 if side == 0 else 1), 16 if side == 0 else 112, 1)
                put(c, x, 0 if side == 0 else 9, jnp.where(edge_lane, far, near))

    z_halo(range(5))
    first_pairs((0, 4), (1, 2, 3, 4, 6, 7))
    finish(1, (1, 2), (0, 3))
    first_pairs((1, 2, 3), (0, 5, 6, 7))
    finish(2, (0, 3), (1, 2))
    first_pairs((0, 4), (0, 5))
    finish(3, (0, 3), (0, 3))

    low_half = iota((1, LANES), 1) < 64
    inner_y = ((iota((1, LANES), 1) + 16) & 63) >= 32
    taken = []
    sides = []
    for chunk in range(4):
        pltpu.make_async_copy(
            leaving.at[chunk, pl.ds(0, NDEV - 1)], arrived.at[chunk, pl.ds(0, NDEV - 1)],
            back_recv.at[chunk],
        ).wait()
        taken.append(dot(place_slots[...], arrived[chunk].reshape(2 * SLOTS, 3 * LANES)))
        if chunk % 2 == 0:
            continue
        inner, outer = taken[chunk - 1], taken[chunk]
        fields = []
        for pair in range(3):
            lanes = slice(pair * LANES, (pair + 1) * LANES)
            fields.append(jnp.where(inner_y, inner[:, lanes], outer[:, lanes]))
            fields.append(pltpu.roll(jnp.where(inner_y, outer[:, lanes], inner[:, lanes]), 96, 1))
        sides.append(fields)
    for half in range(2):
        rows = slice(half * CAP, (half + 1) * CAP)
        for f in range(COUT):
            middle, ends = sides[0][f][rows], sides[1][f][rows]
            lanes = slice(2 * half * LANES, (2 * half + 1) * LANES)
            out_ref[f, :, lanes] = jnp.where(low_half, ends, middle).astype(BF16)
            lanes = slice((2 * half + 1) * LANES, (2 * half + 2) * LANES)
            out_ref[f, :, lanes] = jnp.where(low_half, middle, ends).astype(BF16)
    pltpu.make_async_copy(
        outgoing.at[pl.ds(0, NDEV - 1)], incoming.at[pl.ds(0, NDEV - 1)], send_sem
    ).wait()
    pltpu.make_async_copy(
        leaving.at[:, pl.ds(0, NDEV - 1)], arrived.at[:, pl.ds(0, NDEV - 1)], back_send
    ).wait()


VMEM = pl.BlockSpec(memory_space=pltpu.VMEM)
HBM = pl.BlockSpec(memory_space=pltpu.HBM)


def shards(
    fields, solver_counts, cnn_owner, in_weight, in_bias, depth_weight, depth_bias,
    mix_weight, mix_bias, out_weight, out_bias,
):
    closure = pl.pallas_call(
        closure_body,
        out_shape=jax.ShapeDtypeStruct((COUT, CAP, 4 * LANES), BF16),
        in_specs=[HBM] * 11,
        out_specs=VMEM,
        scratch_shapes=[
            pltpu.VMEM((1, NDEV), I32),
            pltpu.VMEM((64, LANES), I32),
            pltpu.VMEM((CIN, CAP, 4 * LANES), BF16),
            pltpu.VMEM((CIN, HID), BF16),
            pltpu.VMEM((1, HID), F32),
            pltpu.VMEM((HID, 27), F32),
            pltpu.VMEM((1, HID), F32),
            pltpu.VMEM((HID, HID), BF16),
            pltpu.VMEM((1, HID), F32),
            pltpu.VMEM((COUT, HID), BF16),
            pltpu.VMEM((1, COUT), F32),
            pltpu.VMEM((8 * HID, 8 * HID), BF16),
            pltpu.VMEM((8 * COUT, 8 * HID), BF16),
            pltpu.VMEM((8 * COUT, LANES), F32),
            pltpu.VMEM((CIN, ROWS, LANES), F32),
            pltpu.VMEM((NDEV, 8, CIN * LANES), BF16),
            pltpu.VMEM((NDEV, 8, CIN * LANES), BF16),
            pltpu.VMEM((CIN, 640, LANES), F32),
            pltpu.VMEM((7, 16, LANES), F32),
            pltpu.VMEM((HID, 640, LANES), BF16),
            pltpu.VMEM((2, 128 * HID, LANES), F32),
            pltpu.VMEM((HID, 128, 2 * LANES), BF16),
            pltpu.VMEM((8 * HID, LANES), F32),
            pltpu.VMEM((8 * HID, LANES), F32),
            pltpu.VMEM((8, 8 * HID, LANES), BF16),
            pltpu.VMEM((64 * COUT, LANES), F32),
            pltpu.VMEM((2 * SLOTS, LANES), BF16),
            pltpu.VMEM((2 * CAP, 2 * SLOTS), BF16),
            pltpu.VMEM((2, CIN, 64, LANES), BF16),
            pltpu.VMEM((2, CIN, 64, LANES), BF16),
            pltpu.VMEM((2, CIN, 32, LANES), BF16),
            pltpu.VMEM((2, CIN, 32, LANES), BF16),
            pltpu.VMEM((4, CIN, 8, LANES), BF16),
            pltpu.VMEM((4, CIN, 8, LANES), BF16),
            pltpu.VMEM((4, NDEV, 4, 3 * LANES), BF16),
            pltpu.VMEM((4, NDEV, 4, 3 * LANES), BF16),
            pltpu.SemaphoreType.DMA((11,)),
            pltpu.SemaphoreType.DMA,
            pltpu.SemaphoreType.DMA,
            pltpu.SemaphoreType.DMA((8,)),
            pltpu.SemaphoreType.DMA((8,)),
            pltpu.SemaphoreType.DMA,
            pltpu.SemaphoreType.DMA((4,)),
        ],
        compiler_params=pltpu.CompilerParams(
            collective_id=0, has_side_effects=True, vmem_limit_bytes=36 * 1024 * 1024
        ),
        name="closure",
    )(*(
        pltpu.with_memory_space_constraint(operand, pltpu.HBM)
        for operand in (
            solver_counts.reshape(1, NDEV),
            cnn_owner.reshape(64, LANES),
            jnp.transpose(fields, (1, 0, 2)),
            jnp.transpose(in_weight),
            in_bias.reshape(1, HID),
            depth_weight,
            depth_bias.reshape(1, HID),
            mix_weight,
            mix_bias.reshape(1, HID),
            out_weight,
            out_bias.reshape(1, COUT),
        )
    ))
    return jnp.transpose(closure, (1, 0, 2))


def solution(mesh):
    return jax.shard_map(
        shards,
        mesh=mesh,
        in_specs=(P(("gx", "yz"), None, None), P(), P(), P(), P(), P(), P(), P(), P(), P(), P()),
        out_specs=P(("gx", "yz"), None, None),
        check_vma=False,
    )
```

```python
import jax
import jax.numpy as jnp
from jax import lax
from jax.experimental import pallas as pl
from jax.experimental.pallas import tpu as pltpu
from jax.sharding import PartitionSpec as P

MESH = pl.DeviceIdType.MESH
NDEV = 128
N_GX = 4
N_YZ = 32
CAP = 192
CIN = 5
HID = 32
COUT = 6
LANES = 128
SLOTS = 2 * NDEV
ROWS = 4 * SLOTS
F32 = jnp.float32
BF16 = jnp.bfloat16
I32 = jnp.int32
GELU_A = 2.0 * 0.7978845608028654
GELU_B = 8.0 * 0.7978845608028654 * 0.044715


STEPS = sorted(
    [(x, y, z, c) for x in range(4) for y in range(4) for z in range(4) for c in range(2)],
    key=lambda step: -sum(min(part, 4 - part) for part in step[:3]),
)[:-2] + [(0, 0, 0, 1)]


def iota(shape, dim):
    return lax.broadcasted_iota(I32, shape, dim)


def dot(a, b):
    return jnp.dot(a, b, preferred_element_type=F32)


def one_hot(condition):
    return jnp.where(condition, 1.0, 0.0).astype(BF16)


def row_to_col(row):
    count = row.shape[1]
    same = iota((count, count), 0) == iota((count, count), 1)
    return jnp.sum(jnp.where(same, row, 0.0), axis=1, keepdims=True)


def col_to_row(col):
    count = col.shape[0]
    same = iota((count, count), 0) == iota((count, count), 1)
    return jnp.sum(jnp.where(same, col, 0.0), axis=0, keepdims=True)


def gelu_half(y):
    return y + y * jnp.tanh(y * (GELU_A + GELU_B * (y * y)))


def run_cumulative(me, counts, owner):
    lower = iota((NDEV, NDEV), 1) <= iota((NDEV, NDEV), 0)
    run_end = jnp.sum(jnp.where(lower, counts, 0.0), axis=1, keepdims=True).astype(I32)
    mine = one_hot(owner == me)
    rows = iota((NDEV, 64), 1)
    whole = dot(one_hot(rows < (run_end >> 7)), mine)
    part = dot(one_hot(rows == (run_end >> 7)), mine)
    inside = iota((NDEV, LANES), 1) < (run_end & 127)
    return jnp.sum(whole + jnp.where(inside, part, 0.0), axis=1, keepdims=True)


def brick_keys(cum_col):
    cum_row = col_to_row(cum_col)
    row = iota((2 * LANES, NDEV), 0)
    patch = (row & 63).astype(F32)
    below = cum_row <= patch
    source = jnp.sum(jnp.where(below, 1.0, 0.0), axis=1, keepdims=True)
    before = jnp.max(jnp.where(below, cum_row, 0.0), axis=1, keepdims=True)
    row = iota((2 * LANES, 1), 0)
    place = 2.0 * source + ((row & 63).astype(F32) - before)
    key_col = 4 * place.astype(I32) + 2 * ((row >> 6) & 1) + (row >> 7)
    patch = (iota((NDEV, LANES), 1) & 63).astype(F32)
    below = cum_col <= patch
    source = jnp.sum(jnp.where(below, 1.0, 0.0), axis=0, keepdims=True)
    before = jnp.max(jnp.where(below, cum_col, 0.0), axis=0, keepdims=True)
    lane = iota((1, LANES), 1)
    place = 2.0 * source + ((lane & 63).astype(F32) - before)
    key_row = 2 * place.astype(I32) + (lane >> 6)
    return key_col, key_row


def slot_keys(me, counts, owner):
    lane = iota((1, NDEV), 1)
    start = jnp.sum(jnp.where(lane < me, counts, 0.0), axis=1, keepdims=True).astype(I32)
    count = jnp.sum(jnp.where(lane == me, counts, 0.0), axis=1, keepdims=True).astype(I32)
    position = iota((CAP, 1), 0) + start
    rows = dot(one_hot(iota((CAP, 64), 1) == (position >> 7)), owner.astype(F32).astype(BF16))
    here = iota((CAP, LANES), 1) == (position & 127)
    owner_col = jnp.sum(jnp.where(here, rows, 0.0), axis=1, keepdims=True)
    owner_row = col_to_row(owner_col)
    same = owner_col == owner_row
    first = iota((CAP, CAP), 0)
    second = iota((CAP, CAP), 1)
    rank_col = jnp.sum(jnp.where(same & (second < first), 1.0, 0.0), axis=1, keepdims=True)
    rank_row = jnp.sum(jnp.where(same & (first < second), 1.0, 0.0), axis=0, keepdims=True)
    key_col = (2.0 * owner_col + rank_col).astype(I32)
    key_row = (2.0 * owner_row + rank_row).astype(I32)
    key_col = jnp.where(iota((CAP, 1), 0) < count, key_col, -1)
    key_row = jnp.where(iota((1, CAP), 1) < count, key_row, -1)
    return key_col, key_row


def split3(value):
    high = value.astype(BF16).astype(F32)
    middle = (value - high).astype(BF16).astype(F32)
    low = value - high - middle
    return high, middle, low


def repeat_rows(value, count):
    rows, lanes = value.shape
    return jnp.broadcast_to(value[:, None, :], (rows, count, lanes)).reshape(rows * count, lanes)


def first_weights(in_weight, in_bias, z_halo):
    lane = iota((HID, 96), 1)
    base = jnp.zeros((HID, 96), F32)
    for c in range(CIN):
        base = jnp.where((lane >> 4) == c, 0.5 * row_to_col(in_weight[c : c + 1, :]), base)
    for number, part in enumerate(split3(0.5 * row_to_col(in_bias))):
        for mask in range(3):
            base = jnp.where(lane == 80 + 3 * mask + number, part, base)
    base = repeat_rows(base, 16)
    lane = iota((16 * HID, 96), 1)
    cell = iota((16 * HID, 96), 0) & 15
    first = 83 + 3 * ((cell >> 1) & 1) if z_halo else 80
    own = jnp.where(lane < 80, cell, -1) == (lane & 15)
    keep = own | ((lane >= first) & (lane < first + 3))
    return jnp.where(keep, base, 0.0).astype(BF16)


def over_cells(weight):
    rows, depth = weight.shape
    widen = one_hot(iota((depth, 8 * depth), 0) == (iota((depth, 8 * depth), 1) >> 3))
    wide = repeat_rows(dot(weight, widen), 8)
    keep = (iota(wide.shape, 0) & 7) == (iota(wide.shape, 1) & 7)
    return jnp.where(keep, wide, 0.0).astype(BF16)


def tap_places(x, pair):
    lane = iota((1, 2048), 1)
    z = lane >> 8
    side = (lane >> 7) & 1
    row = lane & 127
    regular = row < 96
    inner = row < 112
    near = (row >> 1) & 3
    far = 5 * ((row >> 1) & 1)
    in_x = jnp.where(regular, row >> 4, jnp.where(inner, 1 + near, far))
    in_y = jnp.where(regular, (row >> 3) & 1, row & 1)
    above = jnp.where(inner, row & 8, 2 * (row & 4))
    in_z = jnp.where(regular, row & 7, above + (above >> 3) - 1)
    a = in_x - x
    b = 2 * side + in_y - pair
    c = in_z - z + 1
    valid = (a >= 0) & (a <= 2) & (b >= 0) & (b <= 2) & (c >= 0) & (c <= 2)
    valid = valid & (row < 120)
    tap = jnp.where(valid, 9 * a + 3 * b + c, -1)
    return one_hot(iota((32, 2048), 0) == tap)


def closure_body(
    counts_in, owner_in, fields_in, in_weight_in, in_bias_in, depth_weight_in, depth_bias_in,
    mix_weight_in, mix_bias_in, out_weight_in, out_bias_in,
    out_ref,
    counts_ref, owner_ref, fields_ref, in_weight_ref, in_bias_ref, depth_weight_ref, depth_bias_ref,
    mix_weight_ref, mix_bias_ref, out_weight_ref, out_bias_ref, mix_w, out_w, out_bias,
    spread, outgoing, incoming, grid_in, ones_mask, hidden, band, tap_w, depth_bias, mix_bias, depth, result, scatter,
    place_slots, x_send, x_recv, y_send, y_recv, c_send, c_recv, leaving, arrived,
    fetch_sem, send_sem, recv_sem, halo_send, halo_recv, back_send, back_recv,
):
    fetches = [
        pltpu.make_async_copy(source, target, fetch_sem.at[number])
        for number, (source, target) in enumerate((
            (counts_in, counts_ref), (owner_in, owner_ref), (fields_in, fields_ref),
            (in_weight_in, in_weight_ref), (in_bias_in, in_bias_ref),
            (depth_weight_in, depth_weight_ref), (depth_bias_in, depth_bias_ref),
            (mix_weight_in, mix_weight_ref), (mix_bias_in, mix_bias_ref),
            (out_weight_in, out_weight_ref), (out_bias_in, out_bias_ref),
        ))
    ]
    for fetch in fetches:
        fetch.start()
    gx = lax.axis_index("gx")
    yz = lax.axis_index("yz")
    me = gx * N_YZ + yz
    at_x = [lax.rem(gx + step, 4) for step in range(4)]
    at_y = [8 * lax.rem(lax.div(yz, 8) + step, 4) for step in range(4)]
    at_z = [2 * lax.rem(lax.div(yz, 2) + step, 4) for step in range(4)]
    at_core = [lax.rem(yz + step, 2) for step in range(2)]

    def coords(step):
        where = (at_x[step[0]], at_y[step[1]] + at_z[step[2]] + at_core[step[3]])
        return where[0] * N_YZ + where[1], where

    barrier = pltpu.get_barrier_semaphore()
    for step in STEPS:
        pl.semaphore_signal(barrier, inc=1, device_id=coords(step)[1], device_id_type=MESH)

    for fetch in fetches[:3]:
        fetch.wait()
    counts = counts_ref[...].astype(F32)
    owner = owner_ref[...]
    key_col, key_row = slot_keys(me, counts, owner)
    select = one_hot(iota((SLOTS, CAP), 0) == key_row)
    for c in range(CIN):
        rows = dot(select, fields_ref[c])
        for part in range(4):
            spread[c, pl.ds(part, SLOTS, stride=4), :] = rows[:, part * LANES : (part + 1) * LANES]
    for c in range(CIN):
        outgoing[:, :, c * LANES : (c + 1) * LANES] = (
            spread[c].reshape(NDEV, 8, LANES).astype(BF16)
        )

    pl.semaphore_wait(barrier, NDEV - 1)

    for step in STEPS:
        other, where = coords(step)
        pltpu.make_async_remote_copy(
            src_ref=outgoing.at[other], dst_ref=incoming.at[me],
            send_sem=send_sem, recv_sem=recv_sem, device_id=where, device_id_type=MESH,
        ).start()
    incoming[me] = outgoing[me]

    cum_col = run_cumulative(me, counts, owner)
    brick_col, brick_row = brick_keys(cum_col)
    gather = one_hot(iota((2 * LANES, ROWS), 1) == brick_col)
    scatter[...] = one_hot(iota((2 * SLOTS, LANES), 0) == brick_row)
    for half in range(2):
        wanted = jnp.where(key_col < 0, -1, 2 * key_col + half)
        place_slots[half * CAP : (half + 1) * CAP, :] = one_hot(
            iota((CAP, 2 * SLOTS), 1) == wanted
        )
    lane = iota((1, LANES), 1)
    high_x = ((lane >> 6) & 1) == 1
    along_y = (lane >> 4) & 3
    along_z = lane & 15
    keep_low = jnp.where(gx > 0, 1.0, 0.0).astype(F32)
    keep_high = jnp.where(gx < N_GX - 1, 1.0, 0.0).astype(F32)
    masks = [jnp.ones((1, LANES), F32)] * 6
    masks[0] = jnp.where(high_x, 1.0, keep_low)
    masks[5] = jnp.where(high_x, keep_high, 1.0)
    for x in range(6):
        ones_mask[x] = jnp.broadcast_to(masks[x], (16, LANES))
    line = iota((16, LANES), 0)
    ones_mask[6] = jnp.where(line < 3, 1.0, jnp.where(line < 6, masks[0], masks[5]))
    for fetch in fetches[3:]:
        fetch.wait()
    in_weight = in_weight_ref[...].astype(F32)
    first_w = [first_weights(in_weight, in_bias_ref[...], z_halo) for z_halo in (False, True)]
    mix_w[...] = over_cells((0.5 * mix_weight_ref[...].astype(F32)).astype(BF16))
    out_w[...] = over_cells(out_weight_ref[...])
    depth_bias[...] = repeat_rows(
        jnp.broadcast_to(row_to_col(depth_bias_ref[...]), (HID, LANES)), 8
    )
    mix_bias[...] = repeat_rows(
        jnp.broadcast_to(0.5 * row_to_col(mix_bias_ref[...]), (HID, LANES)), 8
    )
    out_bias[...] = repeat_rows(jnp.broadcast_to(row_to_col(out_bias_ref[...]), (COUT, LANES)), 8)
    taps = jnp.concatenate([depth_weight_ref[...], jnp.zeros((HID, 5), F32)], axis=1)
    high = taps.astype(BF16)
    taps = jnp.concatenate([high, (taps - high.astype(F32)).astype(BF16)], axis=0)

    def band_rows(group, carry):
        rows = dot(taps, tap_places(lax.div(group, 2), lax.rem(group, 2)))
        for z in range(8):
            start = pl.multiple_of((group * 8 + z) * 2 * HID, 2 * HID)
            for side in range(2):
                first = z * 256 + side * LANES
                band[side, pl.ds(start, 2 * HID), :] = rows[:, first : first + LANES]
        return carry

    lax.fori_loop(0, 8, band_rows, 0)

    def band_channel(h, carry):
        row = 0
        for planes in ((1, 2), (0, 3)):
            for part in range(2):
                for x in planes:
                    for side in range(2):
                        rows = band[side, pl.ds(x * 32 * HID + part * HID + h, 16, stride=2 * HID), :]
                        tap_w[h, row : row + 16, side * LANES : (side + 1) * LANES] = rows.astype(BF16)
                    row += 16
        return carry

    lax.fori_loop(0, HID, band_channel, 0)
    grid_in[...] = jnp.zeros_like(grid_in)
    for pair in range(5):
        for tile in (0, 5, 7):
            first = pair * 128 + tile * 16
            hidden[:, first : first + 16, :] = jnp.zeros((HID, 16, LANES), BF16)

    every = pltpu.make_async_copy(
        outgoing.at[pl.ds(0, NDEV - 1)], incoming.at[pl.ds(0, NDEV - 1)], recv_sem
    )
    every.wait()

    def place(x, y):
        return (y // 2) * 128 + x * 16 + (y % 2) * 8

    def get(c, x, y):
        return grid_in[c, place(x, y) : place(x, y) + 8, :]

    def put(c, x, y, value):
        grid_in[c, place(x, y) : place(x, y) + 8, :] = value

    bricks = dot(gather, incoming[...].reshape(ROWS, CIN * LANES))
    for c in range(CIN):
        for m in range(2):
            turned = bricks[m * LANES : (m + 1) * LANES, c * LANES : (c + 1) * LANES].T
            for p in range(2):
                for y in range(8):
                    first = p * 64 + y * 8
                    put(c, 1 + 2 * m + p, 1 + y, turned[first : first + 8])

    for c in range(CIN):
        for side, x in enumerate((4, 1)):
            cells = jnp.concatenate([get(c, x, y) for y in range(1, 9)], axis=0)
            x_send[side, c] = pltpu.roll(cells, 64, 1).astype(BF16)
        last_y = [get(c, x, 8) for x in range(1, 5)]
        first_y = [get(c, x, 1) for x in range(1, 5)]
        y_send[0, c] = pltpu.roll(jnp.concatenate(last_y, axis=0), 80, 1).astype(BF16)
        y_send[1, c] = pltpu.roll(jnp.concatenate(first_y, axis=0), 48, 1).astype(BF16)
        c_send[0, c] = pltpu.roll(last_y[3], 16, 1).astype(BF16)
        c_send[1, c] = pltpu.roll(first_y[3], 112, 1).astype(BF16)
        c_send[2, c] = pltpu.roll(last_y[0], 16, 1).astype(BF16)
        c_send[3, c] = pltpu.roll(first_y[0], 112, 1).astype(BF16)
    up_x = lax.rem(gx + 1, N_GX)
    down_x = lax.rem(gx + N_GX - 1, N_GX)
    up_y = lax.rem(yz + 1, N_YZ)
    down_y = lax.rem(yz + N_YZ - 1, N_YZ)
    halo = []
    for source, target, where in (
        (x_send.at[0], x_recv.at[0], (up_x, yz)),
        (x_send.at[1], x_recv.at[1], (down_x, yz)),
        (y_send.at[0], y_recv.at[0], (gx, up_y)),
        (y_send.at[1], y_recv.at[1], (gx, down_y)),
        (c_send.at[0], c_recv.at[0], (up_x, up_y)),
        (c_send.at[1], c_recv.at[1], (up_x, down_y)),
        (c_send.at[2], c_recv.at[2], (down_x, up_y)),
        (c_send.at[3], c_recv.at[3], (down_x, down_y)),
    ):
        number = len(halo)
        copy = pltpu.make_async_remote_copy(
            src_ref=source, dst_ref=target, send_sem=halo_send.at[number],
            recv_sem=halo_recv.at[number], device_id=where, device_id_type=MESH,
        )
        copy.start()
        halo.append(copy)
    def first_group(pair, tile):
        start = pl.multiple_of(pair * 128 + tile * 16, 16)
        cells = [grid_in[c, pl.ds(start, 16), :] for c in range(CIN)]
        stacked = jnp.concatenate(cells + [ones_mask[{6: 1, 7: 6}.get(tile, tile)]], axis=0).astype(BF16)
        value = gelu_half(dot(first_w[tile == 7], stacked)).astype(BF16)
        for h in range(HID):
            hidden[h, pl.ds(start, 16), :] = value[16 * h : 16 * h + 16]

    def first_pairs(pairs, tiles):
        def pair_tiles(number, carry):
            for tile in tiles:
                first_group(pairs[0] + (pairs[1] - pairs[0]) * number, tile)
            return carry

        lax.fori_loop(0, len(pairs), pair_tiles, 0)

    def z_rows(c, source, count, target):
        for side in range(2):
            rows = grid_in[c, pl.ds(source + 7 * (1 - side), count, stride=8), :]
            edge_lane = along_z == 15 * side
            wrapped = pltpu.roll(rows, 15 if side else 113, 1)
            moved = pltpu.roll(rows, 127 if side else 1, 1)
            first = target + (8 if count == 8 else 4) * side
            grid_in[c, first : first + count, :] = jnp.where(edge_lane, wrapped, moved)

    def z_halo(pairs):
        for c in range(CIN):
            for pair in pairs:
                z_rows(c, pair * 128 + 16, 8, pair * 128 + 96)

    def z_halo_edge(pairs):
        for c in range(CIN):
            for pair in pairs:
                z_rows(c, pair * 128, 2, pair * 128 + 112)
                z_rows(c, pair * 128 + 80, 2, pair * 128 + 114)

    def finish(chunk, planes, pairs):
        tap_rows = slice(64 * (planes[0] == 0), 64 * (planes[0] == 0) + 64)

        def depth_part(group, carry):
            for half in range(2):
                parts = []
                for number in range(2):
                    h = 4 * group + 2 * half + number
                    cells = [hidden[h, 128 * pair : 128 * pair + 256, :] for pair in pairs]
                    both = dot(tap_w[h, tap_rows, :], jnp.concatenate(cells, axis=1))
                    parts.append(both[:32] + both[32:])
                start = pl.multiple_of(32 * group + 16 * half, 16)
                bias = depth_bias[pl.ds(start, 16), :]
                for x in range(2):
                    for y in range(4):
                        first = 16 * x + 8 * (y % 2)
                        lanes = slice((y // 2) * LANES, (y // 2 + 1) * LANES)
                        both = jnp.concatenate(
                            [part[first : first + 8, lanes] for part in parts], axis=0
                        )
                        depth[4 * x + y, pl.ds(start, 16), :] = (both + bias).astype(BF16)
            return carry

        lax.fori_loop(0, 8, depth_part, 0)

        def mix_part(group, carry):
            for number in range(2):
                row = 4 * group + 2 * number
                cells = jnp.concatenate([depth[row], depth[row + 1]], axis=1)
                bias = jnp.concatenate([mix_bias[...]] * 2, axis=1)
                mixed = gelu_half(dot(mix_w[...], cells) + bias).astype(BF16)
                field = dot(out_w[...], mixed)
                for side in range(2):
                    part = field[:, side * LANES : (side + 1) * LANES] + out_bias[...]
                    for f in range(COUT):
                        start = pl.multiple_of(f * 64 + 8 * (row + side), 8)
                        result[pl.ds(start, 8), :] = part[8 * f : 8 * f + 8]
            return carry

        lax.fori_loop(0, 2, mix_part, 0)

        turned = []
        for pair in range(3):
            blocks = [None] * 16
            for x, plane in enumerate(planes):
                for y in range(4):
                    to = 8 * (plane % 2) + 2 * pairs[y // 2] + y % 2
                    for f in range(2):
                        start = (2 * pair + f) * 64 + x * 32 + y * 8
                        blocks[(to + 4 * f) % 16] = result[start : start + 8, :]
            turned.append(jnp.concatenate(blocks, axis=0).T.astype(BF16))
        packed = jnp.concatenate(turned, axis=1)
        leaving[chunk] = dot(scatter[...], packed).reshape(NDEV, 4, 3 * LANES).astype(BF16)
        for step in STEPS:
            other, where = coords(step)
            pltpu.make_async_remote_copy(
                src_ref=leaving.at[chunk, other], dst_ref=arrived.at[chunk, me],
                send_sem=back_send, recv_sem=back_recv.at[chunk], device_id=where,
                device_id_type=MESH,
            ).start()
        arrived[chunk, me] = leaving[chunk, me]

    z_halo((1, 2, 3))
    first_pairs((1, 2, 3), (1, 2, 3, 4, 6))
    finish(0, (1, 2), (1, 2))

    for copy in halo:
        copy.wait()

    def y_rows(c, x, side, far):
        near = pltpu.roll(get(c, x, 8 if side == 0 else 1), 16 if side == 0 else 112, 1)
        put(c, x, 9 * side, jnp.where(along_y == 3 * side, far, near))

    for c in range(CIN):
        for side in range(2):
            own = y_recv[side, c].astype(F32)
            for x in range(1, 5):
                y_rows(c, x, side, own[8 * (x - 1) : 8 * x])
    z_halo((0, 4))
    first_pairs((0, 4), (1, 2, 3, 4, 6))
    finish(1, (1, 2), (0, 3))

    for c in range(CIN):
        low = jnp.where(high_x, x_send[0, c].astype(F32), keep_low * x_recv[0, c].astype(F32))
        high = jnp.where(high_x, keep_high * x_recv[1, c].astype(F32), x_send[1, c].astype(F32))
        for y in range(8):
            put(c, 0, 1 + y, low[8 * y : 8 * y + 8])
            put(c, 5, 1 + y, high[8 * y : 8 * y + 8])
        for side in range(2):
            own = y_recv[side, c].astype(F32)
            corner_low = keep_low * c_recv[0 + side, c].astype(F32)
            corner_high = keep_high * c_recv[2 + side, c].astype(F32)
            y_rows(c, 0, side, jnp.where(high_x, pltpu.roll(own[24:32], 64, 1), corner_low))
            y_rows(c, 5, side, jnp.where(high_x, corner_high, pltpu.roll(own[0:8], 64, 1)))
    z_halo_edge(range(5))
    first_pairs((1, 2, 3), (0, 5, 7))
    finish(2, (0, 3), (1, 2))
    first_pairs((0, 4), (0, 5, 7))
    finish(3, (0, 3), (0, 3))

    low_half = iota((1, LANES), 1) < 64
    inner_y = ((iota((1, LANES), 1) + 16) & 63) >= 32
    taken = []
    sides = []
    for chunk in range(4):
        pltpu.make_async_copy(
            leaving.at[chunk, pl.ds(0, NDEV - 1)], arrived.at[chunk, pl.ds(0, NDEV - 1)],
            back_recv.at[chunk],
        ).wait()
        taken.append(dot(place_slots[...], arrived[chunk].reshape(2 * SLOTS, 3 * LANES)))
        if chunk % 2 == 0:
            continue
        inner, outer = taken[chunk - 1], taken[chunk]
        fields = []
        for pair in range(3):
            lanes = slice(pair * LANES, (pair + 1) * LANES)
            fields.append(jnp.where(inner_y, inner[:, lanes], outer[:, lanes]))
            fields.append(pltpu.roll(jnp.where(inner_y, outer[:, lanes], inner[:, lanes]), 96, 1))
        sides.append(fields)
    for half in range(2):
        rows = slice(half * CAP, (half + 1) * CAP)
        for f in range(COUT):
            middle, ends = sides[0][f][rows], sides[1][f][rows]
            lanes = slice(2 * half * LANES, (2 * half + 1) * LANES)
            out_ref[f, :, lanes] = jnp.where(low_half, ends, middle).astype(BF16)
            lanes = slice((2 * half + 1) * LANES, (2 * half + 2) * LANES)
            out_ref[f, :, lanes] = jnp.where(low_half, middle, ends).astype(BF16)
    pltpu.make_async_copy(
        outgoing.at[pl.ds(0, NDEV - 1)], incoming.at[pl.ds(0, NDEV - 1)], send_sem
    ).wait()
    pltpu.make_async_copy(
        leaving.at[:, pl.ds(0, NDEV - 1)], arrived.at[:, pl.ds(0, NDEV - 1)], back_send
    ).wait()


VMEM = pl.BlockSpec(memory_space=pltpu.VMEM)
HBM = pl.BlockSpec(memory_space=pltpu.HBM)


def shards(
    fields, solver_counts, cnn_owner, in_weight, in_bias, depth_weight, depth_bias,
    mix_weight, mix_bias, out_weight, out_bias,
):
    closure = pl.pallas_call(
        closure_body,
        out_shape=jax.ShapeDtypeStruct((COUT, CAP, 4 * LANES), BF16),
        in_specs=[HBM] * 11,
        out_specs=VMEM,
        scratch_shapes=[
            pltpu.VMEM((1, NDEV), I32),
            pltpu.VMEM((64, LANES), I32),
            pltpu.VMEM((CIN, CAP, 4 * LANES), BF16),
            pltpu.VMEM((CIN, HID), BF16),
            pltpu.VMEM((1, HID), F32),
            pltpu.VMEM((HID, 27), F32),
            pltpu.VMEM((1, HID), F32),
            pltpu.VMEM((HID, HID), BF16),
            pltpu.VMEM((1, HID), F32),
            pltpu.VMEM((COUT, HID), BF16),
            pltpu.VMEM((1, COUT), F32),
            pltpu.VMEM((8 * HID, 8 * HID), BF16),
            pltpu.VMEM((8 * COUT, 8 * HID), BF16),
            pltpu.VMEM((8 * COUT, LANES), F32),
            pltpu.VMEM((CIN, ROWS, LANES), F32),
            pltpu.VMEM((NDEV, 8, CIN * LANES), BF16),
            pltpu.VMEM((NDEV, 8, CIN * LANES), BF16),
            pltpu.VMEM((CIN, 640, LANES), F32),
            pltpu.VMEM((7, 16, LANES), F32),
            pltpu.VMEM((HID, 640, LANES), BF16),
            pltpu.VMEM((2, 128 * HID, LANES), F32),
            pltpu.VMEM((HID, 128, 2 * LANES), BF16),
            pltpu.VMEM((8 * HID, LANES), F32),
            pltpu.VMEM((8 * HID, LANES), F32),
            pltpu.VMEM((8, 8 * HID, LANES), BF16),
            pltpu.VMEM((64 * COUT, LANES), F32),
            pltpu.VMEM((2 * SLOTS, LANES), BF16),
            pltpu.VMEM((2 * CAP, 2 * SLOTS), BF16),
            pltpu.VMEM((2, CIN, 64, LANES), BF16),
            pltpu.VMEM((2, CIN, 64, LANES), BF16),
            pltpu.VMEM((2, CIN, 32, LANES), BF16),
            pltpu.VMEM((2, CIN, 32, LANES), BF16),
            pltpu.VMEM((4, CIN, 8, LANES), BF16),
            pltpu.VMEM((4, CIN, 8, LANES), BF16),
            pltpu.VMEM((4, NDEV, 4, 3 * LANES), BF16),
            pltpu.VMEM((4, NDEV, 4, 3 * LANES), BF16),
            pltpu.SemaphoreType.DMA((11,)),
            pltpu.SemaphoreType.DMA,
            pltpu.SemaphoreType.DMA,
            pltpu.SemaphoreType.DMA((8,)),
            pltpu.SemaphoreType.DMA((8,)),
            pltpu.SemaphoreType.DMA,
            pltpu.SemaphoreType.DMA((4,)),
        ],
        compiler_params=pltpu.CompilerParams(
            collective_id=0, has_side_effects=True, vmem_limit_bytes=36 * 1024 * 1024
        ),
        name="closure",
    )(*(
        pltpu.with_memory_space_constraint(operand, pltpu.HBM)
        for operand in (
            solver_counts.reshape(1, NDEV),
            cnn_owner.reshape(64, LANES),
            jnp.transpose(fields, (1, 0, 2)),
            jnp.transpose(in_weight),
            in_bias.reshape(1, HID),
            depth_weight,
            depth_bias.reshape(1, HID),
            mix_weight,
            mix_bias.reshape(1, HID),
            out_weight,
            out_bias.reshape(1, COUT),
        )
    ))
    return jnp.transpose(closure, (1, 0, 2))


def solution(mesh):
    return jax.shard_map(
        shards,
        mesh=mesh,
        in_specs=(P(("gx", "yz"), None, None), P(), P(), P(), P(), P(), P(), P(), P(), P(), P()),
        out_specs=P(("gx", "yz"), None, None),
        check_vma=False,
    )
```

```python
import jax
import jax.numpy as jnp
from jax import lax
from jax.experimental import pallas as pl
from jax.experimental.pallas import tpu as pltpu
from jax.sharding import PartitionSpec as P

MESH = pl.DeviceIdType.MESH
NDEV = 128
N_GX = 4
N_YZ = 32
CAP = 192
CIN = 5
HID = 32
COUT = 6
LANES = 128
SLOTS = 2 * NDEV
F32 = jnp.float32
BF16 = jnp.bfloat16
I32 = jnp.int32
GELU_A = 2.0 * 0.7978845608028654
GELU_B = 8.0 * 0.7978845608028654 * 0.044715


STEPS = sorted(
    [(x, y, z, c) for x in range(4) for y in range(4) for z in range(4) for c in range(2)],
    key=lambda step: -sum(min(part, 4 - part) for part in step[:3]),
)[:-2] + [(0, 0, 0, 1)]


def iota(shape, dim):
    return lax.broadcasted_iota(I32, shape, dim)


def dot(a, b):
    return jnp.dot(a, b, preferred_element_type=F32)


def one_hot(condition):
    return jnp.where(condition, 1.0, 0.0).astype(BF16)


def row_to_col(row):
    count = row.shape[1]
    same = iota((count, count), 0) == iota((count, count), 1)
    return jnp.sum(jnp.where(same, row, 0.0), axis=1, keepdims=True)


def col_to_row(col):
    count = col.shape[0]
    same = iota((count, count), 0) == iota((count, count), 1)
    return jnp.sum(jnp.where(same, col, 0.0), axis=0, keepdims=True)


def gelu_half(y):
    return y + y * jnp.tanh(y * (GELU_A + GELU_B * (y * y)))


def run_cumulative(me, counts, owner):
    lower = iota((NDEV, NDEV), 1) <= iota((NDEV, NDEV), 0)
    run_end = jnp.sum(jnp.where(lower, counts, 0.0), axis=1, keepdims=True).astype(I32)
    mine = one_hot(owner == me)
    rows = iota((NDEV, 64), 1)
    whole = dot(one_hot(rows < (run_end >> 7)), mine)
    part = dot(one_hot(rows == (run_end >> 7)), mine)
    inside = iota((NDEV, LANES), 1) < (run_end & 127)
    return jnp.sum(whole + jnp.where(inside, part, 0.0), axis=1, keepdims=True)


def brick_keys(cum_col):
    cum_row = col_to_row(cum_col)
    below = cum_row <= (iota((LANES, NDEV), 0) & 63).astype(F32)
    source = jnp.sum(jnp.where(below, 1.0, 0.0), axis=1, keepdims=True)
    before = jnp.max(jnp.where(below, cum_row, 0.0), axis=1, keepdims=True)
    row = iota((LANES, 1), 0)
    place = 2.0 * source + ((row & 63).astype(F32) - before)
    key_col = 2 * place.astype(I32) + (row >> 6)
    below = cum_col <= (iota((NDEV, LANES), 1) & 63).astype(F32)
    source = jnp.sum(jnp.where(below, 1.0, 0.0), axis=0, keepdims=True)
    before = jnp.max(jnp.where(below, cum_col, 0.0), axis=0, keepdims=True)
    lane = iota((1, LANES), 1)
    place = 2.0 * source + ((lane & 63).astype(F32) - before)
    key_row = 2 * place.astype(I32) + (lane >> 6)
    return key_col, key_row


def slot_keys(me, counts, owner):
    lane = iota((1, NDEV), 1)
    start = jnp.sum(jnp.where(lane < me, counts, 0.0), axis=1, keepdims=True).astype(I32)
    count = jnp.sum(jnp.where(lane == me, counts, 0.0), axis=1, keepdims=True).astype(I32)
    position = iota((CAP, 1), 0) + start
    rows = dot(one_hot(iota((CAP, 64), 1) == (position >> 7)), owner.astype(F32).astype(BF16))
    here = iota((CAP, LANES), 1) == (position & 127)
    owner_col = jnp.sum(jnp.where(here, rows, 0.0), axis=1, keepdims=True)
    owner_row = col_to_row(owner_col)
    same = owner_col == owner_row
    first = iota((CAP, CAP), 0)
    second = iota((CAP, CAP), 1)
    rank_col = jnp.sum(jnp.where(same & (second < first), 1.0, 0.0), axis=1, keepdims=True)
    rank_row = jnp.sum(jnp.where(same & (first < second), 1.0, 0.0), axis=0, keepdims=True)
    key_col = (2.0 * owner_col + rank_col).astype(I32)
    key_row = (2.0 * owner_row + rank_row).astype(I32)
    key_col = jnp.where(iota((CAP, 1), 0) < count, key_col, -1)
    key_row = jnp.where(iota((1, CAP), 1) < count, key_row, -1)
    return key_col, key_row


def split3(value):
    high = value.astype(BF16).astype(F32)
    middle = (value - high).astype(BF16).astype(F32)
    low = value - high - middle
    return high, middle, low


def repeat_rows(value, count):
    rows, lanes = value.shape
    return jnp.broadcast_to(value[:, None, :], (rows, count, lanes)).reshape(rows * count, lanes)


def first_weights(in_weight, in_bias, z_halo):
    lane = iota((HID, 96), 1)
    base = jnp.zeros((HID, 96), F32)
    for c in range(CIN):
        base = jnp.where((lane >> 4) == c, 0.5 * row_to_col(in_weight[c : c + 1, :]), base)
    for number, part in enumerate(split3(0.5 * row_to_col(in_bias))):
        for mask in range(3):
            base = jnp.where(lane == 80 + 3 * mask + number, part, base)
    base = repeat_rows(base, 16)
    lane = iota((16 * HID, 96), 1)
    cell = iota((16 * HID, 96), 0) & 15
    first = 83 + 3 * ((cell >> 1) & 1) if z_halo else 80
    own = jnp.where(lane < 80, cell, -1) == (lane & 15)
    keep = own | ((lane >= first) & (lane < first + 3))
    return jnp.where(keep, base, 0.0).astype(BF16)


def over_cells(weight):
    rows, depth = weight.shape
    widen = one_hot(iota((depth, 8 * depth), 0) == (iota((depth, 8 * depth), 1) >> 3))
    wide = repeat_rows(dot(weight, widen), 8)
    keep = (iota(wide.shape, 0) & 7) == (iota(wide.shape, 1) & 7)
    return jnp.where(keep, wide, 0.0).astype(BF16)


def tap_places(x, pair):
    lane = iota((1, 2048), 1)
    z = lane >> 8
    side = (lane >> 7) & 1
    row = lane & 127
    regular = row < 96
    inner = row < 112
    near = (row >> 1) & 3
    far = 5 * ((row >> 1) & 1)
    in_x = jnp.where(regular, row >> 4, jnp.where(inner, 1 + near, far))
    in_y = jnp.where(regular, (row >> 3) & 1, row & 1)
    above = jnp.where(inner, row & 8, 2 * (row & 4))
    in_z = jnp.where(regular, row & 7, above + (above >> 3) - 1)
    a = in_x - x
    b = 2 * side + in_y - pair
    c = in_z - z + 1
    valid = (a >= 0) & (a <= 2) & (b >= 0) & (b <= 2) & (c >= 0) & (c <= 2)
    valid = valid & (row < 120)
    tap = jnp.where(valid, 9 * a + 3 * b + c, -1)
    return one_hot(iota((32, 2048), 0) == tap)


def closure_body(
    counts_in, owner_in, fields_in, in_weight_in, in_bias_in, depth_weight_in, depth_bias_in,
    mix_weight_in, mix_bias_in, out_weight_in, out_bias_in,
    out_ref,
    counts_ref, owner_ref, fields_ref, in_weight_ref, in_bias_ref, depth_weight_ref, depth_bias_ref,
    mix_weight_ref, mix_bias_ref, out_weight_ref, out_bias_ref, mix_w, out_w, out_bias,
    spread, outgoing, incoming, grid_in, ones_mask, hidden, band, tap_w, depth_bias, mix_bias, depth, result, scatter,
    place_slots, x_send, x_recv, y_send, y_recv, c_send, c_recv, leaving, arrived,
    fetch_sem, send_sem, recv_sem, halo_send, halo_recv, back_send, back_recv,
):
    fetches = [
        pltpu.make_async_copy(source, target, fetch_sem.at[number])
        for number, (source, target) in enumerate((
            (counts_in, counts_ref), (owner_in, owner_ref), (fields_in, fields_ref),
            (in_weight_in, in_weight_ref), (in_bias_in, in_bias_ref),
            (depth_weight_in, depth_weight_ref), (depth_bias_in, depth_bias_ref),
            (mix_weight_in, mix_weight_ref), (mix_bias_in, mix_bias_ref),
            (out_weight_in, out_weight_ref), (out_bias_in, out_bias_ref),
        ))
    ]
    for fetch in fetches:
        fetch.start()
    gx = lax.axis_index("gx")
    yz = lax.axis_index("yz")
    me = gx * N_YZ + yz
    at_x = [lax.rem(gx + step, 4) for step in range(4)]
    at_y = [8 * lax.rem(lax.div(yz, 8) + step, 4) for step in range(4)]
    at_z = [2 * lax.rem(lax.div(yz, 2) + step, 4) for step in range(4)]
    at_core = [lax.rem(yz + step, 2) for step in range(2)]

    def coords(step):
        where = (at_x[step[0]], at_y[step[1]] + at_z[step[2]] + at_core[step[3]])
        return where[0] * N_YZ + where[1], where

    barrier = pltpu.get_barrier_semaphore()
    for step in STEPS:
        pl.semaphore_signal(barrier, inc=1, device_id=coords(step)[1], device_id_type=MESH)

    for fetch in fetches[:3]:
        fetch.wait()
    counts = counts_ref[...].astype(F32)
    owner = owner_ref[...]
    key_col, key_row = slot_keys(me, counts, owner)
    select = one_hot(iota((SLOTS, CAP), 0) == key_row)
    for c in range(CIN):
        rows = dot(select, fields_ref[c])
        for part in range(4):
            spread[c, part % 2, pl.ds(part // 2, SLOTS, stride=2), :] = (
                rows[:, part * LANES : (part + 1) * LANES]
            )
    for c in range(CIN):
        for m in range(2):
            outgoing[m, :, :, c * LANES : (c + 1) * LANES] = (
                spread[c, m].reshape(NDEV, 4, LANES).astype(BF16)
            )

    pl.semaphore_wait(barrier, NDEV - 1)

    for m in range(2):
        for step in STEPS:
            other, where = coords(step)
            pltpu.make_async_remote_copy(
                src_ref=outgoing.at[m, other], dst_ref=incoming.at[m, me],
                send_sem=send_sem, recv_sem=recv_sem.at[m], device_id=where, device_id_type=MESH,
            ).start()
        incoming[m, me] = outgoing[m, me]

    cum_col = run_cumulative(me, counts, owner)
    brick_col, brick_row = brick_keys(cum_col)
    gather = one_hot(iota((LANES, 2 * SLOTS), 1) == brick_col)
    scatter[...] = one_hot(iota((2 * SLOTS, LANES), 0) == brick_row)
    for half in range(2):
        wanted = jnp.where(key_col < 0, -1, 2 * key_col + half)
        place_slots[half * CAP : (half + 1) * CAP, :] = one_hot(
            iota((CAP, 2 * SLOTS), 1) == wanted
        )
    lane = iota((1, LANES), 1)
    high_x = ((lane >> 6) & 1) == 1
    along_y = (lane >> 4) & 3
    along_z = lane & 15
    keep_low = jnp.where(gx > 0, 1.0, 0.0).astype(F32)
    keep_high = jnp.where(gx < N_GX - 1, 1.0, 0.0).astype(F32)
    masks = [jnp.ones((1, LANES), F32)] * 6
    masks[0] = jnp.where(high_x, 1.0, keep_low)
    masks[5] = jnp.where(high_x, keep_high, 1.0)
    for x in range(6):
        ones_mask[x] = jnp.broadcast_to(masks[x], (16, LANES))
    line = iota((16, LANES), 0)
    ones_mask[6] = jnp.where(line < 3, 1.0, jnp.where(line < 6, masks[0], masks[5]))
    for fetch in fetches[3:]:
        fetch.wait()
    in_weight = in_weight_ref[...].astype(F32)
    first_w = [first_weights(in_weight, in_bias_ref[...], z_halo) for z_halo in (False, True)]
    mix_w[...] = over_cells((0.5 * mix_weight_ref[...].astype(F32)).astype(BF16))
    out_w[...] = over_cells(out_weight_ref[...])
    depth_bias[...] = repeat_rows(
        jnp.broadcast_to(row_to_col(depth_bias_ref[...]), (HID, LANES)), 8
    )
    mix_bias[...] = repeat_rows(
        jnp.broadcast_to(0.5 * row_to_col(mix_bias_ref[...]), (HID, LANES)), 8
    )
    out_bias[...] = repeat_rows(jnp.broadcast_to(row_to_col(out_bias_ref[...]), (COUT, LANES)), 8)
    taps = jnp.concatenate([depth_weight_ref[...], jnp.zeros((HID, 5), F32)], axis=1)
    high = taps.astype(BF16)
    taps = jnp.concatenate([high, (taps - high.astype(F32)).astype(BF16)], axis=0)

    def band_rows(group, carry):
        rows = dot(taps, tap_places(lax.div(group, 2), lax.rem(group, 2)))
        for z in range(8):
            start = pl.multiple_of((group * 8 + z) * 2 * HID, 2 * HID)
            for side in range(2):
                first = z * 256 + side * LANES
                band[side, pl.ds(start, 2 * HID), :] = rows[:, first : first + LANES]
        return carry

    lax.fori_loop(0, 8, band_rows, 0)

    def band_channel(h, carry):
        row = 0
        for planes in ((1, 2), (0, 3)):
            for part in range(2):
                for x in planes:
                    for side in range(2):
                        rows = band[side, pl.ds(x * 32 * HID + part * HID + h, 16, stride=2 * HID), :]
                        tap_w[h, row : row + 16, side * LANES : (side + 1) * LANES] = rows.astype(BF16)
                    row += 16
        return carry

    lax.fori_loop(0, HID, band_channel, 0)
    grid_in[...] = jnp.zeros_like(grid_in)
    for pair in range(5):
        for tile in (0, 5, 7):
            first = pair * 128 + tile * 16
            hidden[:, first : first + 16, :] = jnp.zeros((HID, 16, LANES), BF16)

    def place(x, y):
        return (y // 2) * 128 + x * 16 + (y % 2) * 8

    def get(c, x, y):
        return grid_in[c, place(x, y) : place(x, y) + 8, :]

    def put(c, x, y, value):
        grid_in[c, place(x, y) : place(x, y) + 8, :] = value

    def first_group(pair, tile):
        start = pl.multiple_of(pair * 128 + tile * 16, 16)
        cells = [grid_in[c, pl.ds(start, 16), :] for c in range(CIN)]
        stacked = jnp.concatenate(cells + [ones_mask[{6: 1, 7: 6}.get(tile, tile)]], axis=0).astype(BF16)
        value = gelu_half(dot(first_w[tile == 7], stacked)).astype(BF16)
        for h in range(HID):
            hidden[h, pl.ds(start, 16), :] = value[16 * h : 16 * h + 16]

    def first_pairs(pairs, tiles):
        def pair_tiles(number, carry):
            for tile in tiles:
                first_group(pairs[0] + (pairs[1] - pairs[0]) * number, tile)
            return carry

        lax.fori_loop(0, len(pairs), pair_tiles, 0)

    for m in range(2):
        pltpu.make_async_copy(
            outgoing.at[m, pl.ds(0, NDEV - 1)], incoming.at[m, pl.ds(0, NDEV - 1)], recv_sem.at[m]
        ).wait()
        bricks = dot(gather, incoming[m].reshape(2 * SLOTS, CIN * LANES))
        planes = (1 + 2 * m, 2 + 2 * m)
        far_x = (1, 4)[m]
        for c in range(CIN):
            turned = bricks[:, c * LANES : (c + 1) * LANES].T
            for p in range(2):
                for y in range(8):
                    first = p * 64 + y * 8
                    put(c, planes[p], 1 + y, turned[first : first + 8])
        for c in range(CIN):
            cells = jnp.concatenate([get(c, far_x, y) for y in range(1, 9)], axis=0)
            x_send[1 - m, c] = pltpu.roll(cells, 64, 1).astype(BF16)
            rows = slice(16 * m, 16 * m + 16)
            last_y = jnp.concatenate([get(c, x, 8) for x in planes], axis=0)
            first_y = jnp.concatenate([get(c, x, 1) for x in planes], axis=0)
            y_send[0, c, rows] = pltpu.roll(last_y, 80, 1).astype(BF16)
            y_send[1, c, rows] = pltpu.roll(first_y, 48, 1).astype(BF16)
            c_send[2 - 2 * m, c] = pltpu.roll(last_y[8 * m : 8 * m + 8], 16, 1).astype(BF16)
            c_send[3 - 2 * m, c] = pltpu.roll(first_y[8 * m : 8 * m + 8], 112, 1).astype(BF16)
        if m == 0:
            first_pairs((1, 2, 3), planes)

    up_x = lax.rem(gx + 1, N_GX)
    down_x = lax.rem(gx + N_GX - 1, N_GX)
    up_y = lax.rem(yz + 1, N_YZ)
    down_y = lax.rem(yz + N_YZ - 1, N_YZ)
    halo = []
    for source, target, where in (
        (x_send.at[0], x_recv.at[0], (up_x, yz)),
        (x_send.at[1], x_recv.at[1], (down_x, yz)),
        (y_send.at[0], y_recv.at[0], (gx, up_y)),
        (y_send.at[1], y_recv.at[1], (gx, down_y)),
        (c_send.at[0], c_recv.at[0], (up_x, up_y)),
        (c_send.at[1], c_recv.at[1], (up_x, down_y)),
        (c_send.at[2], c_recv.at[2], (down_x, up_y)),
        (c_send.at[3], c_recv.at[3], (down_x, down_y)),
    ):
        number = len(halo)
        copy = pltpu.make_async_remote_copy(
            src_ref=source, dst_ref=target, send_sem=halo_send.at[number],
            recv_sem=halo_recv.at[number], device_id=where, device_id_type=MESH,
        )
        copy.start()
        halo.append(copy)
    def z_rows(c, source, count, target):
        for side in range(2):
            rows = grid_in[c, pl.ds(source + 7 * (1 - side), count, stride=8), :]
            edge_lane = along_z == 15 * side
            wrapped = pltpu.roll(rows, 15 if side else 113, 1)
            moved = pltpu.roll(rows, 127 if side else 1, 1)
            first = target + (8 if count == 8 else 4) * side
            grid_in[c, first : first + count, :] = jnp.where(edge_lane, wrapped, moved)

    def z_halo(pairs):
        for c in range(CIN):
            for pair in pairs:
                z_rows(c, pair * 128 + 16, 8, pair * 128 + 96)

    def z_halo_edge(pairs):
        for c in range(CIN):
            for pair in pairs:
                z_rows(c, pair * 128, 2, pair * 128 + 112)
                z_rows(c, pair * 128 + 80, 2, pair * 128 + 114)

    def finish(chunk, planes, pairs):
        tap_rows = slice(64 * (planes[0] == 0), 64 * (planes[0] == 0) + 64)

        def depth_part(group, carry):
            for half in range(2):
                parts = []
                for number in range(2):
                    h = 4 * group + 2 * half + number
                    cells = [hidden[h, 128 * pair : 128 * pair + 256, :] for pair in pairs]
                    both = dot(tap_w[h, tap_rows, :], jnp.concatenate(cells, axis=1))
                    parts.append(both[:32] + both[32:])
                start = pl.multiple_of(32 * group + 16 * half, 16)
                bias = depth_bias[pl.ds(start, 16), :]
                for x in range(2):
                    for y in range(4):
                        first = 16 * x + 8 * (y % 2)
                        lanes = slice((y // 2) * LANES, (y // 2 + 1) * LANES)
                        both = jnp.concatenate(
                            [part[first : first + 8, lanes] for part in parts], axis=0
                        )
                        depth[4 * x + y, pl.ds(start, 16), :] = (both + bias).astype(BF16)
            return carry

        lax.fori_loop(0, 8, depth_part, 0)

        def mix_part(group, carry):
            for number in range(2):
                row = 4 * group + 2 * number
                cells = jnp.concatenate([depth[row], depth[row + 1]], axis=1)
                bias = jnp.concatenate([mix_bias[...]] * 2, axis=1)
                mixed = gelu_half(dot(mix_w[...], cells) + bias).astype(BF16)
                field = dot(out_w[...], mixed)
                for side in range(2):
                    part = field[:, side * LANES : (side + 1) * LANES] + out_bias[...]
                    for f in range(COUT):
                        start = pl.multiple_of(f * 64 + 8 * (row + side), 8)
                        result[pl.ds(start, 8), :] = part[8 * f : 8 * f + 8]
            return carry

        lax.fori_loop(0, 2, mix_part, 0)

        turned = []
        for pair in range(3):
            blocks = [None] * 16
            for x, plane in enumerate(planes):
                for y in range(4):
                    to = 8 * (plane % 2) + 2 * pairs[y // 2] + y % 2
                    for f in range(2):
                        start = (2 * pair + f) * 64 + x * 32 + y * 8
                        blocks[(to + 4 * f) % 16] = result[start : start + 8, :]
            turned.append(jnp.concatenate(blocks, axis=0).T.astype(BF16))
        packed = jnp.concatenate(turned, axis=1)
        leaving[chunk] = dot(scatter[...], packed).reshape(NDEV, 4, 3 * LANES).astype(BF16)
        for step in STEPS:
            other, where = coords(step)
            pltpu.make_async_remote_copy(
                src_ref=leaving.at[chunk, other], dst_ref=arrived.at[chunk, me],
                send_sem=back_send, recv_sem=back_recv.at[chunk], device_id=where,
                device_id_type=MESH,
            ).start()
        arrived[chunk, me] = leaving[chunk, me]

    z_halo((1, 2, 3))
    first_pairs((1, 2, 3), (3, 4, 6))
    finish(0, (1, 2), (1, 2))

    for copy in halo:
        copy.wait()

    def y_rows(c, x, side, far):
        near = pltpu.roll(get(c, x, 8 if side == 0 else 1), 16 if side == 0 else 112, 1)
        put(c, x, 9 * side, jnp.where(along_y == 3 * side, far, near))

    for c in range(CIN):
        for side in range(2):
            own = y_recv[side, c].astype(F32)
            for x in range(1, 5):
                y_rows(c, x, side, own[8 * (x - 1) : 8 * x])
    z_halo((0, 4))
    first_pairs((0, 4), (1, 2, 3, 4, 6))
    finish(1, (1, 2), (0, 3))

    for c in range(CIN):
        low = jnp.where(high_x, x_send[0, c].astype(F32), keep_low * x_recv[0, c].astype(F32))
        high = jnp.where(high_x, keep_high * x_recv[1, c].astype(F32), x_send[1, c].astype(F32))
        for y in range(8):
            put(c, 0, 1 + y, low[8 * y : 8 * y + 8])
            put(c, 5, 1 + y, high[8 * y : 8 * y + 8])
        for side in range(2):
            own = y_recv[side, c].astype(F32)
            corner_low = keep_low * c_recv[0 + side, c].astype(F32)
            corner_high = keep_high * c_recv[2 + side, c].astype(F32)
            y_rows(c, 0, side, jnp.where(high_x, pltpu.roll(own[24:32], 64, 1), corner_low))
            y_rows(c, 5, side, jnp.where(high_x, corner_high, pltpu.roll(own[0:8], 64, 1)))
    z_halo_edge(range(5))
    first_pairs((1, 2, 3), (0, 5, 7))
    finish(2, (0, 3), (1, 2))
    first_pairs((0, 4), (0, 5, 7))
    finish(3, (0, 3), (0, 3))

    low_half = iota((1, LANES), 1) < 64
    inner_y = ((iota((1, LANES), 1) + 16) & 63) >= 32
    taken = []
    sides = []
    for chunk in range(4):
        pltpu.make_async_copy(
            leaving.at[chunk, pl.ds(0, NDEV - 1)], arrived.at[chunk, pl.ds(0, NDEV - 1)],
            back_recv.at[chunk],
        ).wait()
        taken.append(dot(place_slots[...], arrived[chunk].reshape(2 * SLOTS, 3 * LANES)))
        if chunk % 2 == 0:
            continue
        inner, outer = taken[chunk - 1], taken[chunk]
        fields = []
        for pair in range(3):
            lanes = slice(pair * LANES, (pair + 1) * LANES)
            fields.append(jnp.where(inner_y, inner[:, lanes], outer[:, lanes]))
            fields.append(pltpu.roll(jnp.where(inner_y, outer[:, lanes], inner[:, lanes]), 96, 1))
        sides.append(fields)
    for half in range(2):
        rows = slice(half * CAP, (half + 1) * CAP)
        for f in range(COUT):
            middle, ends = sides[0][f][rows], sides[1][f][rows]
            lanes = slice(2 * half * LANES, (2 * half + 1) * LANES)
            out_ref[f, :, lanes] = jnp.where(low_half, ends, middle).astype(BF16)
            lanes = slice((2 * half + 1) * LANES, (2 * half + 2) * LANES)
            out_ref[f, :, lanes] = jnp.where(low_half, middle, ends).astype(BF16)
    pltpu.make_async_copy(
        outgoing.at[:, pl.ds(0, NDEV - 1)], incoming.at[:, pl.ds(0, NDEV - 1)], send_sem
    ).wait()
    pltpu.make_async_copy(
        leaving.at[:, pl.ds(0, NDEV - 1)], arrived.at[:, pl.ds(0, NDEV - 1)], back_send
    ).wait()


VMEM = pl.BlockSpec(memory_space=pltpu.VMEM)
HBM = pl.BlockSpec(memory_space=pltpu.HBM)


def shards(
    fields, solver_counts, cnn_owner, in_weight, in_bias, depth_weight, depth_bias,
    mix_weight, mix_bias, out_weight, out_bias,
):
    closure = pl.pallas_call(
        closure_body,
        out_shape=jax.ShapeDtypeStruct((COUT, CAP, 4 * LANES), BF16),
        in_specs=[HBM] * 11,
        out_specs=VMEM,
        scratch_shapes=[
            pltpu.VMEM((1, NDEV), I32),
            pltpu.VMEM((64, LANES), I32),
            pltpu.VMEM((CIN, CAP, 4 * LANES), BF16),
            pltpu.VMEM((CIN, HID), BF16),
            pltpu.VMEM((1, HID), F32),
            pltpu.VMEM((HID, 27), F32),
            pltpu.VMEM((1, HID), F32),
            pltpu.VMEM((HID, HID), BF16),
            pltpu.VMEM((1, HID), F32),
            pltpu.VMEM((COUT, HID), BF16),
            pltpu.VMEM((1, COUT), F32),
            pltpu.VMEM((8 * HID, 8 * HID), BF16),
            pltpu.VMEM((8 * COUT, 8 * HID), BF16),
            pltpu.VMEM((8 * COUT, LANES), F32),
            pltpu.VMEM((CIN, 2, 2 * SLOTS, LANES), F32),
            pltpu.VMEM((2, NDEV, 4, CIN * LANES), BF16),
            pltpu.VMEM((2, NDEV, 4, CIN * LANES), BF16),
            pltpu.VMEM((CIN, 640, LANES), F32),
            pltpu.VMEM((7, 16, LANES), F32),
            pltpu.VMEM((HID, 640, LANES), BF16),
            pltpu.VMEM((2, 128 * HID, LANES), F32),
            pltpu.VMEM((HID, 128, 2 * LANES), BF16),
            pltpu.VMEM((8 * HID, LANES), F32),
            pltpu.VMEM((8 * HID, LANES), F32),
            pltpu.VMEM((8, 8 * HID, LANES), BF16),
            pltpu.VMEM((64 * COUT, LANES), F32),
            pltpu.VMEM((2 * SLOTS, LANES), BF16),
            pltpu.VMEM((2 * CAP, 2 * SLOTS), BF16),
            pltpu.VMEM((2, CIN, 64, LANES), BF16),
            pltpu.VMEM((2, CIN, 64, LANES), BF16),
            pltpu.VMEM((2, CIN, 32, LANES), BF16),
            pltpu.VMEM((2, CIN, 32, LANES), BF16),
            pltpu.VMEM((4, CIN, 8, LANES), BF16),
            pltpu.VMEM((4, CIN, 8, LANES), BF16),
            pltpu.VMEM((4, NDEV, 4, 3 * LANES), BF16),
            pltpu.VMEM((4, NDEV, 4, 3 * LANES), BF16),
            pltpu.SemaphoreType.DMA((11,)),
            pltpu.SemaphoreType.DMA,
            pltpu.SemaphoreType.DMA((2,)),
            pltpu.SemaphoreType.DMA((8,)),
            pltpu.SemaphoreType.DMA((8,)),
            pltpu.SemaphoreType.DMA,
            pltpu.SemaphoreType.DMA((4,)),
        ],
        compiler_params=pltpu.CompilerParams(
            collective_id=0, has_side_effects=True, vmem_limit_bytes=36 * 1024 * 1024
        ),
        name="closure",
    )(*(
        pltpu.with_memory_space_constraint(operand, pltpu.HBM)
        for operand in (
            solver_counts.reshape(1, NDEV),
            cnn_owner.reshape(64, LANES),
            jnp.transpose(fields, (1, 0, 2)),
            jnp.transpose(in_weight),
            in_bias.reshape(1, HID),
            depth_weight,
            depth_bias.reshape(1, HID),
            mix_weight,
            mix_bias.reshape(1, HID),
            out_weight,
            out_bias.reshape(1, COUT),
        )
    ))
    return jnp.transpose(closure, (1, 0, 2))


def solution(mesh):
    return jax.shard_map(
        shards,
        mesh=mesh,
        in_specs=(P(("gx", "yz"), None, None), P(), P(), P(), P(), P(), P(), P(), P(), P(), P()),
        out_specs=P(("gx", "yz"), None, None),
        check_vma=False,
    )
```

```python
import jax
import jax.numpy as jnp
from jax import lax
from jax.experimental import pallas as pl
from jax.experimental.pallas import tpu as pltpu
from jax.sharding import PartitionSpec as P

MESH = pl.DeviceIdType.MESH
NDEV = 128
N_GX = 4
N_YZ = 32
CAP = 192
CIN = 5
HID = 32
COUT = 6
LANES = 128
SLOTS = 2 * NDEV
F32 = jnp.float32
BF16 = jnp.bfloat16
I32 = jnp.int32
GELU_A = 2.0 * 0.7978845608028654
GELU_B = 8.0 * 0.7978845608028654 * 0.044715


STEPS = sorted(
    [(x, y, z, c) for x in range(4) for y in range(4) for z in range(4) for c in range(2)],
    key=lambda step: -sum(min(part, 4 - part) for part in step[:3]),
)[:-2] + [(0, 0, 0, 1)]


def iota(shape, dim):
    return lax.broadcasted_iota(I32, shape, dim)


def dot(a, b):
    return jnp.dot(a, b, preferred_element_type=F32)


def one_hot(condition):
    return jnp.where(condition, 1.0, 0.0).astype(BF16)


def row_to_col(row):
    count = row.shape[1]
    same = iota((count, count), 0) == iota((count, count), 1)
    return jnp.sum(jnp.where(same, row, 0.0), axis=1, keepdims=True)


def col_to_row(col):
    count = col.shape[0]
    same = iota((count, count), 0) == iota((count, count), 1)
    return jnp.sum(jnp.where(same, col, 0.0), axis=0, keepdims=True)


def gelu_half(y):
    return y + y * jnp.tanh(y * (GELU_A + GELU_B * (y * y)))


def run_cumulative(me, counts, owner):
    lower = iota((NDEV, NDEV), 1) <= iota((NDEV, NDEV), 0)
    run_end = jnp.sum(jnp.where(lower, counts, 0.0), axis=1, keepdims=True).astype(I32)
    mine = one_hot(owner == me)
    rows = iota((NDEV, 64), 1)
    whole = dot(one_hot(rows < (run_end >> 7)), mine)
    part = dot(one_hot(rows == (run_end >> 7)), mine)
    inside = iota((NDEV, LANES), 1) < (run_end & 127)
    return jnp.sum(whole + jnp.where(inside, part, 0.0), axis=1, keepdims=True)


def brick_keys(cum_col):
    cum_row = col_to_row(cum_col)
    below = cum_row <= (iota((LANES, NDEV), 0) & 63).astype(F32)
    source = jnp.sum(jnp.where(below, 1.0, 0.0), axis=1, keepdims=True)
    before = jnp.max(jnp.where(below, cum_row, 0.0), axis=1, keepdims=True)
    row = iota((LANES, 1), 0)
    place = 2.0 * source + ((row & 63).astype(F32) - before)
    key_col = 2 * place.astype(I32) + (row >> 6)
    below = cum_col <= (iota((NDEV, LANES), 1) & 63).astype(F32)
    source = jnp.sum(jnp.where(below, 1.0, 0.0), axis=0, keepdims=True)
    before = jnp.max(jnp.where(below, cum_col, 0.0), axis=0, keepdims=True)
    lane = iota((1, LANES), 1)
    place = 2.0 * source + ((lane & 63).astype(F32) - before)
    key_row = 2 * place.astype(I32) + (lane >> 6)
    return key_col, key_row


def slot_keys(me, counts, owner):
    lane = iota((1, NDEV), 1)
    start = jnp.sum(jnp.where(lane < me, counts, 0.0), axis=1, keepdims=True).astype(I32)
    count = jnp.sum(jnp.where(lane == me, counts, 0.0), axis=1, keepdims=True).astype(I32)
    position = iota((CAP, 1), 0) + start
    rows = dot(one_hot(iota((CAP, 64), 1) == (position >> 7)), owner.astype(F32).astype(BF16))
    here = iota((CAP, LANES), 1) == (position & 127)
    owner_col = jnp.sum(jnp.where(here, rows, 0.0), axis=1, keepdims=True)
    owner_row = col_to_row(owner_col)
    same = owner_col == owner_row
    first = iota((CAP, CAP), 0)
    second = iota((CAP, CAP), 1)
    rank_col = jnp.sum(jnp.where(same & (second < first), 1.0, 0.0), axis=1, keepdims=True)
    rank_row = jnp.sum(jnp.where(same & (first < second), 1.0, 0.0), axis=0, keepdims=True)
    key_col = (2.0 * owner_col + rank_col).astype(I32)
    key_row = (2.0 * owner_row + rank_row).astype(I32)
    key_col = jnp.where(iota((CAP, 1), 0) < count, key_col, -1)
    key_row = jnp.where(iota((1, CAP), 1) < count, key_row, -1)
    return key_col, key_row


def split3(value):
    high = value.astype(BF16).astype(F32)
    middle = (value - high).astype(BF16).astype(F32)
    low = value - high - middle
    return high, middle, low


def repeat_rows(value, count):
    rows, lanes = value.shape
    return jnp.broadcast_to(value[:, None, :], (rows, count, lanes)).reshape(rows * count, lanes)


def first_weights(in_weight, in_bias, z_halo):
    lane = iota((HID, 96), 1)
    base = jnp.zeros((HID, 96), F32)
    for c in range(CIN):
        base = jnp.where((lane >> 4) == c, 0.5 * row_to_col(in_weight[c : c + 1, :]), base)
    for number, part in enumerate(split3(0.5 * row_to_col(in_bias))):
        for mask in range(3):
            base = jnp.where(lane == 80 + 3 * mask + number, part, base)
    base = repeat_rows(base, 16)
    lane = iota((16 * HID, 96), 1)
    cell = iota((16 * HID, 96), 0) & 15
    first = 83 + 3 * ((cell >> 1) & 1) if z_halo else 80
    own = jnp.where(lane < 80, cell, -1) == (lane & 15)
    keep = own | ((lane >= first) & (lane < first + 3))
    return jnp.where(keep, base, 0.0).astype(BF16)


def over_cells(weight):
    rows, depth = weight.shape
    widen = one_hot(iota((depth, 8 * depth), 0) == (iota((depth, 8 * depth), 1) >> 3))
    wide = repeat_rows(dot(weight, widen), 8)
    keep = (iota(wide.shape, 0) & 7) == (iota(wide.shape, 1) & 7)
    return jnp.where(keep, wide, 0.0).astype(BF16)


def tap_places(x, pair):
    lane = iota((1, 2048), 1)
    z = lane >> 8
    side = (lane >> 7) & 1
    row = lane & 127
    regular = row < 96
    inner = row < 112
    near = (row >> 1) & 3
    far = 5 * ((row >> 1) & 1)
    in_x = jnp.where(regular, row >> 4, jnp.where(inner, 1 + near, far))
    in_y = jnp.where(regular, (row >> 3) & 1, row & 1)
    above = jnp.where(inner, row & 8, 2 * (row & 4))
    in_z = jnp.where(regular, row & 7, above + (above >> 3) - 1)
    a = in_x - x
    b = 2 * side + in_y - pair
    c = in_z - z + 1
    valid = (a >= 0) & (a <= 2) & (b >= 0) & (b <= 2) & (c >= 0) & (c <= 2)
    valid = valid & (row < 120)
    tap = jnp.where(valid, 9 * a + 3 * b + c, -1)
    return one_hot(iota((32, 2048), 0) == tap)


def closure_body(
    counts_in, owner_in, fields_in, in_weight_in, in_bias_in, depth_weight_in, depth_bias_in,
    mix_weight_in, mix_bias_in, out_weight_in, out_bias_in,
    out_ref,
    counts_ref, owner_ref, fields_ref, in_weight_ref, in_bias_ref, depth_weight_ref, depth_bias_ref,
    mix_weight_ref, mix_bias_ref, out_weight_ref, out_bias_ref, mix_w, out_w, out_bias,
    spread, outgoing, incoming, grid_in, ones_mask, hidden, band, tap_w, depth_bias, mix_bias, depth, result, scatter,
    place_slots, x_send, x_recv, y_send, y_recv, c_send, c_recv, leaving, arrived,
    fetch_sem, send_sem, recv_sem, halo_send, halo_recv, back_send, back_recv,
):
    fetches = [
        pltpu.make_async_copy(source, target, fetch_sem.at[number])
        for number, (source, target) in enumerate((
            (counts_in, counts_ref), (owner_in, owner_ref), (fields_in, fields_ref),
            (in_weight_in, in_weight_ref), (in_bias_in, in_bias_ref),
            (depth_weight_in, depth_weight_ref), (depth_bias_in, depth_bias_ref),
            (mix_weight_in, mix_weight_ref), (mix_bias_in, mix_bias_ref),
            (out_weight_in, out_weight_ref), (out_bias_in, out_bias_ref),
        ))
    ]
    for fetch in fetches:
        fetch.start()
    gx = lax.axis_index("gx")
    yz = lax.axis_index("yz")
    me = gx * N_YZ + yz
    at_x = [lax.rem(gx + step, 4) for step in range(4)]
    at_y = [8 * lax.rem(lax.div(yz, 8) + step, 4) for step in range(4)]
    at_z = [2 * lax.rem(lax.div(yz, 2) + step, 4) for step in range(4)]
    at_core = [lax.rem(yz + step, 2) for step in range(2)]

    def coords(step):
        where = (at_x[step[0]], at_y[step[1]] + at_z[step[2]] + at_core[step[3]])
        return where[0] * N_YZ + where[1], where

    barrier = pltpu.get_barrier_semaphore()
    for step in STEPS:
        pl.semaphore_signal(barrier, inc=1, device_id=coords(step)[1], device_id_type=MESH)

    for fetch in fetches[:3]:
        fetch.wait()
    counts = counts_ref[...].astype(F32)
    owner = owner_ref[...]
    key_col, key_row = slot_keys(me, counts, owner)
    select = one_hot(iota((SLOTS, CAP), 0) == key_row)
    for c in range(CIN):
        rows = dot(select, fields_ref[c])
        for part in range(4):
            spread[c, part % 2, pl.ds(part // 2, SLOTS, stride=2), :] = (
                rows[:, part * LANES : (part + 1) * LANES]
            )
    for c in range(CIN):
        for m in range(2):
            outgoing[m, :, :, c * LANES : (c + 1) * LANES] = (
                spread[c, m].reshape(NDEV, 4, LANES).astype(BF16)
            )

    pl.semaphore_wait(barrier, NDEV - 1)

    for m in range(2):
        for step in STEPS:
            other, where = coords(step)
            pltpu.make_async_remote_copy(
                src_ref=outgoing.at[m, other], dst_ref=incoming.at[m, me],
                send_sem=send_sem, recv_sem=recv_sem.at[m], device_id=where, device_id_type=MESH,
            ).start()
        incoming[m, me] = outgoing[m, me]

    cum_col = run_cumulative(me, counts, owner)
    brick_col, brick_row = brick_keys(cum_col)
    gather = one_hot(iota((LANES, 2 * SLOTS), 1) == brick_col)
    scatter[...] = one_hot(iota((2 * SLOTS, LANES), 0) == brick_row)
    for half in range(2):
        wanted = jnp.where(key_col < 0, -1, 2 * key_col + half)
        place_slots[half * CAP : (half + 1) * CAP, :] = one_hot(
            iota((CAP, 2 * SLOTS), 1) == wanted
        )
    lane = iota((1, LANES), 1)
    high_x = ((lane >> 6) & 1) == 1
    along_y = (lane >> 4) & 3
    along_z = lane & 15
    keep_low = jnp.where(gx > 0, 1.0, 0.0).astype(F32)
    keep_high = jnp.where(gx < N_GX - 1, 1.0, 0.0).astype(F32)
    masks = [jnp.ones((1, LANES), F32)] * 6
    masks[0] = jnp.where(high_x, 1.0, keep_low)
    masks[5] = jnp.where(high_x, keep_high, 1.0)
    for x in range(6):
        ones_mask[x] = jnp.broadcast_to(masks[x], (16, LANES))
    line = iota((16, LANES), 0)
    ones_mask[6] = jnp.where(line < 3, 1.0, jnp.where(line < 6, masks[0], masks[5]))
    for fetch in fetches[3:]:
        fetch.wait()
    in_weight = in_weight_ref[...].astype(F32)
    first_w = [first_weights(in_weight, in_bias_ref[...], z_halo) for z_halo in (False, True)]
    mix_w[...] = over_cells((0.5 * mix_weight_ref[...].astype(F32)).astype(BF16))
    out_w[...] = over_cells(out_weight_ref[...])
    depth_bias[...] = repeat_rows(
        jnp.broadcast_to(row_to_col(depth_bias_ref[...]), (HID, LANES)), 8
    )
    mix_bias[...] = repeat_rows(
        jnp.broadcast_to(0.5 * row_to_col(mix_bias_ref[...]), (HID, LANES)), 8
    )
    out_bias[...] = repeat_rows(jnp.broadcast_to(row_to_col(out_bias_ref[...]), (COUT, LANES)), 8)
    taps = jnp.concatenate([depth_weight_ref[...], jnp.zeros((HID, 5), F32)], axis=1)
    high = taps.astype(BF16)
    taps = jnp.concatenate([high, (taps - high.astype(F32)).astype(BF16)], axis=0)

    def band_rows(group, carry):
        rows = dot(taps, tap_places(lax.div(group, 2), lax.rem(group, 2)))
        for z in range(8):
            start = pl.multiple_of((group * 8 + z) * 2 * HID, 2 * HID)
            for side in range(2):
                first = z * 256 + side * LANES
                band[side, pl.ds(start, 2 * HID), :] = rows[:, first : first + LANES]
        return carry

    lax.fori_loop(0, 8, band_rows, 0)

    def band_channel(h, carry):
        row = 0
        for planes in ((1, 2), (0, 3)):
            for part in range(2):
                for x in planes:
                    for side in range(2):
                        rows = band[side, pl.ds(x * 32 * HID + part * HID + h, 16, stride=2 * HID), :]
                        tap_w[h, row : row + 16, side * LANES : (side + 1) * LANES] = rows.astype(BF16)
                    row += 16
        return carry

    lax.fori_loop(0, HID, band_channel, 0)
    grid_in[...] = jnp.zeros_like(grid_in)
    for pair in range(5):
        for tile in (0, 5, 7):
            first = pair * 128 + tile * 16
            hidden[:, first : first + 16, :] = jnp.zeros((HID, 16, LANES), BF16)

    def place(x, y):
        return (y // 2) * 128 + x * 16 + (y % 2) * 8

    def get(c, x, y):
        return grid_in[c, place(x, y) : place(x, y) + 8, :]

    def put(c, x, y, value):
        grid_in[c, place(x, y) : place(x, y) + 8, :] = value

    def first_group(pair, tile):
        start = pl.multiple_of(pair * 128 + tile * 16, 16)
        cells = [grid_in[c, pl.ds(start, 16), :] for c in range(CIN)]
        stacked = jnp.concatenate(cells + [ones_mask[{6: 1, 7: 6}.get(tile, tile)]], axis=0).astype(BF16)
        value = gelu_half(dot(first_w[tile == 7], stacked)).astype(BF16)
        for h in range(HID):
            hidden[h, pl.ds(start, 16), :] = value[16 * h : 16 * h + 16]

    def first_pairs(pairs, tiles):
        def pair_tiles(number, carry):
            for tile in tiles:
                first_group(pairs[0] + (pairs[1] - pairs[0]) * number, tile)
            return carry

        lax.fori_loop(0, len(pairs), pair_tiles, 0)

    for m in range(2):
        pltpu.make_async_copy(
            outgoing.at[m, pl.ds(0, NDEV - 1)], incoming.at[m, pl.ds(0, NDEV - 1)], recv_sem.at[m]
        ).wait()
        bricks = dot(gather, incoming[m].reshape(2 * SLOTS, CIN * LANES))
        planes = (1 + 2 * m, 2 + 2 * m)
        far_x = (1, 4)[m]
        for c in range(CIN):
            turned = bricks[:, c * LANES : (c + 1) * LANES].T
            for p in range(2):
                for y in range(8):
                    first = p * 64 + y * 8
                    put(c, planes[p], 1 + y, turned[first : first + 8])
        for c in range(CIN):
            cells = jnp.concatenate([get(c, far_x, y) for y in range(1, 9)], axis=0)
            x_send[1 - m, c] = pltpu.roll(cells, 64, 1).astype(BF16)
            rows = slice(16 * m, 16 * m + 16)
            last_y = jnp.concatenate([get(c, x, 8) for x in planes], axis=0)
            first_y = jnp.concatenate([get(c, x, 1) for x in planes], axis=0)
            y_send[0, c, rows] = pltpu.roll(last_y, 80, 1).astype(BF16)
            y_send[1, c, rows] = pltpu.roll(first_y, 48, 1).astype(BF16)
            c_send[2 - 2 * m, c] = pltpu.roll(last_y[8 * m : 8 * m + 8], 16, 1).astype(BF16)
            c_send[3 - 2 * m, c] = pltpu.roll(first_y[8 * m : 8 * m + 8], 112, 1).astype(BF16)
        if m == 0:
            first_pairs((1, 2, 3), planes)

    up_x = lax.rem(gx + 1, N_GX)
    down_x = lax.rem(gx + N_GX - 1, N_GX)
    up_y = lax.rem(yz + 1, N_YZ)
    down_y = lax.rem(yz + N_YZ - 1, N_YZ)
    halo = []
    for source, target, where in (
        (x_send.at[0], x_recv.at[0], (up_x, yz)),
        (x_send.at[1], x_recv.at[1], (down_x, yz)),
        (y_send.at[0], y_recv.at[0], (gx, up_y)),
        (y_send.at[1], y_recv.at[1], (gx, down_y)),
        (c_send.at[0], c_recv.at[0], (up_x, up_y)),
        (c_send.at[1], c_recv.at[1], (up_x, down_y)),
        (c_send.at[2], c_recv.at[2], (down_x, up_y)),
        (c_send.at[3], c_recv.at[3], (down_x, down_y)),
    ):
        number = len(halo)
        copy = pltpu.make_async_remote_copy(
            src_ref=source, dst_ref=target, send_sem=halo_send.at[number],
            recv_sem=halo_recv.at[number], device_id=where, device_id_type=MESH,
        )
        copy.start()
        halo.append(copy)
    def z_rows(c, source, count, target):
        for side in range(2):
            rows = grid_in[c, pl.ds(source + 7 * (1 - side), count, stride=8), :]
            edge_lane = along_z == 15 * side
            wrapped = pltpu.roll(rows, 15 if side else 113, 1)
            moved = pltpu.roll(rows, 127 if side else 1, 1)
            first = target + (8 if count == 8 else 4) * side
            grid_in[c, first : first + count, :] = jnp.where(edge_lane, wrapped, moved)

    def z_halo(pairs):
        for c in range(CIN):
            for pair in pairs:
                z_rows(c, pair * 128 + 16, 8, pair * 128 + 96)

    def z_halo_edge(pairs):
        for c in range(CIN):
            for pair in pairs:
                z_rows(c, pair * 128, 2, pair * 128 + 112)
                z_rows(c, pair * 128 + 80, 2, pair * 128 + 114)

    def finish(chunk, planes, pairs):
        tap_rows = slice(64 * (planes[0] == 0), 64 * (planes[0] == 0) + 64)

        def depth_part(group, carry):
            for half in range(4):
                parts = []
                for number in range(2):
                    h = 8 * group + 2 * half + number
                    cells = [hidden[h, 128 * pair : 128 * pair + 256, :] for pair in pairs]
                    both = dot(tap_w[h, tap_rows, :], jnp.concatenate(cells, axis=1))
                    parts.append(both[:32] + both[32:])
                start = pl.multiple_of(64 * group + 16 * half, 16)
                bias = depth_bias[pl.ds(start, 16), :]
                for x in range(2):
                    for y in range(4):
                        first = 16 * x + 8 * (y % 2)
                        lanes = slice((y // 2) * LANES, (y // 2 + 1) * LANES)
                        both = jnp.concatenate(
                            [part[first : first + 8, lanes] for part in parts], axis=0
                        )
                        depth[4 * x + y, pl.ds(start, 16), :] = (both + bias).astype(BF16)
            return carry

        lax.fori_loop(0, 4, depth_part, 0)

        for row in range(0, 8, 2):
            cells = jnp.concatenate([depth[row], depth[row + 1]], axis=1)
            bias = jnp.concatenate([mix_bias[...]] * 2, axis=1)
            mixed = gelu_half(dot(mix_w[...], cells) + bias).astype(BF16)
            field = dot(out_w[...], mixed)
            for side in range(2):
                part = field[:, side * LANES : (side + 1) * LANES] + out_bias[...]
                for f in range(COUT):
                    start = f * 64 + 8 * (row + side)
                    result[start : start + 8, :] = part[8 * f : 8 * f + 8]

        turned = []
        for pair in range(3):
            blocks = [None] * 16
            for x, plane in enumerate(planes):
                for y in range(4):
                    to = 8 * (plane % 2) + 2 * pairs[y // 2] + y % 2
                    for f in range(2):
                        start = (2 * pair + f) * 64 + x * 32 + y * 8
                        blocks[(to + 4 * f) % 16] = result[start : start + 8, :]
            turned.append(jnp.concatenate(blocks, axis=0).T.astype(BF16))
        packed = jnp.concatenate(turned, axis=1)
        leaving[chunk] = dot(scatter[...], packed).reshape(NDEV, 4, 3 * LANES).astype(BF16)
        for step in STEPS:
            other, where = coords(step)
            pltpu.make_async_remote_copy(
                src_ref=leaving.at[chunk, other], dst_ref=arrived.at[chunk, me],
                send_sem=back_send, recv_sem=back_recv.at[chunk], device_id=where,
                device_id_type=MESH,
            ).start()
        arrived[chunk, me] = leaving[chunk, me]

    z_halo((1, 2, 3))
    first_pairs((1, 2, 3), (3, 4, 6))
    finish(0, (1, 2), (1, 2))

    for copy in halo:
        copy.wait()

    def y_rows(c, x, side, far):
        near = pltpu.roll(get(c, x, 8 if side == 0 else 1), 16 if side == 0 else 112, 1)
        put(c, x, 9 * side, jnp.where(along_y == 3 * side, far, near))

    for c in range(CIN):
        for side in range(2):
            own = y_recv[side, c].astype(F32)
            for x in range(1, 5):
                y_rows(c, x, side, own[8 * (x - 1) : 8 * x])
    z_halo((0, 4))
    first_pairs((0, 4), (1, 2, 3, 4, 6))
    finish(1, (1, 2), (0, 3))

    for c in range(CIN):
        low = jnp.where(high_x, x_send[0, c].astype(F32), keep_low * x_recv[0, c].astype(F32))
        high = jnp.where(high_x, keep_high * x_recv[1, c].astype(F32), x_send[1, c].astype(F32))
        for y in range(8):
            put(c, 0, 1 + y, low[8 * y : 8 * y + 8])
            put(c, 5, 1 + y, high[8 * y : 8 * y + 8])
        for side in range(2):
            own = y_recv[side, c].astype(F32)
            corner_low = keep_low * c_recv[0 + side, c].astype(F32)
            corner_high = keep_high * c_recv[2 + side, c].astype(F32)
            y_rows(c, 0, side, jnp.where(high_x, pltpu.roll(own[24:32], 64, 1), corner_low))
            y_rows(c, 5, side, jnp.where(high_x, corner_high, pltpu.roll(own[0:8], 64, 1)))
    z_halo_edge(range(5))
    first_pairs((1, 2, 3), (0, 5, 7))
    finish(2, (0, 3), (1, 2))
    first_pairs((0, 4), (0, 5, 7))
    finish(3, (0, 3), (0, 3))

    low_half = iota((1, LANES), 1) < 64
    inner_y = ((iota((1, LANES), 1) + 16) & 63) >= 32
    taken = []
    sides = []
    for chunk in range(4):
        pltpu.make_async_copy(
            leaving.at[chunk, pl.ds(0, NDEV - 1)], arrived.at[chunk, pl.ds(0, NDEV - 1)],
            back_recv.at[chunk],
        ).wait()
        taken.append(dot(place_slots[...], arrived[chunk].reshape(2 * SLOTS, 3 * LANES)))
        if chunk % 2 == 0:
            continue
        inner, outer = taken[chunk - 1], taken[chunk]
        fields = []
        for pair in range(3):
            lanes = slice(pair * LANES, (pair + 1) * LANES)
            fields.append(jnp.where(inner_y, inner[:, lanes], outer[:, lanes]))
            fields.append(pltpu.roll(jnp.where(inner_y, outer[:, lanes], inner[:, lanes]), 96, 1))
        sides.append(fields)
    for half in range(2):
        rows = slice(half * CAP, (half + 1) * CAP)
        for f in range(COUT):
            middle, ends = sides[0][f][rows], sides[1][f][rows]
            lanes = slice(2 * half * LANES, (2 * half + 1) * LANES)
            out_ref[f, :, lanes] = jnp.where(low_half, ends, middle).astype(BF16)
            lanes = slice((2 * half + 1) * LANES, (2 * half + 2) * LANES)
            out_ref[f, :, lanes] = jnp.where(low_half, middle, ends).astype(BF16)
    pltpu.make_async_copy(
        outgoing.at[:, pl.ds(0, NDEV - 1)], incoming.at[:, pl.ds(0, NDEV - 1)], send_sem
    ).wait()
    pltpu.make_async_copy(
        leaving.at[:, pl.ds(0, NDEV - 1)], arrived.at[:, pl.ds(0, NDEV - 1)], back_send
    ).wait()


VMEM = pl.BlockSpec(memory_space=pltpu.VMEM)
HBM = pl.BlockSpec(memory_space=pltpu.HBM)


def shards(
    fields, solver_counts, cnn_owner, in_weight, in_bias, depth_weight, depth_bias,
    mix_weight, mix_bias, out_weight, out_bias,
):
    closure = pl.pallas_call(
        closure_body,
        out_shape=jax.ShapeDtypeStruct((COUT, CAP, 4 * LANES), BF16),
        in_specs=[HBM] * 11,
        out_specs=VMEM,
        scratch_shapes=[
            pltpu.VMEM((1, NDEV), I32),
            pltpu.VMEM((64, LANES), I32),
            pltpu.VMEM((CIN, CAP, 4 * LANES), BF16),
            pltpu.VMEM((CIN, HID), BF16),
            pltpu.VMEM((1, HID), F32),
            pltpu.VMEM((HID, 27), F32),
            pltpu.VMEM((1, HID), F32),
            pltpu.VMEM((HID, HID), BF16),
            pltpu.VMEM((1, HID), F32),
            pltpu.VMEM((COUT, HID), BF16),
            pltpu.VMEM((1, COUT), F32),
            pltpu.VMEM((8 * HID, 8 * HID), BF16),
            pltpu.VMEM((8 * COUT, 8 * HID), BF16),
            pltpu.VMEM((8 * COUT, LANES), F32),
            pltpu.VMEM((CIN, 2, 2 * SLOTS, LANES), F32),
            pltpu.VMEM((2, NDEV, 4, CIN * LANES), BF16),
            pltpu.VMEM((2, NDEV, 4, CIN * LANES), BF16),
            pltpu.VMEM((CIN, 640, LANES), F32),
            pltpu.VMEM((7, 16, LANES), F32),
            pltpu.VMEM((HID, 640, LANES), BF16),
            pltpu.VMEM((2, 128 * HID, LANES), F32),
            pltpu.VMEM((HID, 128, 2 * LANES), BF16),
            pltpu.VMEM((8 * HID, LANES), F32),
            pltpu.VMEM((8 * HID, LANES), F32),
            pltpu.VMEM((8, 8 * HID, LANES), BF16),
            pltpu.VMEM((64 * COUT, LANES), F32),
            pltpu.VMEM((2 * SLOTS, LANES), BF16),
            pltpu.VMEM((2 * CAP, 2 * SLOTS), BF16),
            pltpu.VMEM((2, CIN, 64, LANES), BF16),
            pltpu.VMEM((2, CIN, 64, LANES), BF16),
            pltpu.VMEM((2, CIN, 32, LANES), BF16),
            pltpu.VMEM((2, CIN, 32, LANES), BF16),
            pltpu.VMEM((4, CIN, 8, LANES), BF16),
            pltpu.VMEM((4, CIN, 8, LANES), BF16),
            pltpu.VMEM((4, NDEV, 4, 3 * LANES), BF16),
            pltpu.VMEM((4, NDEV, 4, 3 * LANES), BF16),
            pltpu.SemaphoreType.DMA((11,)),
            pltpu.SemaphoreType.DMA,
            pltpu.SemaphoreType.DMA((2,)),
            pltpu.SemaphoreType.DMA((8,)),
            pltpu.SemaphoreType.DMA((8,)),
            pltpu.SemaphoreType.DMA,
            pltpu.SemaphoreType.DMA((4,)),
        ],
        compiler_params=pltpu.CompilerParams(
            collective_id=0, has_side_effects=True, vmem_limit_bytes=36 * 1024 * 1024
        ),
        name="closure",
    )(*(
        pltpu.with_memory_space_constraint(operand, pltpu.HBM)
        for operand in (
            solver_counts.reshape(1, NDEV),
            cnn_owner.reshape(64, LANES),
            jnp.transpose(fields, (1, 0, 2)),
            jnp.transpose(in_weight),
            in_bias.reshape(1, HID),
            depth_weight,
            depth_bias.reshape(1, HID),
            mix_weight,
            mix_bias.reshape(1, HID),
            out_weight,
            out_bias.reshape(1, COUT),
        )
    ))
    return jnp.transpose(closure, (1, 0, 2))


def solution(mesh):
    return jax.shard_map(
        shards,
        mesh=mesh,
        in_specs=(P(("gx", "yz"), None, None), P(), P(), P(), P(), P(), P(), P(), P(), P(), P()),
        out_specs=P(("gx", "yz"), None, None),
        check_vma=False,
    )
```
